128 devices in a mesh: fsdp: 32 (over y, z, core), dp: 4 (over x).
Axes of the slice: x: 4, y: 4, z: 4, core: 2. Of those that a mesh axis runs over, the one named last changes fastest.
Arguments:
- tokens: bfloat16 [16384, 4096], P(('fsdp', 'dp')), may hold values from -6 to 6
- gain: float32 [4096], replicated, may hold values from 0.5 to 1.5
- tiles: bfloat16 [512, 128, 128], P('fsdp'), may hold values from -0.25 to 0.25
- tile_rows: int32 [512], replicated, may hold values from 0 to 31, as said below
- tile_cols: int32 [512], replicated, may hold values from 0 to 111, as said below
- cotangent: bfloat16 [16384, 14336], P(('fsdp', 'dp')), may hold values from -6 to 6
Outputs:
- projected: bfloat16 [16384, 14336], P(('fsdp', 'dp'))
- token_grad: bfloat16 [16384, 4096], P(('fsdp', 'dp'))
- tile_grad: float32 [512, 128, 128], P('fsdp')
- gain_grad: float32 [4096], replicated
The draws below stay inside these ranges and needn't reach their ends.
Inputs may be any that keep to these rules, and one draw needn't show every extreme that they name: The pairs (tile_rows[i], tile_cols[i]) are all different. `tile_cols`: pairs with tile_rows as above.
All inputs are finite; a program needn't handle non-finite values.
Results may differ from the reference program's by a relative error of at most 0.0049.
Values may be sent and summed in bfloat16 or wider, within the bound.
No kernel may reach another device: no remote copies, remote signals or barrier semaphores. Data moves between devices by JAX's collectives and lax.ppermute only.
A program may use at most 256 MiB of HBM per device.

```python
import jax
import jax.numpy as jnp
from jax import lax

D = 4096
FF = 14336
TILE = 128
NNZ = 512
RB = 32
CB = 112
TOKENS = 16384
N_FSDP = 32


def tile_places(key):
    inner = jax.random.fold_in(key, 7)
    total = RB * CB
    rest = 1 + jax.random.permutation(inner, total - 2)[:NNZ - 2]
    first = jnp.array([total - 1, 0], dtype=jnp.int32)
    return jnp.concatenate([first, rest.astype(jnp.int32)])


def draw_tile_rows(key, part):
    return (tile_places(key) // CB).astype(jnp.int32)


def draw_tile_cols(key, part):
    return (tile_places(key) % CB).astype(jnp.int32)


def levels(stream_key, extent, shards, low, top_value):
    loudness, own = 1.0, jax.random.fold_in(stream_key, 6)
    for axis_at, shards_of in shards:
        steps = jnp.exp(jax.random.uniform(jax.random.fold_in(own, axis_at), (shards_of,), jnp.float32, low / len(shards), top_value / len(shards)))
        loudness = loudness * jnp.repeat(steps, extent[axis_at] // shards_of).reshape([-1 if axis == axis_at else 1 for axis in range(len(extent))])
    return loudness


def normal_values(key, shape, width, bound, cuts=(), held_as=jnp.bfloat16):
    drawn = jax.random.normal(key, shape, jnp.float32) * width
    if len(cuts) > 0:
        drawn = levels(key, shape, cuts, -0.22, 0.18) * drawn
    return jnp.clip(drawn, min=-bound, max=bound).astype(held_as)


def setup_inputs(seed: int = 0) -> dict:
    key_list = jax.random.split(jax.random.key(seed), 7)
    tokens = normal_values(key_list[0], (TOKENS, D), 1.0, 6.0, ((0, 128),))
    gain = jnp.clip(jax.random.uniform(key_list[1], (D,), jnp.float32, 0.5, 1.5), 0.5, 1.5)
    tiles = normal_values(key_list[2], (NNZ, TILE, TILE), (TILE * NNZ // CB) ** -0.5, 0.25, ((0, 32),))
    tile_rows = draw_tile_rows(jax.random.fold_in(key_list[6], 71), 0)
    tile_cols = draw_tile_cols(jax.random.fold_in(key_list[6], 71), 0)
    cotangent = normal_values(key_list[5], (TOKENS, FF), 1.0, 6.0, ((0, 128),))
    return dict(tokens=tokens, gain=gain, tiles=tiles, tile_rows=tile_rows, tile_cols=tile_cols, cotangent=cotangent)


def reference(tokens, gain, tiles, tile_rows, tile_cols, cotangent):
    x32 = tokens.astype(jnp.float32)
    scale = lax.rsqrt(lax.optimization_barrier(jnp.mean(x32 * x32, axis=-1, keepdims=True)) + 1e-05)
    normed = (x32 * scale * gain).astype(jnp.bfloat16)
    xblocks = normed.reshape(TOKENS, RB, TILE)
    gblocks = cotangent.reshape(TOKENS, CB, TILE)
    block = TOKENS // N_FSDP

    def one_block(index):
        xpart = lax.dynamic_slice_in_dim(xblocks, index * block, block, 0)
        gpart = lax.dynamic_slice_in_dim(gblocks, index * block, block, 0)

        def step(carry, which):
            outsum, back = carry
            row_id = tile_rows[which]
            col_id = tile_cols[which]
            weight = tiles[which]
            xrow = lax.dynamic_index_in_dim(xpart, row_id, 1, keepdims=False)
            gcol = lax.dynamic_index_in_dim(gpart, col_id, 1, keepdims=False)
            outsum = outsum.at[:, col_id].add(jnp.dot(xrow, weight, preferred_element_type=jnp.float32))
            back = back.at[:, row_id].add(jnp.dot(gcol, weight.T, preferred_element_type=jnp.float32))
            return ((outsum, back), None)
        start = (jnp.zeros((block, CB, TILE), jnp.float32), jnp.zeros((block, RB, TILE), jnp.float32))
        (outsum, back), _ = lax.scan(step, start, jnp.arange(NNZ, dtype=jnp.int32))
        return (outsum, back)
    outsum, back = lax.map(one_block, jnp.arange(N_FSDP, dtype=jnp.int32))
    projected = outsum.reshape(TOKENS, FF).astype(jnp.bfloat16)
    dnormed = back.reshape(TOKENS, D)
    gain_grad = lax.optimization_barrier(jnp.sum(dnormed * x32 * scale, axis=0))
    inner = lax.optimization_barrier(jnp.mean(x32 * gain * dnormed, axis=-1, keepdims=True))
    token_grad = (scale * gain * dnormed - x32 * scale ** 3 * inner).astype(jnp.bfloat16)

    def tile_term(which):
        xrow = lax.dynamic_index_in_dim(xblocks, tile_rows[which], 1, keepdims=False)
        gcol = lax.dynamic_index_in_dim(gblocks, tile_cols[which], 1, keepdims=False)
        return jnp.dot(xrow.T, gcol, preferred_element_type=jnp.float32)
    tile_grad = lax.map(tile_term, jnp.arange(NNZ, dtype=jnp.int32))
    return (projected, token_grad, tile_grad, gain_grad)
```

```python
import jax
import jax.numpy as jnp
from jax import lax
from jax.experimental import pallas as pl
from jax.experimental.pallas import tpu as pltpu
from jax.sharding import Mesh, PartitionSpec as P

BF = jnp.bfloat16
F4 = jnp.float32
T = 128
ALL = ("y", "z", "c", "x")


def params(limit=56):
    return pltpu.CompilerParams(vmem_limit_bytes=limit * 1024 * 1024)


def whole(shape):
    zeros = (0,) * len(shape)
    return pl.BlockSpec(shape, lambda *_: zeros, pipeline_mode=pl.Buffered(1))


def dot(a, b):
    return jnp.dot(a, b, preferred_element_type=F4)


def dot_t(a, b):
    return lax.dot_general(a, b, (((1,), (1,)), ((), ())), preferred_element_type=F4)


def cols_at(index):
    return pl.ds(pl.multiple_of(index * T, T), T)


def norm_kernel(own_ref, other_ref, gain_ref, normed_ref, turned_ref, scale_ref):
    count, width = own_ref.shape
    blocks = width // T
    for half, ref in enumerate((own_ref, other_ref)):
        def squares(b, total):
            x = ref[:, cols_at(b)].astype(F4)
            return total + x * x

        total = lax.fori_loop(0, blocks, squares, jnp.zeros((count, T), F4), unroll=4)
        mean = jnp.sum(total, axis=1, keepdims=True) / width
        scale = lax.rsqrt(mean + 1e-05)
        if half == 0:
            scale_ref[...] = jnp.broadcast_to(scale, (count, T))

        def fill(b, carry):
            x = ref[:, cols_at(b)].astype(F4)
            normed = (x * scale * gain_ref[:, cols_at(b)]).astype(BF)
            if half == 0:
                normed_ref[:, cols_at(b)] = normed
            turned_ref[b, :, half * count : (half + 1) * count] = normed.T
            return carry

        lax.fori_loop(0, blocks, fill, 0, unroll=4)


def norm(own, other, gain):
    count, width = own.shape
    blocks = width // T
    return pl.pallas_call(
        norm_kernel,
        out_shape=(
            jax.ShapeDtypeStruct((count, width), BF),
            jax.ShapeDtypeStruct((blocks, T, 2 * count), BF),
            jax.ShapeDtypeStruct((count, T), F4),
        ),
        compiler_params=params(),
        cost_estimate=pl.CostEstimate(flops=8 * count * width, bytes_accessed=10 * count * width, transcendentals=0),
        name="norm",
    )(own, other, gain)


def grad_kernel(first, per, step, rows, cols, pos, turned_ref, own_ref, other_ref, out_ref):
    base = pl.program_id(0) * step
    y, z, c = pos[0], pos[1], pos[2]

    def one(k, carry):
        i = base + k
        major, minor, t = i // (4 * per), (i // per) % 4, i % per
        if first == "y":
            place = lax.rem(y + major, 4) * 4 + lax.rem(z + minor, 4)
        else:
            place = lax.rem(y + minor, 4) * 4 + lax.rem(z + major, 4)
        index = place * 32 + c * 16 + (0 if first == "y" else 16 - per) + t
        r, q = rows[index], cols[index]
        left = turned_ref[r]
        right = jnp.concatenate([own_ref[:, cols_at(q)], other_ref[:, cols_at(q)]], axis=0)
        out_ref[k] = dot(left, right).astype(BF)
        return carry

    lax.fori_loop(0, step, one, 0, unroll=8)


def grads(first, per, rows, cols, pos, turned, own, other):
    total, step = 16 * per, 16
    return pl.pallas_call(
        lambda *refs: grad_kernel(first, per, step, *refs),
        out_shape=jax.ShapeDtypeStruct((total, T, T), BF),
        grid_spec=pltpu.PrefetchScalarGridSpec(
            num_scalar_prefetch=3,
            grid=(total // step,),
            in_specs=[whole(turned.shape), whole(own.shape), whole(other.shape)],
            out_specs=pl.BlockSpec((step, T, T), lambda i, *_: (i, 0, 0)),
        ),
        compiler_params=params(),
        cost_estimate=pl.CostEstimate(
            flops=total * T * T * 512, bytes_accessed=2 * total * T * T + 10 * 2**20, transcendentals=0
        ),
        name="grads_" + first,
    )(rows, cols, pos, turned, own, other)


def project_kernel(
    step, rows, cols, tiles_ref, x_ref, normed_ref, scale_ref, gain_ref, g_ref,
    projected_ref, token_grad_ref, gain_ref_out, out_acc, back_acc,
):
    s = pl.program_id(0)
    count, width = x_ref.shape
    blocks = width // T

    @pl.when(s == 0)
    def _():
        out_acc[...] = jnp.zeros_like(out_acc)
        back_acc[...] = jnp.zeros_like(back_acc)

    def one(k, carry):
        r, q = rows[s * step + k], cols[s * step + k]
        weight = tiles_ref[k]
        out_acc[:, cols_at(q)] += dot(normed_ref[:, cols_at(r)], weight)
        back_acc[:, cols_at(r)] += dot_t(g_ref[:, cols_at(q)], weight)
        return carry

    lax.fori_loop(0, step, one, 0, unroll=8)

    @pl.when(s == pl.num_programs(0) - 1)
    def _():
        scale = scale_ref[...]

        def products(b, total):
            at = cols_at(b)
            x = x_ref[:, at].astype(F4)
            back = back_acc[:, at]
            gain_ref_out[:, at] = jnp.sum(back * x * scale, axis=0, keepdims=True)
            return total + x * gain_ref[:, at] * back

        total = lax.fori_loop(0, blocks, products, jnp.zeros((count, T), F4), unroll=2)
        inner = jnp.sum(total, axis=1, keepdims=True) / width
        cubed = scale * scale * scale * inner

        def finish(b, carry):
            at = cols_at(b)
            x = x_ref[:, at].astype(F4)
            token_grad_ref[:, at] = (scale * gain_ref[:, at] * back_acc[:, at] - x * cubed).astype(BF)
            return carry

        lax.fori_loop(0, blocks, finish, 0, unroll=2)

        def write(b, carry):
            projected_ref[:, cols_at(b)] = out_acc[:, cols_at(b)].astype(BF)
            return carry

        lax.fori_loop(0, g_ref.shape[1] // T, write, 0, unroll=4)


def project(rows, cols, tiles, x, normed, scale, gain, g):
    number, step = tiles.shape[0], 32
    count, width = x.shape
    return pl.pallas_call(
        lambda *refs: project_kernel(step, *refs),
        out_shape=(
            jax.ShapeDtypeStruct(g.shape, BF),
            jax.ShapeDtypeStruct(x.shape, BF),
            jax.ShapeDtypeStruct((1, width), F4),
        ),
        grid_spec=pltpu.PrefetchScalarGridSpec(
            num_scalar_prefetch=2,
            grid=(number // step,),
            in_specs=[pl.BlockSpec((step, T, T), lambda i, *_: (i, 0, 0))]
            + [whole(a.shape) for a in (x, normed, scale, gain, g)],
            out_specs=[whole(g.shape), whole(x.shape), whole((1, width))],
            scratch_shapes=[pltpu.VMEM(g.shape, F4), pltpu.VMEM(x.shape, F4)],
        ),
        compiler_params=params(),
        cost_estimate=pl.CostEstimate(
            flops=number * T * T * count * 4, bytes_accessed=2 * number * T * T + 10 * 2**20, transcendentals=0
        ),
        name="project",
    )(rows, cols, tiles, x, normed, scale, gain, g)


def ring(piece, axis, shift):
    return lax.ppermute(piece, axis, [(i, (i + shift) % 4) for i in range(4)])


def stage(pieces, axis):
    got = [ring(pieces[j], axis, j) for j in (1, 3, 2)]
    return sum((p.astype(F4) for p in got), pieces[0].astype(F4))


def shards(tokens, gain, tiles, tile_rows, tile_cols, cotangent):
    gain2 = gain.reshape(1, -1)
    pos = jnp.stack([lax.axis_index(a).astype(jnp.int32) for a in ("y", "z", "c", "x")])
    piece = lax.all_gather(tiles, ("y", "z", "c"), axis=0, tiled=True)
    swap = [(0, 1), (1, 0)]
    tokens_other = lax.ppermute(tokens, "c", swap)
    g_other = lax.ppermute(cotangent, "c", swap)
    normed, turned, scale = norm(tokens, tokens_other, gain2)
    sums = []
    for first, second in (("y", "z"), ("z", "y")):
        part = grads(first, 8, tile_rows, tile_cols, pos, turned, cotangent, g_other)
        part = part.reshape(4, 32, T, T)
        mid = stage([part[j] for j in range(4)], first).astype(BF)
        mid = mid.reshape(4, 8, T, T)
        sums.append(stage([mid[j] for j in range(4)], second))
    projected, token_grad, gain_part = project(
        tile_rows, tile_cols, piece, tokens, normed, scale, gain2, cotangent
    )
    owned = jnp.concatenate(sums, axis=0)
    sent = owned.astype(BF)
    one, three, two = (ring(sent, "x", j).astype(F4) for j in (1, 3, 2))
    tile_grad = (sent.astype(F4) + two) + (one + three)
    gains = lax.all_gather(gain_part.reshape(1, -1, T), ALL, axis=0, tiled=True)
    gain_grad = jnp.sum(gains, axis=0).reshape(-1)
    return (projected, token_grad, tile_grad, gain_grad)


def solution(mesh):
    grid = Mesh(mesh.devices.reshape(4, 4, 2, 4), ALL)
    owners = ("y", "z", "c")
    placed = (P(ALL, None), P(), P(owners, None, None), P(), P(), P(ALL, None))
    return jax.shard_map(
        shards,
        mesh=grid,
        in_specs=placed,
        out_specs=(P(ALL, None), P(ALL, None), P(owners, None, None), P()),
        check_vma=False,
    )
```

```python
import jax
import jax.numpy as jnp
from jax import lax
from jax.experimental import pallas as pl
from jax.experimental.pallas import tpu as pltpu
from jax.sharding import Mesh, PartitionSpec as P

BF = jnp.bfloat16
F4 = jnp.float32
T = 128
ALL = ("y", "z", "c", "x")


def params(limit):
    return pltpu.CompilerParams(vmem_limit_bytes=limit * 1024 * 1024)


def cost(micros, nbytes):
    return pl.CostEstimate(flops=int(micros * 1.1e9), bytes_accessed=nbytes, transcendentals=0)


def whole(shape):
    zeros = (0,) * len(shape)
    return pl.BlockSpec(shape, lambda *_: zeros, pipeline_mode=pl.Buffered(1))


def dot(a, b):
    return jnp.dot(a, b, preferred_element_type=F4)


def dot_t(a, b):
    return lax.dot_general(a, b, (((1,), (1,)), ((), ())), preferred_element_type=F4)


ANY = pl.BlockSpec(memory_space=pl.ANY)


def cols_at(index):
    return pl.ds(pl.multiple_of(index * T, T), T)


def norm_kernel(x_ref, gain_ref, normed_ref, turned_ref, scale_ref):
    count, width = x_ref.shape
    blocks = width // T

    def squares(b, total):
        x = x_ref[:, cols_at(b)].astype(F4)
        return total + x * x

    total = lax.fori_loop(0, blocks, squares, jnp.zeros((count, T), F4), unroll=4)
    scale = lax.rsqrt(jnp.sum(total, axis=1, keepdims=True) / width + 1e-05)
    scale_ref[...] = jnp.broadcast_to(scale, (count, T))

    def fill(b, carry):
        x = x_ref[:, cols_at(b)].astype(F4)
        normed = (x * scale * gain_ref[:, cols_at(b)]).astype(BF)
        normed_ref[:, cols_at(b)] = normed
        turned_ref[b] = normed.T
        return carry

    lax.fori_loop(0, blocks, fill, 0, unroll=4)


def norm(x, gain):
    count, width = x.shape
    return pl.pallas_call(
        norm_kernel,
        out_shape=(
            jax.ShapeDtypeStruct((count, width), BF),
            jax.ShapeDtypeStruct((width // T, T, count), BF),
            jax.ShapeDtypeStruct((count, T), F4),
        ),
        compiler_params=params(56),
        cost_estimate=cost(1, 0),
        name="norm",
    )(x, gain)


def grad_kernel(first, per, step, rows, cols, pos, turned_ref, turned_other_ref, own_ref, other_ref, *refs):
    out_refs = refs[-4:]
    base = pl.program_id(0) * step
    y, z, c = pos[0], pos[1], pos[2]
    each = 4 * per // step

    for major, out_ref in enumerate(out_refs):

        @pl.when(pl.program_id(0) // each == major)
        def _(major=major, out_ref=out_ref):
            def one(k, carry):
                i = base + k - major * 4 * per
                minor, t = i // per, i % per
                if first == "y":
                    place = lax.rem(y + major, 4) * 4 + lax.rem(z + minor, 4)
                else:
                    place = lax.rem(y + minor, 4) * 4 + lax.rem(z + major, 4)
                index = place * 32 + c * 16 + (0 if first == "y" else 16 - per) + t
                r, q = rows[index], cols[index]
                left = jnp.concatenate([turned_ref[r], turned_other_ref[r]], axis=1)
                right = jnp.concatenate([own_ref[:, cols_at(q)], other_ref[:, cols_at(q)]], axis=0)
                out_ref[k] = dot(left, right).astype(BF)
                return carry

            lax.fori_loop(0, step, one, 0, unroll=8)


def grads(first, per, rows, cols, pos, turned, turned_other, own, other, ties=()):
    piece, step = 4 * per, 16
    each = piece // step

    def out_spec(major):
        return pl.BlockSpec((step, T, T), lambda i, *_: (jnp.clip(i - major * each, 0, each - 1), 0, 0))

    return pl.pallas_call(
        lambda *refs: grad_kernel(first, per, step, *refs),
        out_shape=[jax.ShapeDtypeStruct((piece, T, T), BF)] * 4,
        grid_spec=pltpu.PrefetchScalarGridSpec(
            num_scalar_prefetch=3,
            grid=(4 * each,),
            in_specs=[whole(a.shape) for a in (turned, turned_other, own, other)] + [ANY] * len(ties),
            out_specs=[out_spec(major) for major in range(4)],
        ),
        compiler_params=params(56),
        cost_estimate=cost(2, 0),
        name="grads_" + first,
    )(rows, cols, pos, turned, turned_other, own, other, *ties)


def place_of(k, half, step):
    i = pl.program_id(0) * step + k
    return i // 8 * 16 + half * 8 + i % 8


def both_kernel(half, step, rows, cols, tiles_ref, normed_ref, g_ref, *refs):
    out_ref, back_ref = refs[-2:]

    @pl.when(pl.program_id(0) == 0)
    def _():
        out_ref[...] = jnp.zeros_like(out_ref)
        back_ref[...] = jnp.zeros_like(back_ref)

    def one(k, carry):
        index = place_of(k, half, step)
        r, q = rows[index], cols[index]
        weight = tiles_ref[k]
        out_ref[:, cols_at(q)] += dot(normed_ref[:, cols_at(r)], weight)
        back_ref[:, cols_at(r)] += dot_t(g_ref[:, cols_at(q)], weight)
        return carry

    lax.fori_loop(0, step, one, 0, unroll=8)


def both(half, rows, cols, tiles, normed, g, ties=()):
    number, step = tiles.shape[0], 32
    return pl.pallas_call(
        lambda *refs: both_kernel(half, step, *refs),
        out_shape=(jax.ShapeDtypeStruct(g.shape, F4), jax.ShapeDtypeStruct(normed.shape, F4)),
        grid_spec=pltpu.PrefetchScalarGridSpec(
            num_scalar_prefetch=2,
            grid=(number // step,),
            in_specs=[pl.BlockSpec((step, T, T), lambda i, *_: (i, 0, 0)), whole(normed.shape), whole(g.shape)]
            + [ANY] * len(ties),
            out_specs=[whole(g.shape), whole(normed.shape)],
        ),
        compiler_params=params(56),
        cost_estimate=cost(2, 0),
        name="both",
    )(rows, cols, tiles, normed, g, *ties)


def back_kernel(
    half, step, rows, cols, tiles_ref, back_in_ref, x_ref, scale_ref, gain_ref, g_ref, *refs
):
    token_grad_ref, sums_ref, back_acc = refs[-3:]
    count, width = x_ref.shape
    blocks = width // T

    @pl.when(pl.program_id(0) == 0)
    def _():
        back_acc[...] = back_in_ref[...]

    def one(k, carry):
        index = place_of(k, half, step)
        r, q = rows[index], cols[index]
        back_acc[:, cols_at(r)] += dot_t(g_ref[:, cols_at(q)], tiles_ref[k])
        return carry

    lax.fori_loop(0, step, one, 0, unroll=8)

    @pl.when(pl.program_id(0) == pl.num_programs(0) - 1)
    def _():
        scale = scale_ref[...]

        def products(b, total):
            at = cols_at(b)
            x = x_ref[:, at].astype(F4)
            back = back_acc[:, at]
            sums_ref[:, at] = jnp.sum(back * x * scale, axis=0, keepdims=True)
            return total + x * gain_ref[:, at] * back

        total = lax.fori_loop(0, blocks, products, jnp.zeros((count, T), F4), unroll=2)
        inner = jnp.sum(total, axis=1, keepdims=True) / width
        cubed = scale * scale * scale * inner

        def finish(b, carry):
            at = cols_at(b)
            x = x_ref[:, at].astype(F4)
            token_grad_ref[:, at] = (scale * gain_ref[:, at] * back_acc[:, at] - x * cubed).astype(BF)
            return carry

        lax.fori_loop(0, blocks, finish, 0, unroll=2)


def back(half, rows, cols, tiles, back_in, x, scale, gain, g, ties=()):
    number, step = tiles.shape[0], 32
    width = x.shape[1]
    return pl.pallas_call(
        lambda *refs: back_kernel(half, step, *refs),
        out_shape=(jax.ShapeDtypeStruct(x.shape, BF), jax.ShapeDtypeStruct((1, width), F4)),
        grid_spec=pltpu.PrefetchScalarGridSpec(
            num_scalar_prefetch=2,
            grid=(number // step,),
            in_specs=[pl.BlockSpec((step, T, T), lambda i, *_: (i, 0, 0))]
            + [whole(a.shape) for a in (back_in, x, scale, gain, g)]
            + [ANY] * len(ties),
            out_specs=[whole(x.shape), whole((1, width))],
            scratch_shapes=[pltpu.VMEM(x.shape, F4)],
        ),
        compiler_params=params(56),
        cost_estimate=cost(2, 0),
        name="back",
    )(rows, cols, tiles, back_in, x, scale, gain, g, *ties)


def fore_kernel(half, step, rows, cols, tiles_ref, out_in_ref, normed_ref, *refs):
    projected_ref, out_acc = refs[-2:]

    @pl.when(pl.program_id(0) == 0)
    def _():
        out_acc[...] = out_in_ref[...]

    def one(k, carry):
        index = place_of(k, half, step)
        r, q = rows[index], cols[index]
        out_acc[:, cols_at(q)] += dot(normed_ref[:, cols_at(r)], tiles_ref[k])
        return carry

    lax.fori_loop(0, step, one, 0, unroll=8)

    @pl.when(pl.program_id(0) == pl.num_programs(0) - 1)
    def _():
        projected_ref[...] = out_acc[...].astype(BF)


def fore(half, rows, cols, tiles, out_in, normed, ties=()):
    number, step = tiles.shape[0], 32
    return pl.pallas_call(
        lambda *refs: fore_kernel(half, step, *refs),
        out_shape=jax.ShapeDtypeStruct(out_in.shape, BF),
        grid_spec=pltpu.PrefetchScalarGridSpec(
            num_scalar_prefetch=2,
            grid=(number // step,),
            in_specs=[pl.BlockSpec((step, T, T), lambda i, *_: (i, 0, 0)), whole(out_in.shape), whole(normed.shape)]
            + [ANY] * len(ties),
            out_specs=whole(out_in.shape),
            scratch_shapes=[pltpu.VMEM(out_in.shape, F4)],
        ),
        compiler_params=params(56),
        cost_estimate=cost(2, 0),
        name="fore",
    )(rows, cols, tiles, out_in, normed, *ties)


def ring(piece, axis, shift):
    return lax.ppermute(piece, axis, [(i, (i + shift) % 4) for i in range(4)])


def first_sum(pieces, ties):
    each = pieces[0].shape[0] // 4

    def kernel(*refs):
        ins, outs = refs[:4], refs[-4:]
        a, b, c, d = (r[...].astype(F4) for r in ins)
        total = ((a + c) + (b + d)).astype(BF)
        for major, out in enumerate(outs):

            @pl.when(pl.program_id(0) == major)
            def _(out=out):
                out[...] = total

    return pl.pallas_call(
        kernel,
        out_shape=[jax.ShapeDtypeStruct((each, T, T), BF)] * 4,
        grid=(4,),
        in_specs=[pl.BlockSpec((each, T, T), lambda i: (i, 0, 0))] * 4 + [ANY] * len(ties),
        out_specs=[whole((each, T, T))] * 4,
        compiler_params=params(32),
        cost_estimate=cost(1, 0),
        name="first_sum",
    )(*pieces, *ties)


def sum_of_four(groups, dtype, ties, name):
    count = groups[0][0].shape[0]

    def kernel(*refs):
        out = refs[-1]
        for g in range(len(groups)):
            for i in range(count):
                a, b, c, d = (r[i].astype(F4) for r in refs[4 * g : 4 * g + 4])
                out[g * count + i] = ((a + c) + (b + d)).astype(dtype)

    arrays = [a for group in groups for a in group]
    return pl.pallas_call(
        kernel,
        out_shape=jax.ShapeDtypeStruct((count * len(groups), T, T), dtype),
        in_specs=[pl.BlockSpec(memory_space=pltpu.VMEM)] * len(arrays) + [ANY] * len(ties),
        compiler_params=params(32),
        cost_estimate=cost(1, 0),
        name=name,
    )(*arrays, *ties)


def exchange(pieces, axis):
    return [pieces[0]] + [ring(pieces[j], axis, j) for j in (1, 2, 3)]


def shards(tokens, gain, tiles, rows, cols, cotangent):
    gain2 = gain.reshape(1, -1)
    pos = jnp.stack([lax.axis_index(a).astype(jnp.int32) for a in ("y", "z", "c", "x")])
    owners = ("y", "z", "c")
    piece0 = lax.all_gather(tiles[:8], owners, axis=0, tiled=True)
    swap = [(0, 1), (1, 0)]
    tokens_other = lax.ppermute(tokens, "c", swap)
    g_other = lax.ppermute(cotangent, "c", swap)
    normed, turned, scale = norm(tokens, gain2)
    _, turned_other, _ = norm(tokens_other, gain2)
    part_y = grads("y", 8, rows, cols, pos, turned, turned_other, cotangent, g_other)
    part_z = grads("z", 8, rows, cols, pos, turned, turned_other, cotangent, g_other, (part_y[3],))
    piece1 = lax.all_gather(tiles[8:], owners, axis=0, tiled=True)
    out0, back0 = both(0, rows, cols, piece0, normed, cotangent, (part_z[3],))
    mid_y = first_sum(exchange(part_y, "y"), (back0,))
    mid_z = first_sum(exchange(part_z, "z"), (back0,))
    token_grad, gain_part = back(
        1, rows, cols, piece1, back0, tokens, scale, gain2, cotangent, (mid_y[0], mid_z[0])
    )
    gains = lax.all_gather(gain_part.reshape(1, -1, T), ALL, axis=0, tiled=True)
    sent = sum_of_four([exchange(mid_y, "z"), exchange(mid_z, "y")], BF, (token_grad,), "second_sum")
    projected = fore(1, rows, cols, piece1, out0, normed, (sent,))
    tile_grad = sum_of_four([exchange([sent] * 4, "x")], F4, (projected,), "last_sum")
    gain_grad = jnp.sum(gains, axis=0).reshape(-1)
    return (projected, token_grad, tile_grad, gain_grad)


def solution(mesh):
    grid = Mesh(mesh.devices.reshape(4, 4, 2, 4), ALL)
    owners = ("y", "z", "c")
    placed = (P(ALL, None), P(), P(owners, None, None), P(), P(), P(ALL, None))
    return jax.shard_map(
        shards,
        mesh=grid,
        in_specs=placed,
        out_specs=(P(ALL, None), P(ALL, None), P(owners, None, None), P()),
        check_vma=False,
    )
```

```python
import jax
import jax.numpy as jnp
from jax import lax
from jax.experimental import pallas as pl
from jax.experimental.pallas import tpu as pltpu
from jax.sharding import Mesh, PartitionSpec as P

BF = jnp.bfloat16
F4 = jnp.float32
T = 128
ALL = ("y", "z", "c", "x")


def params(limit):
    return pltpu.CompilerParams(vmem_limit_bytes=limit * 1024 * 1024)


def cost(micros, nbytes):
    return pl.CostEstimate(flops=int(micros * 1.1e9), bytes_accessed=nbytes, transcendentals=0)


def whole(shape):
    zeros = (0,) * len(shape)
    return pl.BlockSpec(shape, lambda *_: zeros, pipeline_mode=pl.Buffered(1))


def dot(a, b):
    return jnp.dot(a, b, preferred_element_type=F4)


def dot_t(a, b):
    return lax.dot_general(a, b, (((1,), (1,)), ((), ())), preferred_element_type=F4)


ANY = pl.BlockSpec(memory_space=pl.ANY)


def cols_at(index):
    return pl.ds(pl.multiple_of(index * T, T), T)


def norm_kernel(x_ref, gain_ref, normed_ref, turned_ref, scale_ref):
    count, width = x_ref.shape
    blocks = width // T

    def squares(b, total):
        x = x_ref[:, cols_at(b)].astype(F4)
        return total + x * x

    total = lax.fori_loop(0, blocks, squares, jnp.zeros((count, T), F4), unroll=4)
    scale = lax.rsqrt(jnp.sum(total, axis=1, keepdims=True) / width + 1e-05)
    scale_ref[...] = jnp.broadcast_to(scale, (count, T))

    def fill(b, carry):
        x = x_ref[:, cols_at(b)].astype(F4)
        normed = (x * scale * gain_ref[:, cols_at(b)]).astype(BF)
        normed_ref[:, cols_at(b)] = normed
        turned_ref[b] = normed.T
        return carry

    lax.fori_loop(0, blocks, fill, 0, unroll=4)


def norm(x, gain):
    count, width = x.shape
    return pl.pallas_call(
        norm_kernel,
        out_shape=(
            jax.ShapeDtypeStruct((count, width), BF),
            jax.ShapeDtypeStruct((width // T, T, count), BF),
            jax.ShapeDtypeStruct((count, T), F4),
        ),
        compiler_params=params(56),
        cost_estimate=cost(1, 0),
        name="norm",
    )(x, gain)


def grad_kernel(first, per, step, rows, cols, pos, turned_ref, turned_other_ref, own_ref, other_ref, *refs):
    out_refs = refs[-4:]
    base = pl.program_id(0) * step
    y, z, c = pos[0], pos[1], pos[2]
    each = 4 * per // step

    for major, out_ref in enumerate(out_refs):

        @pl.when(pl.program_id(0) // each == major)
        def _(major=major, out_ref=out_ref):
            def one(k, carry):
                i = base + k - major * 4 * per
                minor, t = i // per, i % per
                if first == "y":
                    place = lax.rem(y + major, 4) * 4 + lax.rem(z + minor, 4)
                else:
                    place = lax.rem(y + minor, 4) * 4 + lax.rem(z + major, 4)
                index = place * 32 + c * 16 + (0 if first == "y" else 16 - per) + t
                r, q = rows[index], cols[index]
                left = jnp.concatenate([turned_ref[r], turned_other_ref[r]], axis=1)
                right = jnp.concatenate([own_ref[:, cols_at(q)], other_ref[:, cols_at(q)]], axis=0)
                out_ref[k] = dot(left, right).astype(BF)
                return carry

            lax.fori_loop(0, step, one, 0, unroll=8)


def grads(first, per, rows, cols, pos, turned, turned_other, own, other, ties=()):
    piece, step = 4 * per, 16
    each = piece // step

    def out_spec(major):
        return pl.BlockSpec((step, T, T), lambda i, *_: (jnp.clip(i - major * each, 0, each - 1), 0, 0))

    return pl.pallas_call(
        lambda *refs: grad_kernel(first, per, step, *refs),
        out_shape=[jax.ShapeDtypeStruct((piece, T, T), BF)] * 4,
        grid_spec=pltpu.PrefetchScalarGridSpec(
            num_scalar_prefetch=3,
            grid=(4 * each,),
            in_specs=[whole(a.shape) for a in (turned, turned_other, own, other)] + [ANY] * len(ties),
            out_specs=[out_spec(major) for major in range(4)],
        ),
        compiler_params=params(56),
        cost_estimate=cost(2, 0),
        name="grads_" + first,
    )(rows, cols, pos, turned, turned_other, own, other, *ties)


def project_kernel(
    step, rows, cols, tiles_ref, x_ref, normed_ref, scale_ref, gain_ref, g_ref, *refs
):
    projected_ref, token_grad_ref, sums_ref, out_acc, back_acc = refs[-5:]
    s = pl.program_id(0)
    count, width = x_ref.shape
    blocks = width // T

    @pl.when(s == 0)
    def _():
        out_acc[...] = jnp.zeros_like(out_acc)
        back_acc[...] = jnp.zeros_like(back_acc)

    def one(k, carry):
        r, q = rows[s * step + k], cols[s * step + k]
        weight = tiles_ref[k]
        out_acc[:, cols_at(q)] += dot(normed_ref[:, cols_at(r)], weight)
        back_acc[:, cols_at(r)] += dot_t(g_ref[:, cols_at(q)], weight)
        return carry

    lax.fori_loop(0, step, one, 0, unroll=8)

    @pl.when(s == pl.num_programs(0) - 1)
    def _():
        scale = scale_ref[...]

        def products(b, total):
            at = cols_at(b)
            x = x_ref[:, at].astype(F4)
            back = back_acc[:, at]
            sums_ref[:, at] = jnp.sum(back * x * scale, axis=0, keepdims=True)
            return total + x * gain_ref[:, at] * back

        total = lax.fori_loop(0, blocks, products, jnp.zeros((count, T), F4), unroll=2)
        inner = jnp.sum(total, axis=1, keepdims=True) / width
        cubed = scale * scale * scale * inner

        def finish(b, carry):
            at = cols_at(b)
            x = x_ref[:, at].astype(F4)
            token_grad_ref[:, at] = (scale * gain_ref[:, at] * back_acc[:, at] - x * cubed).astype(BF)
            return carry

        lax.fori_loop(0, blocks, finish, 0, unroll=2)

        def write(b, carry):
            projected_ref[:, cols_at(b)] = out_acc[:, cols_at(b)].astype(BF)
            return carry

        lax.fori_loop(0, g_ref.shape[1] // T, write, 0, unroll=4)


def project(rows, cols, tiles, x, normed, scale, gain, g, ties=()):
    number, step = tiles.shape[0], 32
    count, width = x.shape
    return pl.pallas_call(
        lambda *refs: project_kernel(step, *refs),
        out_shape=(
            jax.ShapeDtypeStruct(g.shape, BF),
            jax.ShapeDtypeStruct(x.shape, BF),
            jax.ShapeDtypeStruct((1, width), F4),
        ),
        grid_spec=pltpu.PrefetchScalarGridSpec(
            num_scalar_prefetch=2,
            grid=(number // step,),
            in_specs=[pl.BlockSpec((step, T, T), lambda i, *_: (i, 0, 0))]
            + [whole(a.shape) for a in (x, normed, scale, gain, g)]
            + [ANY] * len(ties),
            out_specs=[whole(g.shape), whole(x.shape), whole((1, width))],
            scratch_shapes=[pltpu.VMEM(g.shape, F4), pltpu.VMEM(x.shape, F4)],
        ),
        compiler_params=params(32),
        cost_estimate=cost(2, 0),
        name="project",
    )(rows, cols, tiles, x, normed, scale, gain, g, *ties)


def ring(piece, axis, shift):
    return lax.ppermute(piece, axis, [(i, (i + shift) % 4) for i in range(4)])


def first_sum(pieces, ties):
    each = pieces[0].shape[0] // 4

    def kernel(*refs):
        ins, outs = refs[:4], refs[-4:]
        a, b, c, d = (r[...].astype(F4) for r in ins)
        total = ((a + c) + (b + d)).astype(BF)
        for major, out in enumerate(outs):

            @pl.when(pl.program_id(0) == major)
            def _(out=out):
                out[...] = total

    return pl.pallas_call(
        kernel,
        out_shape=[jax.ShapeDtypeStruct((each, T, T), BF)] * 4,
        grid=(4,),
        in_specs=[pl.BlockSpec((each, T, T), lambda i: (i, 0, 0))] * 4 + [ANY] * len(ties),
        out_specs=[whole((each, T, T))] * 4,
        compiler_params=params(32),
        cost_estimate=cost(1, 0),
        name="first_sum",
    )(*pieces, *ties)


def sum_of_four(groups, dtype, passed, name):
    count = groups[0][0].shape[0]
    arrays = [a for group in groups for a in group]

    def kernel(*refs):
        out = refs[len(arrays) + len(passed)]
        for g in range(len(groups)):
            for i in range(count):
                a, b, c, d = (r[i].astype(F4) for r in refs[4 * g : 4 * g + 4])
                out[g * count + i] = ((a + c) + (b + d)).astype(dtype)
        for k in range(len(passed)):
            refs[len(arrays) + len(passed) + 1 + k][...] = refs[len(arrays) + k][...]

    return pl.pallas_call(
        kernel,
        out_shape=[jax.ShapeDtypeStruct((count * len(groups), T, T), dtype)]
        + [jax.ShapeDtypeStruct(a.shape, a.dtype) for a in passed],
        in_specs=[pl.BlockSpec(memory_space=pltpu.VMEM)] * (len(arrays) + len(passed)),
        compiler_params=params(32),
        cost_estimate=cost(1, 0),
        name=name,
    )(*arrays, *passed)


def exchange(pieces, axis):
    return [pieces[0]] + [ring(pieces[j], axis, j) for j in (1, 2, 3)]


def shards(tokens, gain, tiles, rows, cols, cotangent):
    gain2 = gain.reshape(1, -1)
    pos = jnp.stack([lax.axis_index(a).astype(jnp.int32) for a in ("y", "z", "c", "x")])
    owners = ("y", "z", "c")
    piece = lax.all_gather(tiles, owners, axis=0, tiled=True)
    swap = [(0, 1), (1, 0)]
    tokens_other = lax.ppermute(tokens, "c", swap)
    g_other = lax.ppermute(cotangent, "c", swap)
    normed, turned, scale = norm(tokens, gain2)
    _, turned_other, _ = norm(tokens_other, gain2)
    part_y = grads("y", 8, rows, cols, pos, turned, turned_other, cotangent, g_other)
    part_z = grads("z", 8, rows, cols, pos, turned, turned_other, cotangent, g_other, (part_y[3],))
    mid_y = first_sum(exchange(part_y, "y"), (part_z[3],))
    mid_z = first_sum(exchange(part_z, "z"), ())
    projected, token_grad, sums = project(
        rows, cols, piece, tokens, normed, scale, gain2, cotangent, (mid_y[0], mid_z[0])
    )
    sums = sums.reshape(-1, T)
    sent, sums = sum_of_four([exchange(mid_y, "z"), exchange(mid_z, "y")], BF, (sums,), "second_sum")
    (tile_grad,) = sum_of_four([exchange([sent] * 4, "x")], F4, (), "last_sum")
    sums = sums + lax.ppermute(sums, "c", swap)
    for axis in ("z", "y", "x"):
        own, right, opposite, left = exchange([sums] * 4, axis)
        sums = (own + opposite) + (right + left)
    return (projected, token_grad, tile_grad, sums.reshape(-1))


def solution(mesh):
    grid = Mesh(mesh.devices.reshape(4, 4, 2, 4), ALL)
    owners = ("y", "z", "c")
    placed = (P(ALL, None), P(), P(owners, None, None), P(), P(), P(ALL, None))
    return jax.shard_map(
        shards,
        mesh=grid,
        in_specs=placed,
        out_specs=(P(ALL, None), P(ALL, None), P(owners, None, None), P()),
        check_vma=False,
    )
```

```python
import jax
import jax.numpy as jnp
from jax import lax
from jax.experimental import pallas as pl
from jax.experimental.pallas import tpu as pltpu
from jax.sharding import Mesh, PartitionSpec as P

BF = jnp.bfloat16
F4 = jnp.float32
T = 128
ALL = ("y", "z", "c", "x")


def params(limit):
    return pltpu.CompilerParams(vmem_limit_bytes=limit * 1024 * 1024)


def cost(micros, nbytes):
    return pl.CostEstimate(flops=int(micros * 1.1e9), bytes_accessed=nbytes, transcendentals=0)


def whole(shape):
    zeros = (0,) * len(shape)
    return pl.BlockSpec(shape, lambda *_: zeros, pipeline_mode=pl.Buffered(1))


def dot(a, b):
    return jnp.dot(a, b, preferred_element_type=F4)


def dot_t(a, b):
    return lax.dot_general(a, b, (((1,), (1,)), ((), ())), preferred_element_type=F4)


ANY = pl.BlockSpec(memory_space=pl.ANY)


def cols_at(index):
    return pl.ds(pl.multiple_of(index * T, T), T)


def norm_kernel(x_ref, gain_ref, normed_ref, turned_ref, scale_ref):
    count, width = x_ref.shape
    blocks = width // T

    def squares(b, total):
        x = x_ref[:, cols_at(b)].astype(F4)
        return total + x * x

    total = lax.fori_loop(0, blocks, squares, jnp.zeros((count, T), F4), unroll=4)
    scale = lax.rsqrt(jnp.sum(total, axis=1, keepdims=True) / width + 1e-05)
    scale_ref[...] = jnp.broadcast_to(scale, (count, T))

    def fill(b, carry):
        x = x_ref[:, cols_at(b)].astype(F4)
        normed = (x * scale * gain_ref[:, cols_at(b)]).astype(BF)
        normed_ref[:, cols_at(b)] = normed
        turned_ref[b] = normed.T
        return carry

    lax.fori_loop(0, blocks, fill, 0, unroll=4)


def norm(x, gain):
    count, width = x.shape
    return pl.pallas_call(
        norm_kernel,
        out_shape=(
            jax.ShapeDtypeStruct((count, width), BF),
            jax.ShapeDtypeStruct((width // T, T, count), BF),
            jax.ShapeDtypeStruct((count, T), F4),
        ),
        compiler_params=params(56),
        cost_estimate=cost(1, 0),
        name="norm",
    )(x, gain)


def listed(kind, ahead, i, y, z, c, x):
    if kind == "x":
        to_y, to_z, t = i // 8, i // 2 % 4, 2 * lax.rem(x + ahead, 4) + i % 2
    elif kind == "y":
        to_y, to_z, t = ahead, i // 4, 8 + i % 4
    else:
        to_y, to_z, t = i // 4, ahead, 12 + i % 4
    return (lax.rem(y + to_y, 4) * 4 + lax.rem(z + to_z, 4)) * 32 + c * 16 + t


STEP = 16


def grad_kernel(plan, rows, cols, pos, turned_ref, turned_other_ref, own_ref, other_ref, *refs):
    out_refs = refs[-len(plan) :]
    y, z, c, x = pos[0], pos[1], pos[2], pos[3]

    for (kind, ahead, start, each), out_ref in zip(plan, out_refs):
        at = pl.program_id(0)

        @pl.when((at >= start) & (at < start + each))
        def _(kind=kind, ahead=ahead, start=start, out_ref=out_ref, at=at):
            def one(k, carry):
                index = listed(kind, ahead, (at - start) * STEP + k, y, z, c, x)
                r, q = rows[index], cols[index]
                left = jnp.concatenate([turned_ref[r], turned_other_ref[r]], axis=1)
                right = jnp.concatenate([own_ref[:, cols_at(q)], other_ref[:, cols_at(q)]], axis=0)
                out_ref[k] = dot(left, right).astype(BF)
                return carry

            lax.fori_loop(0, STEP, one, 0, unroll=8)


def grads(kinds, rows, cols, pos, turned, turned_other, own, other, ties=()):
    plan, steps = [], 0
    for kind, size in kinds:
        for ahead in range(4):
            plan.append((kind, ahead, steps, size // STEP))
            steps += size // STEP

    def out_spec(start, each):
        return pl.BlockSpec((STEP, T, T), lambda i, *_: (jnp.clip(i - start, 0, each - 1), 0, 0))

    return pl.pallas_call(
        lambda *refs: grad_kernel(plan, *refs),
        out_shape=[jax.ShapeDtypeStruct((each * STEP, T, T), BF) for _, _, _, each in plan],
        grid_spec=pltpu.PrefetchScalarGridSpec(
            num_scalar_prefetch=3,
            grid=(steps,),
            in_specs=[whole(a.shape) for a in (turned, turned_other, own, other)] + [ANY] * len(ties),
            out_specs=[out_spec(start, each) for _, _, start, each in plan],
        ),
        compiler_params=params(40),
        cost_estimate=cost(2, 0),
        name="grads_" + kinds[0][0],
    )(rows, cols, pos, turned, turned_other, own, other, *ties)


def project_kernel(
    step, rows, cols, tiles_ref, x_ref, normed_ref, scale_ref, gain_ref, g_ref, *refs
):
    projected_ref, token_grad_ref, sums_ref, out_acc, back_acc = refs[-5:]
    s = pl.program_id(0)
    count, width = x_ref.shape
    blocks = width // T

    @pl.when(s == 0)
    def _():
        out_acc[...] = jnp.zeros_like(out_acc)
        back_acc[...] = jnp.zeros_like(back_acc)

    def one(k, carry):
        r, q = rows[s * step + k], cols[s * step + k]
        weight = tiles_ref[k]
        out_acc[:, cols_at(q)] += dot(normed_ref[:, cols_at(r)], weight)
        back_acc[:, cols_at(r)] += dot_t(g_ref[:, cols_at(q)], weight)
        return carry

    lax.fori_loop(0, step, one, 0, unroll=8)

    @pl.when(s == pl.num_programs(0) - 1)
    def _():
        scale = scale_ref[...]

        def products(b, total):
            at = cols_at(b)
            x = x_ref[:, at].astype(F4)
            back = back_acc[:, at]
            sums_ref[:, at] = jnp.sum(back * x * scale, axis=0, keepdims=True)
            return total + x * gain_ref[:, at] * back

        total = lax.fori_loop(0, blocks, products, jnp.zeros((count, T), F4), unroll=2)
        inner = jnp.sum(total, axis=1, keepdims=True) / width
        cubed = scale * scale * scale * inner

        def finish(b, carry):
            at = cols_at(b)
            x = x_ref[:, at].astype(F4)
            token_grad_ref[:, at] = (scale * gain_ref[:, at] * back_acc[:, at] - x * cubed).astype(BF)
            return carry

        lax.fori_loop(0, blocks, finish, 0, unroll=2)

        def write(b, carry):
            projected_ref[:, cols_at(b)] = out_acc[:, cols_at(b)].astype(BF)
            return carry

        lax.fori_loop(0, g_ref.shape[1] // T, write, 0, unroll=4)


def project(rows, cols, tiles, x, normed, scale, gain, g, ties=()):
    number, step = tiles.shape[0], 32
    count, width = x.shape
    return pl.pallas_call(
        lambda *refs: project_kernel(step, *refs),
        out_shape=(
            jax.ShapeDtypeStruct(g.shape, BF),
            jax.ShapeDtypeStruct(x.shape, BF),
            jax.ShapeDtypeStruct((1, width), F4),
        ),
        grid_spec=pltpu.PrefetchScalarGridSpec(
            num_scalar_prefetch=2,
            grid=(number // step,),
            in_specs=[pl.BlockSpec((step, T, T), lambda i, *_: (i, 0, 0))]
            + [whole(a.shape) for a in (x, normed, scale, gain, g)]
            + [ANY] * len(ties),
            out_specs=[whole(g.shape), whole(x.shape), whole((1, width))],
            scratch_shapes=[pltpu.VMEM(g.shape, F4), pltpu.VMEM(x.shape, F4)],
        ),
        compiler_params=params(32),
        cost_estimate=cost(2, 0),
        name="project",
    )(rows, cols, tiles, x, normed, scale, gain, g, *ties)


def ring(piece, axis, shift):
    return lax.ppermute(piece, axis, [(i, (i + shift) % 4) for i in range(4)])


def first_sum(pieces, ties):
    each = pieces[0].shape[0] // 4

    def kernel(*refs):
        ins, outs = refs[:4], refs[-4:]
        total = add_four(ins, ...).astype(BF)
        for major, out in enumerate(outs):

            @pl.when(pl.program_id(0) == major)
            def _(out=out):
                out[...] = total

    return pl.pallas_call(
        kernel,
        out_shape=[jax.ShapeDtypeStruct((each, T, T), BF)] * 4,
        grid=(4,),
        in_specs=[pl.BlockSpec((each, T, T), lambda i: (i, 0, 0))] * 4 + [ANY] * len(ties),
        out_specs=[whole((each, T, T))] * 4,
        compiler_params=params(32),
        cost_estimate=cost(1, 0),
        name="first_sum",
    )(*pieces, *ties)


def add_four(refs, i):
    a, b, c, d = (r[i].astype(F4) for r in refs)
    return (a + c) + (b + d)


def second_sum(groups):
    count = groups[0][0].shape[0]
    arrays = [a for group in groups for a in group]

    def kernel(*refs):
        for g in range(len(groups)):
            for i in range(count):
                refs[-1][g * count + i] = add_four(refs[4 * g : 4 * g + 4], i).astype(BF)

    return pl.pallas_call(
        kernel,
        out_shape=jax.ShapeDtypeStruct((count * len(groups), T, T), BF),
        in_specs=[pl.BlockSpec(memory_space=pltpu.VMEM)] * len(arrays),
        compiler_params=params(32),
        cost_estimate=cost(1, 0),
        name="second_sum",
    )(*arrays)


def third_sum(pieces, others, passed):
    count, more = pieces[0].shape[0], others.shape[0]

    def kernel(*refs):
        others_ref, passed_ref, out_ref, passed_out = refs[4:]
        for i in range(count):
            out_ref[i] = add_four(refs[:4], i).astype(BF)
        out_ref[count:] = others_ref[...]
        passed_out[...] = passed_ref[...]

    return pl.pallas_call(
        kernel,
        out_shape=(
            jax.ShapeDtypeStruct((count + more, T, T), BF),
            jax.ShapeDtypeStruct(passed.shape, passed.dtype),
        ),
        in_specs=[pl.BlockSpec(memory_space=pltpu.VMEM)] * 6,
        compiler_params=params(32),
        cost_estimate=cost(1, 0),
        name="third_sum",
    )(*pieces, others, passed)


def last_sum(pieces, pos):
    def kernel(pos_ref, *refs):
        out_ref = refs[-1]
        for back in range(4):
            source = lax.rem(pos_ref[3] + 4 - back, 4)
            for u in range(2):
                out_ref[2 * source + u] = refs[back][u].astype(F4)
        for i in range(2, 10):
            out_ref[6 + i] = add_four(refs[:4], i)

    return pl.pallas_call(
        kernel,
        out_shape=jax.ShapeDtypeStruct((16, T, T), F4),
        in_specs=[pl.BlockSpec(memory_space=pltpu.SMEM)] + [pl.BlockSpec(memory_space=pltpu.VMEM)] * 4,
        compiler_params=params(32),
        cost_estimate=cost(1, 0),
        name="last_sum",
    )(pos, *pieces)


def exchange(pieces, axis):
    return [pieces[0]] + [ring(pieces[j], axis, j) for j in (1, 2, 3)]


def shards(tokens, gain, tiles, rows, cols, cotangent):
    gain2 = gain.reshape(1, -1)
    pos = jnp.stack([lax.axis_index(a).astype(jnp.int32) for a in ("y", "z", "c", "x")])
    owners = ("y", "z", "c")
    piece = lax.all_gather(tiles, owners, axis=0, tiled=True)
    swap = [(0, 1), (1, 0)]
    tokens_other = lax.ppermute(tokens, "c", swap)
    g_other = lax.ppermute(cotangent, "c", swap)
    normed, turned, scale = norm(tokens, gain2)
    _, turned_other, _ = norm(tokens_other, gain2)
    part_x = grads([("x", 32)], rows, cols, pos, turned, turned_other, cotangent, g_other)
    parts = grads([("y", 16), ("z", 16)], rows, cols, pos, turned, turned_other, cotangent, g_other, (part_x[3],))
    mid_y = first_sum(exchange(parts[:4], "y"), ())
    mid_z = first_sum(exchange(parts[4:], "z"), (mid_y[0],))
    mid_x = first_sum(exchange(part_x, "x"), (mid_z[0],))
    over_x = second_sum([exchange(mid_y, "z"), exchange(mid_z, "y")])
    last_x = first_sum(exchange(mid_x, "y"), (over_x,))
    projected, token_grad, sums = project(
        rows, cols, piece, tokens, normed, scale, gain2, cotangent, (last_x[0], over_x)
    )
    sent, sums = third_sum(exchange(last_x, "z"), over_x, sums.reshape(-1, T))
    tile_grad = last_sum(exchange([sent] * 4, "x"), pos)
    sums = sums + lax.ppermute(sums, "c", swap)
    for axis in ("z", "y", "x"):
        own, right, opposite, left = exchange([sums] * 4, axis)
        sums = (own + opposite) + (right + left)
    return (projected, token_grad, tile_grad, sums.reshape(-1))


def solution(mesh):
    grid = Mesh(mesh.devices.reshape(4, 4, 2, 4), ALL)
    owners = ("y", "z", "c")
    placed = (P(ALL, None), P(), P(owners, None, None), P(), P(), P(ALL, None))
    return jax.shard_map(
        shards,
        mesh=grid,
        in_specs=placed,
        out_specs=(P(ALL, None), P(ALL, None), P(owners, None, None), P()),
        check_vma=False,
    )
```

```python
import jax
import jax.numpy as jnp
from jax import lax
from jax.experimental import pallas as pl
from jax.experimental.pallas import tpu as pltpu
from jax.sharding import Mesh, PartitionSpec as P

BF = jnp.bfloat16
F4 = jnp.float32
T = 128
ALL = ("y", "z", "c", "x")


def params(limit):
    return pltpu.CompilerParams(vmem_limit_bytes=limit * 1024 * 1024)


def cost(micros, nbytes):
    return pl.CostEstimate(flops=int(micros * 1.1e9), bytes_accessed=nbytes, transcendentals=0)


def whole(shape):
    zeros = (0,) * len(shape)
    return pl.BlockSpec(shape, lambda *_: zeros, pipeline_mode=pl.Buffered(1))


def dot(a, b):
    return jnp.dot(a, b, preferred_element_type=F4)


def dot_t(a, b):
    return lax.dot_general(a, b, (((1,), (1,)), ((), ())), preferred_element_type=F4)


ANY = pl.BlockSpec(memory_space=pl.ANY)


def cols_at(index):
    return pl.ds(pl.multiple_of(index * T, T), T)


def norm_kernel(x_ref, gain_ref, normed_ref, turned_ref, scale_ref):
    count, width = x_ref.shape
    blocks = width // T

    def squares(b, total):
        x = x_ref[:, cols_at(b)].astype(F4)
        return total + x * x

    total = lax.fori_loop(0, blocks, squares, jnp.zeros((count, T), F4), unroll=4)
    scale = lax.rsqrt(jnp.sum(total, axis=1, keepdims=True) / width + 1e-05)
    scale_ref[...] = jnp.broadcast_to(scale, (count, T))

    def fill(b, carry):
        x = x_ref[:, cols_at(b)].astype(F4)
        normed = (x * scale * gain_ref[:, cols_at(b)]).astype(BF)
        normed_ref[:, cols_at(b)] = normed
        turned_ref[b] = normed.T
        return carry

    lax.fori_loop(0, blocks, fill, 0, unroll=4)


def norm(x, gain):
    count, width = x.shape
    return pl.pallas_call(
        norm_kernel,
        out_shape=(
            jax.ShapeDtypeStruct((count, width), BF),
            jax.ShapeDtypeStruct((width // T, T, count), BF),
            jax.ShapeDtypeStruct((count, T), F4),
        ),
        compiler_params=params(56),
        cost_estimate=cost(1, 0),
        name="norm",
    )(x, gain)


def listed(half, ahead, i, y, z, c, x):
    owner = lax.rem(y + i // 8, 4) * 4 + lax.rem(z + i // 2 % 4, 4)
    return owner * 32 + c * 16 + 8 * half + 2 * lax.rem(x + ahead, 4) + i % 2


STEP = 16


def grad_kernel(half, each, rows, cols, pos, turned_ref, turned_other_ref, own_ref, other_ref, *refs):
    at = pl.program_id(0)
    y, z, c, x = pos[0], pos[1], pos[2], pos[3]

    for ahead, out_ref in enumerate(refs[-4:]):

        @pl.when(at // each == ahead)
        def _(ahead=ahead, out_ref=out_ref):
            def one(k, carry):
                index = listed(half, ahead, (at - ahead * each) * STEP + k, y, z, c, x)
                r, q = rows[index], cols[index]
                left = jnp.concatenate([turned_ref[r], turned_other_ref[r]], axis=1)
                right = jnp.concatenate([own_ref[:, cols_at(q)], other_ref[:, cols_at(q)]], axis=0)
                out_ref[k] = dot(left, right).astype(BF)
                return carry

            lax.fori_loop(0, STEP, one, 0, unroll=8)


def grads(half, rows, cols, pos, turned, turned_other, own, other, ties=()):
    piece = 32
    each = piece // STEP

    def out_spec(ahead):
        return pl.BlockSpec((STEP, T, T), lambda i, *_: (jnp.clip(i - ahead * each, 0, each - 1), 0, 0))

    return pl.pallas_call(
        lambda *refs: grad_kernel(half, each, *refs),
        out_shape=[jax.ShapeDtypeStruct((piece, T, T), BF)] * 4,
        grid_spec=pltpu.PrefetchScalarGridSpec(
            num_scalar_prefetch=3,
            grid=(4 * each,),
            in_specs=[whole(a.shape) for a in (turned, turned_other, own, other)] + [ANY] * len(ties),
            out_specs=[out_spec(ahead) for ahead in range(4)],
        ),
        compiler_params=params(40),
        cost_estimate=cost(2, 0),
        name="grads",
    )(rows, cols, pos, turned, turned_other, own, other, *ties)


def project_kernel(
    step, rows, cols, tiles_ref, x_ref, normed_ref, scale_ref, gain_ref, g_ref, *refs
):
    projected_ref, token_grad_ref, sums_ref, out_acc, back_acc = refs[-5:]
    s = pl.program_id(0)
    count, width = x_ref.shape
    blocks = width // T

    @pl.when(s == 0)
    def _():
        out_acc[...] = jnp.zeros_like(out_acc)
        back_acc[...] = jnp.zeros_like(back_acc)

    def one(k, carry):
        r, q = rows[s * step + k], cols[s * step + k]
        weight = tiles_ref[k]
        out_acc[:, cols_at(q)] += dot(normed_ref[:, cols_at(r)], weight)
        back_acc[:, cols_at(r)] += dot_t(g_ref[:, cols_at(q)], weight)
        return carry

    lax.fori_loop(0, step, one, 0, unroll=8)

    @pl.when(s == pl.num_programs(0) - 1)
    def _():
        scale = scale_ref[...]

        def products(b, total):
            at = cols_at(b)
            x = x_ref[:, at].astype(F4)
            back = back_acc[:, at]
            sums_ref[pl.ds(b, 1), :] = jnp.sum(back * x * scale, axis=0, keepdims=True)
            return total + x * gain_ref[:, at] * back

        total = lax.fori_loop(0, blocks, products, jnp.zeros((count, T), F4), unroll=2)
        inner = jnp.sum(total, axis=1, keepdims=True) / width
        cubed = scale * scale * scale * inner

        def finish(b, carry):
            at = cols_at(b)
            x = x_ref[:, at].astype(F4)
            token_grad_ref[:, at] = (scale * gain_ref[:, at] * back_acc[:, at] - x * cubed).astype(BF)
            return carry

        lax.fori_loop(0, blocks, finish, 0, unroll=2)

        def write(b, carry):
            projected_ref[:, cols_at(b)] = out_acc[:, cols_at(b)].astype(BF)
            return carry

        lax.fori_loop(0, g_ref.shape[1] // T, write, 0, unroll=4)


def project(rows, cols, tiles, x, normed, scale, gain, g, ties=()):
    number, step = tiles.shape[0], 32
    count, width = x.shape
    return pl.pallas_call(
        lambda *refs: project_kernel(step, *refs),
        out_shape=(
            jax.ShapeDtypeStruct(g.shape, BF),
            jax.ShapeDtypeStruct(x.shape, BF),
            jax.ShapeDtypeStruct((width // T, T), F4),
        ),
        grid_spec=pltpu.PrefetchScalarGridSpec(
            num_scalar_prefetch=2,
            grid=(number // step,),
            in_specs=[pl.BlockSpec((step, T, T), lambda i, *_: (i, 0, 0))]
            + [whole(a.shape) for a in (x, normed, scale, gain, g)]
            + [ANY] * len(ties),
            out_specs=[whole(g.shape), whole(x.shape), whole((width // T, T))],
            scratch_shapes=[pltpu.VMEM(g.shape, F4), pltpu.VMEM(x.shape, F4)],
        ),
        compiler_params=params(50),
        cost_estimate=cost(2, 0),
        name="project",
    )(rows, cols, tiles, x, normed, scale, gain, g, *ties)


def ring(piece, axis, shift):
    return lax.ppermute(piece, axis, [(i, (i + shift) % 4) for i in range(4)])


def add_four(refs, i):
    a, b, c, d = (r[i].astype(F4) for r in refs)
    return (a + c) + (b + d)


def put_sums(ref, i, value):
    rows = value.shape[0]
    for part in range(3):
        rounded = value.astype(BF)
        ref[i, part * rows : (part + 1) * rows] = rounded
        value = value - rounded.astype(F4)
    ref[i, 3 * rows :] = jnp.zeros((T - 3 * rows, T), BF)


def get_sums(ref, i, rows):
    low, mid, high = (ref[i, part * rows : (part + 1) * rows].astype(F4) for part in (2, 1, 0))
    return (low + mid) + high


def add_sums(refs, i, rows):
    a, b, c, d = (get_sums(r, i, rows) for r in refs)
    return (a + c) + (b + d)


def first_sum(pieces, sums=()):
    each = pieces[0].shape[0] // 4
    more = 1 if sums else 0

    def kernel(*refs):
        outs = refs[-4:]
        total = add_four(refs[:4], ...).astype(BF)
        for ahead, out in enumerate(outs):

            @pl.when(pl.program_id(0) == ahead)
            def _(out=out):
                out[:each] = total
                if sums:
                    put_sums(out, each, refs[4][...] + refs[5][...])

    return pl.pallas_call(
        kernel,
        out_shape=[jax.ShapeDtypeStruct((each + more, T, T), BF)] * 4,
        grid=(4,),
        in_specs=[pl.BlockSpec((each, T, T), lambda i: (i, 0, 0))] * 4 + [whole(a.shape) for a in sums],
        out_specs=[whole((each + more, T, T))] * 4,
        compiler_params=params(32),
        cost_estimate=cost(1, 0),
        name="first_sum",
    )(*pieces, *sums)


def second_sum(plain, with_sums, rows):
    each = plain[0].shape[0] // 4

    def kernel(*refs):
        ins, outs = refs[:8], refs[8:]
        sums = add_sums(ins[4:], 4 * each, rows)
        for ahead, out in enumerate(outs):
            for i in range(each):
                out[i] = add_four(ins[:4], ahead * each + i).astype(BF)
                out[each + i] = add_four(ins[4:], ahead * each + i).astype(BF)
            put_sums(out, 2 * each, sums)

    return pl.pallas_call(
        kernel,
        out_shape=[jax.ShapeDtypeStruct((2 * each + 1, T, T), BF)] * 4,
        in_specs=[pl.BlockSpec(memory_space=pltpu.VMEM)] * 8,
        compiler_params=params(32),
        cost_estimate=cost(1, 0),
        name="second_sum",
    )(*plain, *with_sums)


def third_sum(pieces, rows):
    count = pieces[0].shape[0] - 1

    def kernel(*refs):
        for i in range(count):
            refs[4][i] = add_four(refs[:4], i).astype(BF)
        put_sums(refs[4], count, add_sums(refs[:4], count, rows))

    return pl.pallas_call(
        kernel,
        out_shape=jax.ShapeDtypeStruct((count + 1, T, T), BF),
        in_specs=[pl.BlockSpec(memory_space=pltpu.VMEM)] * 4,
        compiler_params=params(32),
        cost_estimate=cost(1, 0),
        name="third_sum",
    )(*pieces)


def last_sum(pieces, pos, rows):
    def kernel(pos_ref, *refs):
        out_ref, sums_ref = refs[4:]
        for back in range(4):
            source = lax.rem(pos_ref[3] + 4 - back, 4)
            for half in range(2):
                for u in range(2):
                    out_ref[8 * half + 2 * source + u] = refs[back][2 * half + u].astype(F4)
        sums_ref[...] = add_sums(refs[:4], 4, rows)

    return pl.pallas_call(
        kernel,
        out_shape=(jax.ShapeDtypeStruct((16, T, T), F4), jax.ShapeDtypeStruct((rows, T), F4)),
        in_specs=[pl.BlockSpec(memory_space=pltpu.SMEM)] + [pl.BlockSpec(memory_space=pltpu.VMEM)] * 4,
        compiler_params=params(32),
        cost_estimate=cost(1, 0),
        name="last_sum",
    )(pos, *pieces)


def exchange(pieces, axis):
    return [pieces[0]] + [ring(pieces[j], axis, j) for j in (1, 2, 3)]


def shards(tokens, gain, tiles, rows, cols, cotangent):
    gain2 = gain.reshape(1, -1)
    pos = jnp.stack([lax.axis_index(a).astype(jnp.int32) for a in ("y", "z", "c", "x")])
    owners = ("y", "z", "c")
    piece = lax.all_gather(tiles, owners, axis=0, tiled=True)
    swap = [(0, 1), (1, 0)]
    tokens_other = lax.ppermute(tokens, "c", swap)
    g_other = lax.ppermute(cotangent, "c", swap)
    normed, turned, scale = norm(tokens, gain2)
    _, turned_other, _ = norm(tokens_other, gain2)
    part0 = grads(0, rows, cols, pos, turned, turned_other, cotangent, g_other)
    part1 = grads(1, rows, cols, pos, turned, turned_other, cotangent, g_other, (part0[3],))
    mid0 = first_sum(exchange(part0, "x"))
    projected, token_grad, sums = project(
        rows, cols, piece, tokens, normed, scale, gain2, cotangent, (mid0[0],)
    )
    mid1 = first_sum(exchange(part1, "x"), (sums, lax.ppermute(sums, "c", swap)))
    count = sums.shape[0]
    ends = second_sum(exchange(mid0, "y"), exchange(mid1, "y"), count)
    sent = third_sum(exchange(ends, "z"), count)
    tile_grad, sums = last_sum(exchange([sent] * 4, "x"), pos, count)
    return (projected, token_grad, tile_grad, sums.reshape(-1))


def solution(mesh):
    grid = Mesh(mesh.devices.reshape(4, 4, 2, 4), ALL)
    owners = ("y", "z", "c")
    placed = (P(ALL, None), P(), P(owners, None, None), P(), P(), P(ALL, None))
    return jax.shard_map(
        shards,
        mesh=grid,
        in_specs=placed,
        out_specs=(P(ALL, None), P(ALL, None), P(owners, None, None), P()),
        check_vma=False,
    )
```

```python
import jax
import jax.numpy as jnp
from jax import lax
from jax.experimental import pallas as pl
from jax.experimental.pallas import tpu as pltpu
from jax.sharding import Mesh, PartitionSpec as P

BF = jnp.bfloat16
F4 = jnp.float32
T = 128
ALL = ("y", "z", "c", "x")


def params(limit):
    return pltpu.CompilerParams(vmem_limit_bytes=limit * 1024 * 1024)


def cost(micros, nbytes):
    return pl.CostEstimate(flops=int(micros * 1.1e9), bytes_accessed=nbytes, transcendentals=0)


def whole(shape):
    zeros = (0,) * len(shape)
    return pl.BlockSpec(shape, lambda *_: zeros, pipeline_mode=pl.Buffered(1))


def dot(a, b):
    return jnp.dot(a, b, preferred_element_type=F4)


def dot_t(a, b):
    return lax.dot_general(a, b, (((1,), (1,)), ((), ())), preferred_element_type=F4)


ANY = pl.BlockSpec(memory_space=pl.ANY)


def cols_at(index):
    return pl.ds(pl.multiple_of(index * T, T), T)


def norm_kernel(x_ref, gain_ref, normed_ref, turned_ref, scale_ref):
    count, width = x_ref.shape
    blocks = width // T

    def squares(b, total):
        x = x_ref[:, cols_at(b)].astype(F4)
        return total + x * x

    total = lax.fori_loop(0, blocks, squares, jnp.zeros((count, T), F4), unroll=4)
    scale = lax.rsqrt(jnp.sum(total, axis=1, keepdims=True) / width + 1e-05)
    scale_ref[...] = jnp.broadcast_to(scale, (count, T))

    def fill(b, carry):
        x = x_ref[:, cols_at(b)].astype(F4)
        normed = (x * scale * gain_ref[:, cols_at(b)]).astype(BF)
        normed_ref[:, cols_at(b)] = normed
        turned_ref[b] = normed.T
        return carry

    lax.fori_loop(0, blocks, fill, 0, unroll=4)


def norm(x, gain):
    count, width = x.shape
    return pl.pallas_call(
        norm_kernel,
        out_shape=(
            jax.ShapeDtypeStruct((count, width), BF),
            jax.ShapeDtypeStruct((width // T, T, count), BF),
            jax.ShapeDtypeStruct((count, T), F4),
        ),
        compiler_params=params(56),
        cost_estimate=cost(1, 0),
        name="norm",
    )(x, gain)


def first_second(pos):
    y, z, c = pos[0], pos[1], pos[2]
    return jnp.where(c == 0, z, y), jnp.where(c == 0, y, z)


def owned_at(pos, first, second):
    first, second, c = lax.rem(first, 4), lax.rem(second, 4), pos[2]
    return jnp.where(c == 0, second * 4 + first, first * 4 + second) * 32 + c * 16


ORDER = (("x", "y", "z"), ("y", "z", "x"))


def listed(ahead, i, pos):
    y, z, c, x = pos[0], pos[1], pos[2], pos[3]
    one, two, three = ahead, i // 16, i // 4 % 4
    to_x = x + jnp.where(c == 0, one, three)
    to_y = y + jnp.where(c == 0, two, one)
    to_z = z + jnp.where(c == 0, three, two)
    return (lax.rem(to_y, 4) * 4 + lax.rem(to_z, 4)) * 32 + c * 16 + 4 * lax.rem(to_x, 4) + i % 4


STEP = 16


def grad_kernel(each, rows, cols, pos, turned_ref, turned_other_ref, own_ref, other_ref, *refs):
    at = pl.program_id(0)

    for ahead, out_ref in enumerate(refs[-4:]):

        @pl.when(at // each == ahead)
        def _(ahead=ahead, out_ref=out_ref):
            def one(k, carry):
                index = listed(ahead, (at - ahead * each) * STEP + k, pos)
                r, q = rows[index], cols[index]
                left = jnp.concatenate([turned_ref[r], turned_other_ref[r]], axis=1)
                right = jnp.concatenate([own_ref[:, cols_at(q)], other_ref[:, cols_at(q)]], axis=0)
                out_ref[k] = dot(left, right).astype(BF)
                return carry

            lax.fori_loop(0, STEP, one, 0, unroll=8)


def grads(rows, cols, pos, turned, turned_other, own, other, ties=()):
    piece = 64
    each = piece // STEP

    def out_spec(ahead):
        return pl.BlockSpec((STEP, T, T), lambda i, *_: (jnp.clip(i - ahead * each, 0, each - 1), 0, 0))

    return pl.pallas_call(
        lambda *refs: grad_kernel(each, *refs),
        out_shape=[jax.ShapeDtypeStruct((piece, T, T), BF)] * 4,
        grid_spec=pltpu.PrefetchScalarGridSpec(
            num_scalar_prefetch=3,
            grid=(4 * each,),
            in_specs=[whole(a.shape) for a in (turned, turned_other, own, other)] + [ANY] * len(ties),
            out_specs=[out_spec(ahead) for ahead in range(4)],
        ),
        compiler_params=params(40),
        cost_estimate=cost(2, 0),
        name="grads",
    )(rows, cols, pos, turned, turned_other, own, other, *ties)


def share_kernel(
    plan, rows, cols, pos, normed_ref, normed_other_ref, g_ref, g_other_ref, *refs
):
    tile_refs = refs[: len(plan)]
    shared_ref, out_acc, back_acc = refs[-3:]
    at = pl.program_id(0)
    count = normed_ref.shape[0]
    first, second = first_second(pos)

    @pl.when(at == 0)
    def _():
        out_acc[...] = jnp.zeros_like(out_acc)
        back_acc[...] = jnp.zeros_like(back_acc)

    for (behind, offset, start, each), tiles_ref in zip(plan, tile_refs):

        @pl.when((at >= start) & (at < start + each))
        def _(behind=behind, offset=offset, start=start, tiles_ref=tiles_ref):
            def one(k, carry):
                i = offset + (at - start) * 32 + k
                index = owned_at(pos, first + 4 - i // 16, second + 4 - behind) + i % 16
                r, q = cols_at(rows[index]), cols_at(cols[index])
                weight = tiles_ref[k]
                out = dot(jnp.concatenate([normed_ref[:, r], normed_other_ref[:, r]], axis=0), weight)
                back = dot_t(jnp.concatenate([g_ref[:, q], g_other_ref[:, q]], axis=0), weight)
                out_acc[:, q] += out
                back_acc[:, r] += back
                return carry

            lax.fori_loop(0, 32, one, 0, unroll=8)

    @pl.when(at == pl.num_programs(0) - 1)
    def _():
        width = back_acc.shape[1]
        for half, core in ((0, pos[2]), (1, 1 - pos[2])):
            part = slice(half * count, half * count + count)
            shared_ref[core, :, :width] = back_acc[part].astype(BF)
            shared_ref[core, :, width:] = out_acc[part].astype(BF)


def share(rows, cols, pos, blocks, normed, normed_other, g, g_other):
    plan, steps = [], 0
    for tiles, behind, offset in blocks:
        each = tiles.shape[0] // 32
        plan.append((behind, offset, steps, each))
        steps += each

    def tile_spec(start, each):
        return pl.BlockSpec((32, T, T), lambda i, *_: (jnp.clip(i - start, 0, each - 1), 0, 0))

    resident = (normed, normed_other, g, g_other)
    count = g.shape[0]
    shared = (2, count, normed.shape[1] + g.shape[1])
    return pl.pallas_call(
        lambda *refs: share_kernel(plan, *refs),
        out_shape=jax.ShapeDtypeStruct(shared, BF),
        grid_spec=pltpu.PrefetchScalarGridSpec(
            num_scalar_prefetch=3,
            grid=(steps,),
            in_specs=[whole(a.shape) for a in resident] + [tile_spec(start, each) for _, _, start, each in plan],
            out_specs=whole(shared),
            scratch_shapes=[pltpu.VMEM((2 * count, g.shape[1]), F4), pltpu.VMEM((2 * count, normed.shape[1]), F4)],
        ),
        compiler_params=params(56),
        cost_estimate=cost(2, 0),
        name="share",
    )(rows, cols, pos, *resident, *(tiles for tiles, _, _ in blocks))


def finish_kernel(x_ref, scale_ref, gain_ref, parts_ref, shared_ref, *refs):
    projected_ref, token_grad_ref, sums_ref, back_acc = refs[-4:]
    count, width = x_ref.shape
    blocks = width // T
    projected_ref[...] = (shared_ref[0].astype(F4) + shared_ref[1].astype(F4)).astype(BF)

    @pl.when(pl.program_id(0) == 0)
    def _():
        scale = scale_ref[...]

        def products(b, total):
            at = cols_at(b)
            x = x_ref[:, at].astype(F4)
            back = parts_ref[0, :, at].astype(F4) + parts_ref[1, :, at].astype(F4)
            back_acc[:, at] = back
            sums_ref[pl.ds(b, 1), :] = jnp.sum(back * x * scale, axis=0, keepdims=True)
            return total + x * gain_ref[:, at] * back

        total = lax.fori_loop(0, blocks, products, jnp.zeros((count, T), F4), unroll=2)
        inner = jnp.sum(total, axis=1, keepdims=True) / width
        cubed = scale * scale * scale * inner

        def finish(b, carry):
            at = cols_at(b)
            x = x_ref[:, at].astype(F4)
            token_grad_ref[:, at] = (scale * gain_ref[:, at] * back_acc[:, at] - x * cubed).astype(BF)
            return carry

        lax.fori_loop(0, blocks, finish, 0, unroll=2)


def finish(x, scale, gain, shared, ties=()):
    count, width = x.shape
    columns = shared.shape[2] - width
    chunk = columns // 7
    return pl.pallas_call(
        finish_kernel,
        out_shape=(
            jax.ShapeDtypeStruct((count, columns), BF),
            jax.ShapeDtypeStruct(x.shape, BF),
            jax.ShapeDtypeStruct((width // T, T), F4),
        ),
        grid=(7,),
        in_specs=[
            whole(x.shape),
            whole(scale.shape),
            whole(gain.shape),
            whole((2, count, width)),
            pl.BlockSpec((2, count, chunk), lambda i: (0, 0, i + width // chunk)),
        ]
        + [ANY] * len(ties),
        out_specs=[pl.BlockSpec((count, chunk), lambda i: (0, i)), whole(x.shape), whole((width // T, T))],
        scratch_shapes=[pltpu.VMEM(x.shape, F4)],
        compiler_params=params(40),
        cost_estimate=cost(2, 0),
        name="finish",
    )(x, scale, gain, shared, shared, *ties)


def joined(pieces, tie):
    each = pieces[0].shape[0]

    def kernel(*refs):
        for j in range(4):
            refs[-1][j] = refs[j][...]

    return pl.pallas_call(
        kernel,
        out_shape=jax.ShapeDtypeStruct((4, each, T, T), BF),
        grid=(4,),
        in_specs=[pl.BlockSpec((each // 4, T, T), lambda i: (i, 0, 0))] * 4 + [ANY],
        out_specs=pl.BlockSpec((4, each // 4, T, T), lambda i: (0, i, 0, 0)),
        compiler_params=params(32),
        cost_estimate=cost(1, 0),
        name="joined",
    )(*pieces, tie).reshape(4 * each, T, T)


def relayed(left, right, tie):
    half = left.shape[0] // 2

    def kernel(left_ref, right_ref, tie_ref, left_out, right_out):
        left_out[...] = left_ref[...]
        right_out[...] = right_ref[...]

    return pl.pallas_call(
        kernel,
        out_shape=[jax.ShapeDtypeStruct((half, T, T), BF)] * 2,
        grid=(2,),
        in_specs=[
            pl.BlockSpec((half // 2, T, T), lambda i: (i, 0, 0)),
            pl.BlockSpec((half // 2, T, T), lambda i: (2 + i, 0, 0)),
            ANY,
        ],
        out_specs=[pl.BlockSpec((half // 2, T, T), lambda i: (i, 0, 0))] * 2,
        compiler_params=params(32),
        cost_estimate=cost(1, 0),
        name="relayed",
    )(left, right, tie)


def ring(piece, axes, shift):
    if isinstance(axes, str):
        axes = (axes, axes)
    pairs = []
    for source in range(128):
        at = dict(y=source // 32, z=source // 8 % 4, c=source // 4 % 2, x=source % 4)
        axis = axes[at["c"]]
        to = dict(at, **{axis: (at[axis] + shift) % 4})
        pairs.append((source, to["y"] * 32 + to["z"] * 8 + to["c"] * 4 + to["x"]))
    return lax.ppermute(piece, ALL, pairs)


def exchange(pieces, axis):
    return [pieces[0]] + [ring(pieces[j], axis, j) for j in (1, 2, 3)]


def add_four(refs, i):
    a, b, c, d = (r[i].astype(F4) for r in refs)
    return (a + c) + (b + d)


def cut_sum(pieces, ties=()):
    each = pieces[0].shape[0] // 4

    def kernel(*refs):
        total = add_four(refs[:4], ...).astype(BF)
        for ahead, out in enumerate(refs[-4:]):

            @pl.when(pl.program_id(0) == ahead)
            def _(out=out):
                out[...] = total

    return pl.pallas_call(
        kernel,
        out_shape=[jax.ShapeDtypeStruct((each, T, T), BF)] * 4,
        grid=(4,),
        in_specs=[pl.BlockSpec((each, T, T), lambda i: (i, 0, 0))] * 4 + [ANY] * len(ties),
        out_specs=[whole((each, T, T))] * 4,
        compiler_params=params(32),
        cost_estimate=cost(1, 0),
        name="cut_sum",
    )(*pieces, *ties)


def join_sums(groups, ties=()):
    arrays = [a for group in groups for a in group]
    total = sum(group[0].shape[0] for group in groups)

    def kernel(*refs):
        at = 0
        for g, group in enumerate(groups):
            for i in range(group[0].shape[0]):
                refs[-1][at] = add_four(refs[4 * g : 4 * g + 4], i).astype(BF)
                at += 1

    return pl.pallas_call(
        kernel,
        out_shape=jax.ShapeDtypeStruct((total, T, T), BF),
        in_specs=[pl.BlockSpec(memory_space=pltpu.VMEM)] * len(arrays) + [ANY] * len(ties),
        compiler_params=params(32),
        cost_estimate=cost(1, 0),
        name="join_sums",
    )(*arrays, *ties)


def place(pieces, pos):
    def kernel(pos_ref, *refs):
        for back in range(4):
            source = lax.rem(pos_ref[3] + 4 - back, 4)
            for u in range(4):
                refs[-1][4 * source + u] = refs[back][u].astype(F4)

    return pl.pallas_call(
        kernel,
        out_shape=jax.ShapeDtypeStruct((16, T, T), F4),
        in_specs=[pl.BlockSpec(memory_space=pltpu.SMEM)] + [pl.BlockSpec(memory_space=pltpu.VMEM)] * 4,
        compiler_params=params(32),
        cost_estimate=cost(1, 0),
        name="place",
    )(pos, *pieces)


def shards(tokens, gain, tiles, rows, cols, cotangent):
    gain2 = gain.reshape(1, -1)
    pos = jnp.stack([lax.axis_index(a).astype(jnp.int32) for a in ("y", "z", "c", "x")])
    first, second = ("z", "y"), ("y", "z")
    one, two, three = (tuple(order[k] for order in ORDER) for k in range(3))
    swap = [(0, 1), (1, 0)]
    tokens_other = lax.ppermute(tokens, "c", swap)
    g_other = lax.ppermute(cotangent, "c", swap)
    normed, turned, scale = norm(tokens, gain2)
    normed_other, turned_other, _ = norm(tokens_other, gain2)
    line = joined(exchange([tiles] * 4, first), turned_other)
    left, right = ring(line, second, 1), ring(line, second, 3)
    part = grads(rows, cols, pos, turned, turned_other, cotangent, g_other)
    left_half, right_half = relayed(left, right, part[3])
    blocks = [
        (line, 0, 0),
        (left, 1, 0),
        (right, 3, 0),
        (ring(left_half, second, 1), 2, 0),
        (ring(right_half, second, 3), 2, 32),
    ]
    shared = share(rows, cols, pos, blocks, normed, normed_other, cotangent, g_other)
    shared = lax.all_to_all(shared, "c", 0, 0, tiled=True)
    mid = cut_sum(exchange(part, one), (shared,))
    projected, token_grad, sums = finish(tokens, scale, gain2, shared, (mid[0],))
    ends = cut_sum(exchange(mid, two), (sums,))
    sent = join_sums([exchange(ends, three)])
    tile_grad = place(exchange([sent] * 4, "x"), pos)
    sums = sums + lax.ppermute(sums, "c", swap)
    for axis in ("z", "y", "x"):
        own, right, opposite, left = exchange([sums] * 4, axis)
        sums = (own + opposite) + (right + left)
    return (projected, token_grad, tile_grad, sums.reshape(-1))


def solution(mesh):
    grid = Mesh(mesh.devices.reshape(4, 4, 2, 4), ALL)
    owners = ("y", "z", "c")
    placed = (P(ALL, None), P(), P(owners, None, None), P(), P(), P(ALL, None))
    return jax.shard_map(
        shards,
        mesh=grid,
        in_specs=placed,
        out_specs=(P(ALL, None), P(ALL, None), P(owners, None, None), P()),
        check_vma=False,
    )
```

```python
import jax
import jax.numpy as jnp
from jax import lax
from jax.experimental import pallas as pl
from jax.experimental.pallas import tpu as pltpu
from jax.sharding import Mesh, PartitionSpec as P

BF = jnp.bfloat16
F4 = jnp.float32
T = 128
ALL = ("y", "z", "c", "x")


def params(limit):
    return pltpu.CompilerParams(vmem_limit_bytes=limit * 1024 * 1024)


def cost(micros, nbytes):
    return pl.CostEstimate(flops=int(micros * 1.1e9), bytes_accessed=nbytes, transcendentals=0)


def whole(shape):
    zeros = (0,) * len(shape)
    return pl.BlockSpec(shape, lambda *_: zeros, pipeline_mode=pl.Buffered(1))


def dot(a, b):
    return jnp.dot(a, b, preferred_element_type=F4)


def dot_t(a, b):
    return lax.dot_general(a, b, (((1,), (1,)), ((), ())), preferred_element_type=F4)


ANY = pl.BlockSpec(memory_space=pl.ANY)


def cols_at(index):
    return pl.ds(pl.multiple_of(index * T, T), T)


def norm_kernel(x_ref, gain_ref, normed_ref, turned_ref, scale_ref):
    count, width = x_ref.shape
    blocks = width // T

    def squares(b, total):
        x = x_ref[:, cols_at(b)].astype(F4)
        return total + x * x

    total = lax.fori_loop(0, blocks, squares, jnp.zeros((count, T), F4), unroll=4)
    scale = lax.rsqrt(jnp.sum(total, axis=1, keepdims=True) / width + 1e-05)
    scale_ref[...] = jnp.broadcast_to(scale, (count, T))

    def fill(b, carry):
        x = x_ref[:, cols_at(b)].astype(F4)
        normed = (x * scale * gain_ref[:, cols_at(b)]).astype(BF)
        normed_ref[:, cols_at(b)] = normed
        turned_ref[b] = normed.T
        return carry

    lax.fori_loop(0, blocks, fill, 0, unroll=4)


def norm(x, gain):
    count, width = x.shape
    return pl.pallas_call(
        norm_kernel,
        out_shape=(
            jax.ShapeDtypeStruct((count, width), BF),
            jax.ShapeDtypeStruct((width // T, T, count), BF),
            jax.ShapeDtypeStruct((count, T), F4),
        ),
        compiler_params=params(56),
        cost_estimate=cost(1, 0),
        name="norm",
    )(x, gain)


def owned_at(pos, core, to_first, to_second):
    to_z = jnp.where(core == 0, to_first, to_second)
    to_y = jnp.where(core == 0, to_second, to_first)
    return (lax.rem(pos[0] + to_y, 4) * 4 + lax.rem(pos[1] + to_z, 4)) * 32 + core * 16


ORDER = (("x", "y", "z"), ("y", "z", "x"))


def listed(ahead, i, pos):
    y, z, c, x = pos[0], pos[1], pos[2], pos[3]
    one, two, three = ahead, i // 16, i // 4 % 4
    to_x = x + jnp.where(c == 0, one, three)
    to_y = y + jnp.where(c == 0, two, one)
    to_z = z + jnp.where(c == 0, three, two)
    return (lax.rem(to_y, 4) * 4 + lax.rem(to_z, 4)) * 32 + c * 16 + 4 * lax.rem(to_x, 4) + i % 4


STEP = 16


def grad_kernel(aheads, each, rows, cols, pos, turned_ref, turned_other_ref, own_ref, other_ref, *refs):
    at = pl.program_id(0)

    for k, (ahead, out_ref) in enumerate(zip(aheads, refs[-len(aheads) :])):

        @pl.when(at // each == k)
        def _(k=k, ahead=ahead, out_ref=out_ref):
            def one(t, carry):
                index = listed(ahead, (at - k * each) * STEP + t, pos)
                r, q = rows[index], cols[index]
                left = jnp.concatenate([turned_ref[r], turned_other_ref[r]], axis=1)
                right = jnp.concatenate([own_ref[:, cols_at(q)], other_ref[:, cols_at(q)]], axis=0)
                out_ref[t] = dot(left, right).astype(BF)
                return carry

            lax.fori_loop(0, STEP, one, 0, unroll=8)


def grads(aheads, rows, cols, pos, turned, turned_other, own, other, carried=(), ties=()):
    piece = 64
    each = piece // STEP

    def out_spec(k):
        return pl.BlockSpec((STEP, T, T), lambda i, *_: (jnp.clip(i - k * each, 0, each - 1), 0, 0))

    resident = (turned, turned_other, own, other)
    return pl.pallas_call(
        lambda *refs: grad_kernel(aheads, each, *refs),
        out_shape=[jax.ShapeDtypeStruct(a.shape, a.dtype) for a in carried]
        + [jax.ShapeDtypeStruct((piece, T, T), BF)] * len(aheads),
        grid_spec=pltpu.PrefetchScalarGridSpec(
            num_scalar_prefetch=3,
            grid=(len(aheads) * each,),
            in_specs=[whole(a.shape) for a in resident] + [ANY] * (len(carried) + len(ties)),
            out_specs=[ANY] * len(carried) + [out_spec(k) for k in range(len(aheads))],
        ),
        input_output_aliases={7 + k: k for k in range(len(carried))},
        compiler_params=params(40),
        cost_estimate=cost(2, 0),
        name="grads",
    )(rows, cols, pos, *resident, *carried, *ties)


def project_kernel(plan, rows, cols, pos, x_ref, normed_ref, scale_ref, gain_ref, g_ref, *refs):
    projected_ref, token_grad_ref, sums_ref, out_acc, back_acc = refs[-5:]
    s = pl.program_id(0)
    count, width = x_ref.shape
    blocks = width // T

    @pl.when(s == 0)
    def _():
        out_acc[...] = jnp.zeros_like(out_acc)
        back_acc[...] = jnp.zeros_like(back_acc)

    for (other, behind, offset, start, each), tiles_ref in zip(plan, refs):

        @pl.when((s >= start) & (s < start + each))
        def _(other=other, behind=behind, offset=offset, start=start, tiles_ref=tiles_ref):
            core = 1 - pos[2] if other else pos[2]

            def one(k, carry):
                i = offset + (s - start) * 32 + k
                index = owned_at(pos, core, 4 - i // 16, 4 - behind) + i % 16
                r, q = cols_at(rows[index]), cols_at(cols[index])
                weight = tiles_ref[k]
                out_acc[:, q] += dot(normed_ref[:, r], weight)
                back_acc[:, r] += dot_t(g_ref[:, q], weight)
                return carry

            lax.fori_loop(0, 32, one, 0, unroll=8)

    @pl.when(s == pl.num_programs(0) - 1)
    def _():
        scale = scale_ref[...]

        def products(b, total):
            at = cols_at(b)
            x = x_ref[:, at].astype(F4)
            back = back_acc[:, at]
            sums_ref[pl.ds(b, 1), :] = jnp.sum(back * x * scale, axis=0, keepdims=True)
            return total + x * gain_ref[:, at] * back

        total = lax.fori_loop(0, blocks, products, jnp.zeros((count, T), F4), unroll=2)
        inner = jnp.sum(total, axis=1, keepdims=True) / width
        cubed = scale * scale * scale * inner

        def finish(b, carry):
            at = cols_at(b)
            x = x_ref[:, at].astype(F4)
            token_grad_ref[:, at] = (scale * gain_ref[:, at] * back_acc[:, at] - x * cubed).astype(BF)
            return carry

        lax.fori_loop(0, blocks, finish, 0, unroll=2)

        def write(b, carry):
            projected_ref[:, cols_at(b)] = out_acc[:, cols_at(b)].astype(BF)
            return carry

        lax.fori_loop(0, g_ref.shape[1] // T, write, 0, unroll=4)


def project(rows, cols, pos, arrays, x, normed, scale, gain, g):
    plan, steps = [], 0
    for tiles, other, behind, offset in arrays:
        each = tiles.shape[0] // 32
        plan.append((other, behind, offset, steps, each))
        steps += each

    def tile_spec(start, each):
        return pl.BlockSpec((32, T, T), lambda i, *_: (jnp.clip(i - start, 0, each - 1), 0, 0))

    resident = (x, normed, scale, gain, g)
    sums = (x.shape[1] // T, T)
    return pl.pallas_call(
        lambda *refs: project_kernel(plan, *refs),
        out_shape=(
            jax.ShapeDtypeStruct(g.shape, BF),
            jax.ShapeDtypeStruct(x.shape, BF),
            jax.ShapeDtypeStruct(sums, F4),
        ),
        grid_spec=pltpu.PrefetchScalarGridSpec(
            num_scalar_prefetch=3,
            grid=(steps,),
            in_specs=[whole(a.shape) for a in resident] + [tile_spec(p[3], p[4]) for p in plan],
            out_specs=[whole(g.shape), whole(x.shape), whole(sums)],
            scratch_shapes=[pltpu.VMEM(g.shape, F4), pltpu.VMEM(x.shape, F4)],
        ),
        compiler_params=params(54),
        cost_estimate=cost(2, 0),
        name="project",
    )(rows, cols, pos, *resident, *(a[0] for a in arrays))


def joined(pieces, tie):
    each = pieces[0].shape[0]

    def kernel(*refs):
        for j in range(4):
            refs[-1][j] = refs[j][...]

    return pl.pallas_call(
        kernel,
        out_shape=jax.ShapeDtypeStruct((4, each, T, T), BF),
        grid=(4,),
        in_specs=[pl.BlockSpec((each // 4, T, T), lambda i: (i, 0, 0))] * 4 + [ANY],
        out_specs=pl.BlockSpec((4, each // 4, T, T), lambda i: (0, i, 0, 0)),
        compiler_params=params(32),
        cost_estimate=cost(1, 0),
        name="joined",
    )(*pieces, tie).reshape(4 * each, T, T)


def held(values, tie):
    return pl.pallas_call(
        lambda *refs: None,
        out_shape=[jax.ShapeDtypeStruct(a.shape, a.dtype) for a in values],
        in_specs=[ANY] * (len(values) + 1),
        out_specs=[ANY] * len(values),
        input_output_aliases={k: k for k in range(len(values))},
        cost_estimate=cost(1, 0),
        name="held",
    )(*values, tie)


def relayed(left, right, tie):
    half = left.shape[0] // 2

    def kernel(left_ref, right_ref, tie_ref, left_out, right_out):
        left_out[...] = left_ref[...]
        right_out[...] = right_ref[...]

    return pl.pallas_call(
        kernel,
        out_shape=[jax.ShapeDtypeStruct((half, T, T), BF)] * 2,
        grid=(2,),
        in_specs=[
            pl.BlockSpec((half // 2, T, T), lambda i: (i, 0, 0)),
            pl.BlockSpec((half // 2, T, T), lambda i: (2 + i, 0, 0)),
            ANY,
        ],
        out_specs=[pl.BlockSpec((half // 2, T, T), lambda i: (i, 0, 0))] * 2,
        compiler_params=params(32),
        cost_estimate=cost(1, 0),
        name="relayed",
    )(left, right, tie)


def ring(piece, axes, shift):
    if isinstance(axes, str):
        axes = (axes, axes)
    pairs = []
    for source in range(128):
        at = dict(y=source // 32, z=source // 8 % 4, c=source // 4 % 2, x=source % 4)
        axis = axes[at["c"]]
        to = dict(at, **{axis: (at[axis] + shift) % 4})
        pairs.append((source, to["y"] * 32 + to["z"] * 8 + to["c"] * 4 + to["x"]))
    return lax.ppermute(piece, ALL, pairs)


def exchange(pieces, axis):
    return [pieces[0]] + [ring(pieces[j], axis, j) for j in (1, 2, 3)]


def add_four(refs, i):
    a, b, c, d = (r[i].astype(F4) for r in refs)
    return (a + c) + (b + d)


def put_sums(ref, i, value):
    rows = value.shape[0]
    for part in range(3):
        rounded = value.astype(BF)
        ref[i, part * rows : (part + 1) * rows] = rounded
        value = value - rounded.astype(F4)
    ref[i, 3 * rows :] = jnp.zeros((T - 3 * rows, T), BF)


def get_sums(ref, i, rows):
    low, mid, high = (ref[i, part * rows : (part + 1) * rows].astype(F4) for part in (2, 1, 0))
    return (low + mid) + high


def add_sums(refs, i, rows):
    a, b, c, d = (get_sums(r, i, rows) for r in refs)
    return (a + c) + (b + d)


def cut_sum(pieces, sums):
    each = pieces[0].shape[0] // 4

    def kernel(*refs):
        total = add_four(refs[:4], ...).astype(BF)
        for ahead, out in enumerate(refs[-4:]):

            @pl.when(pl.program_id(0) == ahead)
            def _(out=out):
                out[:each] = total
                put_sums(out, each, refs[4][...] + refs[5][...])

    return pl.pallas_call(
        kernel,
        out_shape=[jax.ShapeDtypeStruct((each + 1, T, T), BF)] * 4,
        grid=(4,),
        in_specs=[pl.BlockSpec((each, T, T), lambda i: (i, 0, 0))] * 4 + [whole(a.shape) for a in sums],
        out_specs=[whole((each + 1, T, T))] * 4,
        compiler_params=params(32),
        cost_estimate=cost(1, 0),
        name="cut_sum",
    )(*pieces, *sums)


def next_sum(pieces, rows, cuts):
    each = (pieces[0].shape[0] - 1) // cuts

    def kernel(*refs):
        sums = add_sums(refs[:4], cuts * each, rows)
        for ahead, out in enumerate(refs[4:]):
            for i in range(each):
                out[i] = add_four(refs[:4], ahead * each + i).astype(BF)
            put_sums(out, each, sums)

    return pl.pallas_call(
        kernel,
        out_shape=[jax.ShapeDtypeStruct((each + 1, T, T), BF)] * cuts,
        in_specs=[pl.BlockSpec(memory_space=pltpu.VMEM)] * 4,
        compiler_params=params(32),
        cost_estimate=cost(1, 0),
        name="next_sum",
    )(*pieces)


def place(pieces, pos, rows):
    def kernel(pos_ref, *refs):
        out_ref, sums_ref = refs[4:]
        for back in range(4):
            source = lax.rem(pos_ref[3] + 4 - back, 4)
            for u in range(4):
                out_ref[4 * source + u] = refs[back][u].astype(F4)
        sums_ref[...] = add_sums(refs[:4], 4, rows)

    return pl.pallas_call(
        kernel,
        out_shape=(jax.ShapeDtypeStruct((16, T, T), F4), jax.ShapeDtypeStruct((rows, T), F4)),
        in_specs=[pl.BlockSpec(memory_space=pltpu.SMEM)] + [pl.BlockSpec(memory_space=pltpu.VMEM)] * 4,
        compiler_params=params(32),
        cost_estimate=cost(1, 0),
        name="place",
    )(pos, *pieces)


def shards(tokens, gain, tiles, rows, cols, cotangent):
    gain2 = gain.reshape(1, -1)
    pos = jnp.stack([lax.axis_index(a).astype(jnp.int32) for a in ("y", "z", "c", "x")])
    first, second = ("z", "y"), ("y", "z")
    one, two, three = (tuple(order[k] for order in ORDER) for k in range(3))

    def other_core(value):
        return lax.ppermute(value, "c", [(0, 1), (1, 0)])

    tokens_other, g_other = other_core(tokens), other_core(cotangent)
    normed, turned, scale = norm(tokens, gain2)
    _, turned_other, _ = norm(tokens_other, gain2)
    line = joined(exchange([tiles] * 4, first), turned_other)
    left, right = ring(line, second, 1), ring(line, second, 3)
    operands = (rows, cols, pos, turned, turned_other, cotangent, g_other)
    part0, part2 = grads((0, 2), *operands)
    left_half, right_half = relayed(left, right, part0)
    left, right = held((left, right), left_half)
    part0, part2, part1, part3 = grads((1, 3), *operands, (part0, part2), (left_half,))
    far0, far1 = held((ring(left_half, second, 1), ring(right_half, second, 3)), part3)
    blocks = [(line, 0, 0), (left, 1, 0), (right, 3, 0), (far0, 2, 0), (far1, 2, 32)]
    arrays = [(block, False, *where) for block, *where in blocks]
    arrays += [(other_core(block), True, *where) for block, *where in blocks]
    projected, token_grad, sums = project(rows, cols, pos, arrays, tokens, normed, scale, gain2, cotangent)
    count = sums.shape[0]
    mid = cut_sum(exchange([part0, part1, part2, part3], one), (sums, other_core(sums)))
    ends = next_sum(exchange(mid, two), count, 4)
    (sent,) = next_sum(exchange(ends, three), count, 1)
    tile_grad, sums = place(exchange([sent] * 4, "x"), pos, count)
    sums = jnp.where(pos[2] == 0, sums, other_core(sums))
    return (projected, token_grad, tile_grad, sums.reshape(-1))


def solution(mesh):
    grid = Mesh(mesh.devices.reshape(4, 4, 2, 4), ALL)
    owners = ("y", "z", "c")
    placed = (P(ALL, None), P(), P(owners, None, None), P(), P(), P(ALL, None))
    return jax.shard_map(
        shards,
        mesh=grid,
        in_specs=placed,
        out_specs=(P(ALL, None), P(ALL, None), P(owners, None, None), P()),
        check_vma=False,
    )
```

```python
import jax
import jax.numpy as jnp
from jax import lax
from jax.experimental import pallas as pl
from jax.experimental.pallas import tpu as pltpu
from jax.sharding import Mesh, PartitionSpec as P

BF = jnp.bfloat16
F4 = jnp.float32
T = 128
ALL = ("y", "z", "c", "x")


def params(limit):
    return pltpu.CompilerParams(vmem_limit_bytes=limit * 1024 * 1024)


def cost(micros, nbytes):
    return pl.CostEstimate(flops=int(micros * 1.1e9), bytes_accessed=nbytes, transcendentals=0)


def whole(shape):
    zeros = (0,) * len(shape)
    return pl.BlockSpec(shape, lambda *_: zeros, pipeline_mode=pl.Buffered(1))


def dot(a, b):
    return jnp.dot(a, b, preferred_element_type=F4)


def dot_t(a, b):
    return lax.dot_general(a, b, (((1,), (1,)), ((), ())), preferred_element_type=F4)


ANY = pl.BlockSpec(memory_space=pl.ANY)


def cols_at(index):
    return pl.ds(pl.multiple_of(index * T, T), T)


def norm_kernel(x_ref, gain_ref, normed_ref, turned_ref, scale_ref):
    count, width = x_ref.shape
    blocks = width // T

    def squares(b, total):
        x = x_ref[:, cols_at(b)].astype(F4)
        return total + x * x

    total = lax.fori_loop(0, blocks, squares, jnp.zeros((count, T), F4), unroll=4)
    scale = lax.rsqrt(jnp.sum(total, axis=1, keepdims=True) / width + 1e-05)
    scale_ref[...] = jnp.broadcast_to(scale, (count, T))

    def fill(b, carry):
        x = x_ref[:, cols_at(b)].astype(F4)
        normed = (x * scale * gain_ref[:, cols_at(b)]).astype(BF)
        normed_ref[:, cols_at(b)] = normed
        turned_ref[b] = normed.T
        return carry

    lax.fori_loop(0, blocks, fill, 0, unroll=4)


def norm(x, gain):
    count, width = x.shape
    return pl.pallas_call(
        norm_kernel,
        out_shape=(
            jax.ShapeDtypeStruct((count, width), BF),
            jax.ShapeDtypeStruct((width // T, T, count), BF),
            jax.ShapeDtypeStruct((count, T), F4),
        ),
        compiler_params=params(60),
        cost_estimate=cost(1, 0),
        name="norm",
    )(x, gain)


def owned_at(pos, core, to_first, to_second):
    to_z = jnp.where(core == 0, to_first, to_second)
    to_y = jnp.where(core == 0, to_second, to_first)
    return (lax.rem(pos[0] + to_y, 4) * 4 + lax.rem(pos[1] + to_z, 4)) * 32 + core * 16


ORDER = (("x", "y", "z"), ("y", "z", "x"))


def listed(ahead, i, pos):
    y, z, c, x = pos[0], pos[1], pos[2], pos[3]
    one, two, three = ahead, i // 16, i // 4 % 4
    to_x = x + jnp.where(c == 0, one, three)
    to_y = y + jnp.where(c == 0, two, one)
    to_z = z + jnp.where(c == 0, three, two)
    return (lax.rem(to_y, 4) * 4 + lax.rem(to_z, 4)) * 32 + c * 16 + 4 * lax.rem(to_x, 4) + i % 4


STEP = 16


def grad_kernel(aheads, each, rows, cols, pos, turned_ref, turned_other_ref, own_ref, other_ref, *refs):
    at = pl.program_id(0)

    for k, (ahead, out_ref) in enumerate(zip(aheads, refs[-len(aheads) :])):

        @pl.when(at // each == k)
        def _(k=k, ahead=ahead, out_ref=out_ref):
            def one(t, carry):
                index = listed(ahead, (at - k * each) * STEP + t, pos)
                r, q = rows[index], cols[index]
                left = jnp.concatenate([turned_ref[r], turned_other_ref[r]], axis=1)
                right = jnp.concatenate([own_ref[:, cols_at(q)], other_ref[:, cols_at(q)]], axis=0)
                out_ref[t] = dot(left, right).astype(BF)
                return carry

            lax.fori_loop(0, STEP, one, 0, unroll=8)


def grads(aheads, rows, cols, pos, turned, turned_other, own, other, carried=(), ties=()):
    piece = 64
    each = piece // STEP

    def out_spec(k):
        return pl.BlockSpec((STEP, T, T), lambda i, *_: (jnp.clip(i - k * each, 0, each - 1), 0, 0))

    resident = (turned, turned_other, own, other)
    return pl.pallas_call(
        lambda *refs: grad_kernel(aheads, each, *refs),
        out_shape=[jax.ShapeDtypeStruct(a.shape, a.dtype) for a in carried]
        + [jax.ShapeDtypeStruct((piece, T, T), BF)] * len(aheads),
        grid_spec=pltpu.PrefetchScalarGridSpec(
            num_scalar_prefetch=3,
            grid=(len(aheads) * each,),
            in_specs=[whole(a.shape) for a in resident] + [ANY] * (len(carried) + len(ties)),
            out_specs=[ANY] * len(carried) + [out_spec(k) for k in range(len(aheads))],
        ),
        input_output_aliases={7 + k: k for k in range(len(carried))},
        compiler_params=params(60),
        cost_estimate=cost(2, 0),
        name="grads",
    )(rows, cols, pos, *resident, *carried, *ties)


def project_kernel(sources, rows, cols, pos, x_ref, normed_ref, scale_ref, gain_ref, g_ref, *refs):
    projected_ref, token_grad_ref, sums_ref, out_acc, back_acc, held_ref, sem = refs[-7:]
    s = pl.program_id(0)
    count, width = x_ref.shape
    blocks = width // T
    slot = lax.rem(s, 2)

    def fetch(k):
        array, offset = sources[k]
        pltpu.make_async_copy(refs[array].at[pl.ds(offset, 32)], held_ref.at[k % 2], sem.at[k % 2]).start()

    @pl.when(s == 0)
    def _():
        fetch(0)
        out_acc[...] = jnp.zeros_like(out_acc)
        back_acc[...] = jnp.zeros_like(back_acc)

    for k in range(1, len(sources)):

        @pl.when(s == k - 1)
        def _(k=k):
            fetch(k)

    pltpu.make_async_copy(refs[0].at[pl.ds(0, 32)], held_ref.at[slot], sem.at[slot]).wait()
    core = jnp.where(s < 8, pos[2], 1 - pos[2])
    pair = lax.rem(s, 8) // 2
    behind = jnp.where(pair < 2, pair, 5 - pair)

    def one(k, carry):
        i = lax.rem(s, 2) * 32 + k
        index = owned_at(pos, core, 4 - i // 16, 4 - behind) + i % 16
        r, q = cols_at(rows[index]), cols_at(cols[index])
        weight = held_ref[slot, k]
        out_acc[:, q] += dot(normed_ref[:, r], weight)
        back_acc[:, r] += dot_t(g_ref[:, q], weight)
        return carry

    lax.fori_loop(0, 32, one, 0, unroll=8)

    @pl.when(s == pl.num_programs(0) - 1)
    def _():
        scale = scale_ref[...]

        def products(b, total):
            at = cols_at(b)
            x = x_ref[:, at].astype(F4)
            back = back_acc[:, at]
            sums_ref[pl.ds(b, 1), :] = jnp.sum(back * x * scale, axis=0, keepdims=True)
            return total + x * gain_ref[:, at] * back

        total = lax.fori_loop(0, blocks, products, jnp.zeros((count, T), F4), unroll=2)
        inner = jnp.sum(total, axis=1, keepdims=True) / width
        cubed = scale * scale * scale * inner

        def finish(b, carry):
            at = cols_at(b)
            x = x_ref[:, at].astype(F4)
            token_grad_ref[:, at] = (scale * gain_ref[:, at] * back_acc[:, at] - x * cubed).astype(BF)
            return carry

        lax.fori_loop(0, blocks, finish, 0, unroll=2)

        def write(b, carry):
            projected_ref[:, cols_at(b)] = out_acc[:, cols_at(b)].astype(BF)
            return carry

        lax.fori_loop(0, g_ref.shape[1] // T, write, 0, unroll=4)


def project(rows, cols, pos, arrays, x, normed, scale, gain, g):
    sources = [(k, offset) for k, tiles in enumerate(arrays) for offset in range(0, tiles.shape[0], 32)]
    resident = (x, normed, scale, gain, g)
    sums = (x.shape[1] // T, T)
    return pl.pallas_call(
        lambda *refs: project_kernel(sources, *refs),
        out_shape=(
            jax.ShapeDtypeStruct(g.shape, BF),
            jax.ShapeDtypeStruct(x.shape, BF),
            jax.ShapeDtypeStruct(sums, F4),
        ),
        grid_spec=pltpu.PrefetchScalarGridSpec(
            num_scalar_prefetch=3,
            grid=(len(sources),),
            in_specs=[whole(a.shape) for a in resident] + [ANY] * len(arrays),
            out_specs=[whole(g.shape), whole(x.shape), whole(sums)],
            scratch_shapes=[
                pltpu.VMEM(g.shape, F4),
                pltpu.VMEM(x.shape, F4),
                pltpu.VMEM((2, 32, T, T), BF),
                pltpu.SemaphoreType.DMA((2,)),
            ],
        ),
        compiler_params=params(60),
        cost_estimate=cost(2, 0),
        name="project",
    )(rows, cols, pos, *resident, *arrays)


def joined(pieces, tie):
    each = pieces[0].shape[0]

    def kernel(*refs):
        for j in range(4):
            refs[-1][j] = refs[j][...]

    return pl.pallas_call(
        kernel,
        out_shape=jax.ShapeDtypeStruct((4, each, T, T), BF),
        grid=(4,),
        in_specs=[pl.BlockSpec((each // 4, T, T), lambda i: (i, 0, 0))] * 4 + [ANY],
        out_specs=pl.BlockSpec((4, each // 4, T, T), lambda i: (0, i, 0, 0)),
        compiler_params=params(32),
        cost_estimate=cost(1, 0),
        name="joined",
    )(*pieces, tie).reshape(4 * each, T, T)


def held(values, *ties):
    return pl.pallas_call(
        lambda *refs: None,
        out_shape=[jax.ShapeDtypeStruct(a.shape, a.dtype) for a in values],
        in_specs=[ANY] * (len(values) + len(ties)),
        out_specs=[ANY] * len(values),
        input_output_aliases={k: k for k in range(len(values))},
        cost_estimate=cost(1, 0),
        name="held",
    )(*values, *ties)


def relayed(left, right, tie):
    half = left.shape[0] // 2

    def kernel(left_ref, right_ref, tie_ref, left_out, right_out):
        left_out[...] = left_ref[...]
        right_out[...] = right_ref[...]

    return pl.pallas_call(
        kernel,
        out_shape=[jax.ShapeDtypeStruct((half, T, T), BF)] * 2,
        grid=(2,),
        in_specs=[
            pl.BlockSpec((half // 2, T, T), lambda i: (i, 0, 0)),
            pl.BlockSpec((half // 2, T, T), lambda i: (2 + i, 0, 0)),
            ANY,
        ],
        out_specs=[pl.BlockSpec((half // 2, T, T), lambda i: (i, 0, 0))] * 2,
        compiler_params=params(60),
        cost_estimate=cost(1, 0),
        name="relayed",
    )(left, right, tie)


def ring(piece, axes, shift):
    if isinstance(axes, str):
        axes = (axes, axes)
    pairs = []
    for source in range(128):
        at = dict(y=source // 32, z=source // 8 % 4, c=source // 4 % 2, x=source % 4)
        axis = axes[at["c"]]
        to = dict(at, **{axis: (at[axis] + shift) % 4})
        pairs.append((source, to["y"] * 32 + to["z"] * 8 + to["c"] * 4 + to["x"]))
    return lax.ppermute(piece, ALL, pairs)


def exchange(pieces, axis):
    return [pieces[0]] + [ring(pieces[j], axis, j) for j in (1, 2, 3)]


def add_four(refs, i):
    a, b, c, d = (r[i].astype(F4) for r in refs)
    return (a + c) + (b + d)


def put_sums(ref, i, value):
    rows = value.shape[0]
    for part in range(3):
        rounded = value.astype(BF)
        ref[i, part * rows : (part + 1) * rows] = rounded
        value = value - rounded.astype(F4)
    ref[i, 3 * rows :] = jnp.zeros((T - 3 * rows, T), BF)


def get_sums(ref, i, rows):
    low, mid, high = (ref[i, part * rows : (part + 1) * rows].astype(F4) for part in (2, 1, 0))
    return (low + mid) + high


def add_sums(refs, i, rows):
    a, b, c, d = (get_sums(r, i, rows) for r in refs)
    return (a + c) + (b + d)


def cut_sum(pieces, sums):
    each = pieces[0].shape[0] // 4

    def kernel(*refs):
        total = add_four(refs[:4], ...).astype(BF)
        for ahead, out in enumerate(refs[-4:]):

            @pl.when(pl.program_id(0) == ahead)
            def _(out=out):
                out[:each] = total
                put_sums(out, each, refs[4][...] + refs[5][...])

    return pl.pallas_call(
        kernel,
        out_shape=[jax.ShapeDtypeStruct((each + 1, T, T), BF)] * 4,
        grid=(4,),
        in_specs=[pl.BlockSpec((each, T, T), lambda i: (i, 0, 0))] * 4 + [whole(a.shape) for a in sums],
        out_specs=[whole((each + 1, T, T))] * 4,
        compiler_params=params(32),
        cost_estimate=cost(1, 0),
        name="cut_sum",
    )(*pieces, *sums)


def next_sum(pieces, rows, cuts):
    each = (pieces[0].shape[0] - 1) // cuts

    def kernel(*refs):
        sums = add_sums(refs[:4], cuts * each, rows)
        for ahead, out in enumerate(refs[4:]):
            for i in range(each):
                out[i] = add_four(refs[:4], ahead * each + i).astype(BF)
            put_sums(out, each, sums)

    return pl.pallas_call(
        kernel,
        out_shape=[jax.ShapeDtypeStruct((each + 1, T, T), BF)] * cuts,
        in_specs=[pl.BlockSpec(memory_space=pltpu.VMEM)] * 4,
        compiler_params=params(16),
        cost_estimate=cost(1, 0),
        name="next_sum",
    )(*pieces)


def place(pieces, pos, rows):
    def kernel(pos_ref, *refs):
        out_ref, sums_ref = refs[4:]
        for back in range(4):
            source = lax.rem(pos_ref[3] + 4 - back, 4)
            for u in range(4):
                out_ref[4 * source + u] = refs[back][u].astype(F4)
        sums_ref[...] = add_sums(refs[:4], 4, rows)

    return pl.pallas_call(
        kernel,
        out_shape=(jax.ShapeDtypeStruct((16, T, T), F4), jax.ShapeDtypeStruct((rows, T), F4)),
        in_specs=[pl.BlockSpec(memory_space=pltpu.SMEM)] + [pl.BlockSpec(memory_space=pltpu.VMEM)] * 4,
        compiler_params=params(16),
        cost_estimate=cost(1, 0),
        name="place",
    )(pos, *pieces)


def shards(tokens, gain, tiles, rows, cols, cotangent):
    gain2 = gain.reshape(1, -1)
    pos = jnp.stack([lax.axis_index(a).astype(jnp.int32) for a in ("y", "z", "c", "x")])
    first, second = ("z", "y"), ("y", "z")
    one, two, three = (tuple(order[k] for order in ORDER) for k in range(3))

    def other_core(value):
        return lax.ppermute(value, "c", [(0, 1), (1, 0)])

    tokens_other, g_other = other_core(tokens), other_core(cotangent)
    normed, turned, scale = norm(tokens, gain2)
    _, turned_other, _ = norm(tokens_other, gain2)
    line = joined(exchange([tiles] * 4, first), turned_other)
    left, right = ring(line, second, 1), ring(line, second, 3)
    operands = (rows, cols, pos, turned, turned_other, cotangent, g_other)
    part0, part2, part1 = grads((0, 2, 1), *operands)
    left_half, right_half = relayed(left, right, part0)
    left, right = held((left, right), left_half)
    part0, part2, part1, part3 = grads((3,), *operands, (part0, part2, part1), (left_half,))
    near = [line, left, right]
    swapped = [other_core(block) for block in near]
    far = held((ring(left_half, second, 1), ring(right_half, second, 3)), part3, *swapped)
    arrays = near + list(far) + swapped + [other_core(block) for block in far]
    projected, token_grad, sums = project(rows, cols, pos, arrays, tokens, normed, scale, gain2, cotangent)
    count = sums.shape[0]
    mid = cut_sum(exchange([part0, part1, part2, part3], one), (sums, other_core(sums)))
    ends = next_sum(exchange(mid, two), count, 4)
    (sent,) = next_sum(exchange(ends, three), count, 1)
    tile_grad, sums = place(exchange([sent] * 4, "x"), pos, count)
    sums = jnp.where(pos[2] == 0, sums, other_core(sums))
    return (projected, token_grad, tile_grad, sums.reshape(-1))


def solution(mesh):
    grid = Mesh(mesh.devices.reshape(4, 4, 2, 4), ALL)
    owners = ("y", "z", "c")
    placed = (P(ALL, None), P(), P(owners, None, None), P(), P(), P(ALL, None))
    return jax.shard_map(
        shards,
        mesh=grid,
        in_specs=placed,
        out_specs=(P(ALL, None), P(ALL, None), P(owners, None, None), P()),
        check_vma=False,
    )
```

```python
import jax
import jax.numpy as jnp
from jax import lax
from jax.experimental import pallas as pl
from jax.experimental.pallas import tpu as pltpu
from jax.sharding import Mesh, PartitionSpec as P

BF = jnp.bfloat16
F4 = jnp.float32
T = 128
ALL = ("y", "z", "c", "x")


def params(limit):
    return pltpu.CompilerParams(vmem_limit_bytes=limit * 1024 * 1024)


def cost(micros, nbytes):
    return pl.CostEstimate(flops=int(micros * 1.1e9), bytes_accessed=nbytes, transcendentals=0)


def whole(shape):
    zeros = (0,) * len(shape)
    return pl.BlockSpec(shape, lambda *_: zeros, pipeline_mode=pl.Buffered(1))


def dot(a, b):
    return jnp.dot(a, b, preferred_element_type=F4)


def dot_t(a, b):
    return lax.dot_general(a, b, (((1,), (1,)), ((), ())), preferred_element_type=F4)


ANY = pl.BlockSpec(memory_space=pl.ANY)


def cols_at(index):
    return pl.ds(pl.multiple_of(index * T, T), T)


def norm_kernel(x_ref, gain_ref, normed_ref, turned_ref, scale_ref):
    count, width = x_ref.shape
    blocks = width // T

    def squares(b, total):
        x = x_ref[:, cols_at(b)].astype(F4)
        return total + x * x

    total = lax.fori_loop(0, blocks, squares, jnp.zeros((count, T), F4), unroll=4)
    scale = lax.rsqrt(jnp.sum(total, axis=1, keepdims=True) / width + 1e-05)
    scale_ref[...] = jnp.broadcast_to(scale, (count, T))

    def fill(b, carry):
        x = x_ref[:, cols_at(b)].astype(F4)
        normed = (x * scale * gain_ref[:, cols_at(b)]).astype(BF)
        normed_ref[:, cols_at(b)] = normed
        turned_ref[b] = normed.T
        return carry

    lax.fori_loop(0, blocks, fill, 0, unroll=4)


def norm(x, gain):
    count, width = x.shape
    return pl.pallas_call(
        norm_kernel,
        out_shape=(
            jax.ShapeDtypeStruct((count, width), BF),
            jax.ShapeDtypeStruct((width // T, T, count), BF),
            jax.ShapeDtypeStruct((count, T), F4),
        ),
        compiler_params=params(60),
        cost_estimate=cost(1, 0),
        name="norm",
    )(x, gain)


def owned_at(pos, core, to_first, to_second):
    to_z = jnp.where(core == 0, to_first, to_second)
    to_y = jnp.where(core == 0, to_second, to_first)
    return (lax.rem(pos[0] + to_y, 4) * 4 + lax.rem(pos[1] + to_z, 4)) * 32 + core * 16


ORDER = (("x", "y", "z"), ("y", "z", "x"))


def listed(ahead, i, pos):
    y, z, c, x = pos[0], pos[1], pos[2], pos[3]
    one, two, three = ahead, i // 16, i // 4 % 4
    to_x = x + jnp.where(c == 0, one, three)
    to_y = y + jnp.where(c == 0, two, one)
    to_z = z + jnp.where(c == 0, three, two)
    return (lax.rem(to_y, 4) * 4 + lax.rem(to_z, 4)) * 32 + c * 16 + 4 * lax.rem(to_x, 4) + i % 4


STEP = 16


def grad_kernel(aheads, each, rows, cols, pos, turned_ref, turned_other_ref, own_ref, other_ref, *refs):
    at = pl.program_id(0)

    for k, (ahead, out_ref) in enumerate(zip(aheads, refs[-len(aheads) :])):

        @pl.when(at // each == k)
        def _(k=k, ahead=ahead, out_ref=out_ref):
            def one(t, carry):
                index = listed(ahead, (at - k * each) * STEP + t, pos)
                r, q = rows[index], cols[index]
                left = jnp.concatenate([turned_ref[r], turned_other_ref[r]], axis=1)
                right = jnp.concatenate([own_ref[:, cols_at(q)], other_ref[:, cols_at(q)]], axis=0)
                out_ref[t] = dot(left, right).astype(BF)
                return carry

            lax.fori_loop(0, STEP, one, 0, unroll=8)


def grads(aheads, rows, cols, pos, turned, turned_other, own, other, carried=(), ties=()):
    piece = 64
    each = piece // STEP

    def out_spec(k):
        return pl.BlockSpec((STEP, T, T), lambda i, *_: (jnp.clip(i - k * each, 0, each - 1), 0, 0))

    resident = (turned, turned_other, own, other)
    return pl.pallas_call(
        lambda *refs: grad_kernel(aheads, each, *refs),
        out_shape=[jax.ShapeDtypeStruct(a.shape, a.dtype) for a in carried]
        + [jax.ShapeDtypeStruct((piece, T, T), BF)] * len(aheads),
        grid_spec=pltpu.PrefetchScalarGridSpec(
            num_scalar_prefetch=3,
            grid=(len(aheads) * each,),
            in_specs=[whole(a.shape) for a in resident] + [ANY] * (len(carried) + len(ties)),
            out_specs=[ANY] * len(carried) + [out_spec(k) for k in range(len(aheads))],
        ),
        input_output_aliases={7 + k: k for k in range(len(carried))},
        compiler_params=params(60),
        cost_estimate=cost(2, 0),
        name="grads",
    )(rows, cols, pos, *resident, *carried, *ties)


def project_kernel(sources, rows, cols, pos, x_ref, normed_ref, scale_ref, gain_ref, g_ref, *refs):
    projected_ref, token_grad_ref, sums_ref, out_acc, back_acc, held_ref, sem = refs[-7:]
    s = pl.program_id(0)
    count, width = x_ref.shape
    blocks = width // T
    slot = lax.rem(s, 2)

    def fetch(k):
        array, offset = sources[k]
        pltpu.make_async_copy(refs[array].at[pl.ds(offset, 32)], held_ref.at[k % 2], sem.at[k % 2]).start()

    @pl.when(s == 0)
    def _():
        fetch(0)
        out_acc[...] = jnp.zeros_like(out_acc)
        back_acc[...] = jnp.zeros_like(back_acc)

    for k in range(1, len(sources)):

        @pl.when(s == k - 1)
        def _(k=k):
            fetch(k)

    pltpu.make_async_copy(refs[0].at[pl.ds(0, 32)], held_ref.at[slot], sem.at[slot]).wait()
    core = jnp.where(s < 8, pos[2], 1 - pos[2])
    pair = lax.rem(s, 8) // 2
    behind = jnp.where(pair < 2, pair, 5 - pair)

    def one(k, carry):
        i = lax.rem(s, 2) * 32 + k
        index = owned_at(pos, core, 4 - i // 16, 4 - behind) + i % 16
        r, q = cols_at(rows[index]), cols_at(cols[index])
        weight = held_ref[slot, k]
        out_acc[:, q] += dot(normed_ref[:, r], weight)
        back_acc[:, r] += dot_t(g_ref[:, q], weight)
        return carry

    lax.fori_loop(0, 32, one, 0, unroll=8)

    @pl.when(s == pl.num_programs(0) - 1)
    def _():
        scale = scale_ref[...]

        def products(b, total):
            at = cols_at(b)
            x = x_ref[:, at].astype(F4)
            back = back_acc[:, at]
            sums_ref[pl.ds(b, 1), :] = jnp.sum(back * x * scale, axis=0, keepdims=True)
            return total + x * gain_ref[:, at] * back

        total = lax.fori_loop(0, blocks, products, jnp.zeros((count, T), F4), unroll=2)
        inner = jnp.sum(total, axis=1, keepdims=True) / width
        cubed = scale * scale * scale * inner

        def finish(b, carry):
            at = cols_at(b)
            x = x_ref[:, at].astype(F4)
            token_grad_ref[:, at] = (scale * gain_ref[:, at] * back_acc[:, at] - x * cubed).astype(BF)
            return carry

        lax.fori_loop(0, blocks, finish, 0, unroll=2)

        def write(b, carry):
            projected_ref[:, cols_at(b)] = out_acc[:, cols_at(b)].astype(BF)
            return carry

        lax.fori_loop(0, g_ref.shape[1] // T, write, 0, unroll=4)


def project(rows, cols, pos, arrays, x, normed, scale, gain, g):
    sources = [(k, offset) for k, tiles in enumerate(arrays) for offset in range(0, tiles.shape[0], 32)]
    resident = (x, normed, scale, gain, g)
    sums = (x.shape[1] // T, T)
    return pl.pallas_call(
        lambda *refs: project_kernel(sources, *refs),
        out_shape=(
            jax.ShapeDtypeStruct(g.shape, BF),
            jax.ShapeDtypeStruct(x.shape, BF),
            jax.ShapeDtypeStruct(sums, F4),
        ),
        grid_spec=pltpu.PrefetchScalarGridSpec(
            num_scalar_prefetch=3,
            grid=(len(sources),),
            in_specs=[whole(a.shape) for a in resident] + [ANY] * len(arrays),
            out_specs=[whole(g.shape), whole(x.shape), whole(sums)],
            scratch_shapes=[
                pltpu.VMEM(g.shape, F4),
                pltpu.VMEM(x.shape, F4),
                pltpu.VMEM((2, 32, T, T), BF),
                pltpu.SemaphoreType.DMA((2,)),
            ],
        ),
        compiler_params=params(60),
        cost_estimate=cost(2, 0),
        name="project",
    )(rows, cols, pos, *resident, *arrays)


def moved(plan, shapes, values, ties, name):
    def kernel(*refs):
        outs, sem = refs[-1 - len(shapes) : -1], refs[-1]
        copies = [
            pltpu.make_async_copy(refs[v].at[pl.ds(i, n)], outs[o].at[pl.ds(j, n)], sem.at[k])
            for k, (v, i, o, j, n) in enumerate(plan)
        ]
        for copy in copies:
            copy.start()
        for copy in copies:
            copy.wait()

    return pl.pallas_call(
        kernel,
        out_shape=[jax.ShapeDtypeStruct(shape, BF) for shape in shapes],
        in_specs=[ANY] * (len(values) + len(ties)),
        out_specs=[ANY] * len(shapes),
        scratch_shapes=[pltpu.SemaphoreType.DMA((len(plan),))],
        compiler_params=params(60),
        cost_estimate=cost(1, 0),
        name=name,
    )(*values, *ties)


def joined(pieces, *ties):
    each = pieces[0].shape[0]
    plan = [(j, 0, 0, j * each, each) for j in range(4)]
    return moved(plan, [(4 * each, T, T)], pieces, ties, "joined")[0]


def held(values, *ties):
    return pl.pallas_call(
        lambda *refs: None,
        out_shape=[jax.ShapeDtypeStruct(a.shape, a.dtype) for a in values],
        in_specs=[ANY] * (len(values) + len(ties)),
        out_specs=[ANY] * len(values),
        input_output_aliases={k: k for k in range(len(values))},
        cost_estimate=cost(1, 0),
        name="held",
    )(*values, *ties)


def relayed(left, right, tie):
    half = left.shape[0] // 2
    plan = [(0, 0, 0, 0, half), (1, half, 1, 0, half)]
    return moved(plan, [(half, T, T)] * 2, (left, right), (tie,), "relayed")


def ring(piece, axes, shift):
    if isinstance(axes, str):
        axes = (axes, axes)
    pairs = []
    for source in range(128):
        at = dict(y=source // 32, z=source // 8 % 4, c=source // 4 % 2, x=source % 4)
        axis = axes[at["c"]]
        to = dict(at, **{axis: (at[axis] + shift) % 4})
        pairs.append((source, to["y"] * 32 + to["z"] * 8 + to["c"] * 4 + to["x"]))
    return lax.ppermute(piece, ALL, pairs)


def exchange(pieces, axis):
    return [pieces[0]] + [ring(pieces[j], axis, j) for j in (1, 2, 3)]


def add_four(refs, i):
    a, b, c, d = (r[i].astype(F4) for r in refs)
    return (a + c) + (b + d)


def put_sums(ref, i, value):
    rows = value.shape[0]
    for part in range(3):
        rounded = value.astype(BF)
        ref[i, part * rows : (part + 1) * rows] = rounded
        value = value - rounded.astype(F4)
    ref[i, 3 * rows :] = jnp.zeros((T - 3 * rows, T), BF)


def get_sums(ref, i, rows):
    low, mid, high = (ref[i, part * rows : (part + 1) * rows].astype(F4) for part in (2, 1, 0))
    return (low + mid) + high


def add_sums(refs, i, rows):
    a, b, c, d = (get_sums(r, i, rows) for r in refs)
    return (a + c) + (b + d)


def cut_sum(pieces, sums):
    each = pieces[0].shape[0] // 4

    def kernel(*refs):
        total = add_four(refs[:4], ...).astype(BF)
        for ahead, out in enumerate(refs[-4:]):

            @pl.when(pl.program_id(0) == ahead)
            def _(out=out):
                out[:each] = total
                put_sums(out, each, refs[4][...] + refs[5][...])

    return pl.pallas_call(
        kernel,
        out_shape=[jax.ShapeDtypeStruct((each + 1, T, T), BF)] * 4,
        grid=(4,),
        in_specs=[pl.BlockSpec((each, T, T), lambda i: (i, 0, 0))] * 4 + [whole(a.shape) for a in sums],
        out_specs=[whole((each + 1, T, T))] * 4,
        compiler_params=params(32),
        cost_estimate=cost(1, 0),
        name="cut_sum",
    )(*pieces, *sums)


def next_sum(pieces, rows, cuts):
    each = (pieces[0].shape[0] - 1) // cuts

    def kernel(*refs):
        sums = add_sums(refs[:4], cuts * each, rows)
        for ahead, out in enumerate(refs[4:]):
            for i in range(each):
                out[i] = add_four(refs[:4], ahead * each + i).astype(BF)
            put_sums(out, each, sums)

    return pl.pallas_call(
        kernel,
        out_shape=[jax.ShapeDtypeStruct((each + 1, T, T), BF)] * cuts,
        in_specs=[pl.BlockSpec(memory_space=pltpu.VMEM)] * 4,
        compiler_params=params(16),
        cost_estimate=cost(1, 0),
        name="next_sum",
    )(*pieces)


def place(pieces, pos, rows):
    def kernel(pos_ref, *refs):
        out_ref, sums_ref = refs[4:]
        for back in range(4):
            source = lax.rem(pos_ref[3] + 4 - back, 4)
            for u in range(4):
                out_ref[4 * source + u] = refs[back][u].astype(F4)
        sums_ref[...] = add_sums(refs[:4], 4, rows)

    return pl.pallas_call(
        kernel,
        out_shape=(jax.ShapeDtypeStruct((16, T, T), F4), jax.ShapeDtypeStruct((rows, T), F4)),
        in_specs=[pl.BlockSpec(memory_space=pltpu.SMEM)] + [pl.BlockSpec(memory_space=pltpu.VMEM)] * 4,
        compiler_params=params(16),
        cost_estimate=cost(1, 0),
        name="place",
    )(pos, *pieces)


def shards(tokens, gain, tiles, rows, cols, cotangent):
    gain2 = gain.reshape(1, -1)
    pos = jnp.stack([lax.axis_index(a).astype(jnp.int32) for a in ("y", "z", "c", "x")])
    first, second = ("z", "y"), ("y", "z")
    one, two, three = (tuple(order[k] for order in ORDER) for k in range(3))

    def other_core(value):
        return lax.ppermute(value, "c", [(0, 1), (1, 0)])

    tokens_other, g_other = other_core(tokens), other_core(cotangent)
    normed, turned, scale = norm(tokens, gain2)
    _, turned_other, _ = norm(tokens_other, gain2)
    line = joined(exchange([tiles] * 4, first), turned, turned_other)
    left, right = ring(line, second, 1), ring(line, second, 3)
    operands = (rows, cols, pos, turned, turned_other, cotangent, g_other)
    parts = grads((0, 2, 1, 3), *operands)
    left_half, right_half = relayed(left, right, parts[0])
    left, right = held((left, right), left_half)
    part0, part2, part1, part3 = held(parts, left_half)
    near = [line, left, right]
    swapped = [other_core(block) for block in near]
    far = held((ring(left_half, second, 1), ring(right_half, second, 3)), *swapped)
    arrays = near + list(far) + swapped + [other_core(block) for block in far]
    projected, token_grad, sums = project(rows, cols, pos, arrays, tokens, normed, scale, gain2, cotangent)
    count = sums.shape[0]
    mid = cut_sum(exchange([part0, part1, part2, part3], one), (sums, other_core(sums)))
    ends = next_sum(exchange(mid, two), count, 4)
    (sent,) = next_sum(exchange(ends, three), count, 1)
    tile_grad, sums = place(exchange([sent] * 4, "x"), pos, count)
    sums = jnp.where(pos[2] == 0, sums, other_core(sums))
    return (projected, token_grad, tile_grad, sums.reshape(-1))


def solution(mesh):
    grid = Mesh(mesh.devices.reshape(4, 4, 2, 4), ALL)
    owners = ("y", "z", "c")
    placed = (P(ALL, None), P(), P(owners, None, None), P(), P(), P(ALL, None))
    return jax.shard_map(
        shards,
        mesh=grid,
        in_specs=placed,
        out_specs=(P(ALL, None), P(ALL, None), P(owners, None, None), P()),
        check_vma=False,
    )
```

```python
import jax
import jax.numpy as jnp
from jax import lax
from jax.experimental import pallas as pl
from jax.experimental.pallas import tpu as pltpu
from jax.sharding import Mesh, PartitionSpec as P

BF = jnp.bfloat16
F4 = jnp.float32
T = 128
ALL = ("y", "z", "c", "x")


def params(limit):
    return pltpu.CompilerParams(vmem_limit_bytes=limit * 1024 * 1024)


def cost(micros, nbytes):
    return pl.CostEstimate(flops=int(micros * 1.1e9), bytes_accessed=nbytes, transcendentals=0)


def whole(shape):
    zeros = (0,) * len(shape)
    return pl.BlockSpec(shape, lambda *_: zeros, pipeline_mode=pl.Buffered(1))


def dot(a, b):
    return jnp.dot(a, b, preferred_element_type=F4)


def dot_t(a, b):
    return lax.dot_general(a, b, (((1,), (1,)), ((), ())), preferred_element_type=F4)


ANY = pl.BlockSpec(memory_space=pl.ANY)


def cols_at(index):
    return pl.ds(pl.multiple_of(index * T, T), T)


def norm_kernel(x_ref, gain_ref, normed_ref, turned_ref, scale_ref):
    count, width = x_ref.shape
    blocks = width // T

    def squares(b, total):
        x = x_ref[:, cols_at(b)].astype(F4)
        return total + x * x

    total = lax.fori_loop(0, blocks, squares, jnp.zeros((count, T), F4), unroll=4)
    scale = lax.rsqrt(jnp.sum(total, axis=1, keepdims=True) / width + 1e-05)
    scale_ref[...] = jnp.broadcast_to(scale, (count, T))

    def fill(b, carry):
        x = x_ref[:, cols_at(b)].astype(F4)
        normed = (x * scale * gain_ref[:, cols_at(b)]).astype(BF)
        normed_ref[:, cols_at(b)] = normed
        turned_ref[b] = normed.T
        return carry

    lax.fori_loop(0, blocks, fill, 0, unroll=4)


def norm(x, gain):
    count, width = x.shape
    return pl.pallas_call(
        norm_kernel,
        out_shape=(
            jax.ShapeDtypeStruct((count, width), BF),
            jax.ShapeDtypeStruct((width // T, T, count), BF),
            jax.ShapeDtypeStruct((count, T), F4),
        ),
        compiler_params=params(16),
        cost_estimate=cost(1, 0),
        name="norm",
    )(x, gain)


def owned_at(pos, core, to_first, to_second):
    to_z = jnp.where(core == 0, to_first, to_second)
    to_y = jnp.where(core == 0, to_second, to_first)
    return (lax.rem(pos[0] + to_y, 4) * 4 + lax.rem(pos[1] + to_z, 4)) * 32 + core * 16


ORDER = (("x", "y", "z"), ("y", "z", "x"))


def listed(ahead, i, pos):
    y, z, c, x = pos[0], pos[1], pos[2], pos[3]
    one, two, three = ahead, i // 16, i // 4 % 4
    to_x = x + jnp.where(c == 0, one, three)
    to_y = y + jnp.where(c == 0, two, one)
    to_z = z + jnp.where(c == 0, three, two)
    return (lax.rem(to_y, 4) * 4 + lax.rem(to_z, 4)) * 32 + c * 16 + 4 * lax.rem(to_x, 4) + i % 4


STEP = 16


def grad_kernel(aheads, each, rows, cols, pos, turned_ref, turned_other_ref, own_ref, other_ref, *refs):
    at = pl.program_id(0)

    for k, (ahead, out_ref) in enumerate(zip(aheads, refs[-len(aheads) :])):

        @pl.when(at // each == k)
        def _(k=k, ahead=ahead, out_ref=out_ref):
            def one(t, carry):
                index = listed(ahead, (at - k * each) * STEP + t, pos)
                r, q = rows[index], cols[index]
                left = jnp.concatenate([turned_ref[r], turned_other_ref[r]], axis=1)
                right = jnp.concatenate([own_ref[:, cols_at(q)], other_ref[:, cols_at(q)]], axis=0)
                out_ref[t] = dot(left, right).astype(BF)
                return carry

            lax.fori_loop(0, STEP, one, 0, unroll=16)


def grads(aheads, rows, cols, pos, turned, turned_other, own, other, carried=(), ties=()):
    piece = 64
    each = piece // STEP

    def out_spec(k):
        return pl.BlockSpec((STEP, T, T), lambda i, *_: (jnp.clip(i - k * each, 0, each - 1), 0, 0))

    resident = (turned, turned_other, own, other)
    return pl.pallas_call(
        lambda *refs: grad_kernel(aheads, each, *refs),
        out_shape=[jax.ShapeDtypeStruct(a.shape, a.dtype) for a in carried]
        + [jax.ShapeDtypeStruct((piece, T, T), BF)] * len(aheads),
        grid_spec=pltpu.PrefetchScalarGridSpec(
            num_scalar_prefetch=3,
            grid=(len(aheads) * each,),
            in_specs=[whole(a.shape) for a in resident] + [ANY] * (len(carried) + len(ties)),
            out_specs=[ANY] * len(carried) + [out_spec(k) for k in range(len(aheads))],
        ),
        input_output_aliases={7 + k: k for k in range(len(carried))},
        compiler_params=params(60),
        cost_estimate=cost(2, 0),
        name="grads",
    )(rows, cols, pos, *resident, *carried, *ties)


def project_kernel(sources, rows, cols, pos, x_ref, normed_ref, scale_ref, gain_ref, g_ref, *refs):
    projected_ref, token_grad_ref, sums_ref, out_acc, back_acc, held_ref, sem = refs[-7:]
    s = pl.program_id(0)
    count, width = x_ref.shape
    blocks = width // T
    slot = lax.rem(s, 2)

    def fetch(k):
        array, offset = sources[k]
        pltpu.make_async_copy(refs[array].at[pl.ds(offset, 32)], held_ref.at[k % 2], sem.at[k % 2]).start()

    @pl.when(s == 0)
    def _():
        fetch(0)
        out_acc[...] = jnp.zeros_like(out_acc)
        back_acc[...] = jnp.zeros_like(back_acc)

    for k in range(1, len(sources)):

        @pl.when(s == k - 1)
        def _(k=k):
            fetch(k)

    pltpu.make_async_copy(refs[0].at[pl.ds(0, 32)], held_ref.at[slot], sem.at[slot]).wait()
    core = jnp.where(s < 8, pos[2], 1 - pos[2])
    pair = lax.rem(s, 8) // 2
    behind = jnp.where(pair < 2, pair, 5 - pair)

    def one(k, carry):
        i = lax.rem(s, 2) * 32 + k
        index = owned_at(pos, core, 4 - i // 16, 4 - behind) + i % 16
        r, q = cols_at(rows[index]), cols_at(cols[index])
        weight = held_ref[slot, k]
        out_acc[:, q] += dot(normed_ref[:, r], weight)
        back_acc[:, r] += dot_t(g_ref[:, q], weight)
        return carry

    lax.fori_loop(0, 32, one, 0, unroll=32)

    @pl.when(s == pl.num_programs(0) - 1)
    def _():
        scale = scale_ref[...]

        def products(b, total):
            at = cols_at(b)
            x = x_ref[:, at].astype(F4)
            back = back_acc[:, at]
            sums_ref[pl.ds(b, 1), :] = jnp.sum(back * x * scale, axis=0, keepdims=True)
            return total + x * gain_ref[:, at] * back

        total = lax.fori_loop(0, blocks, products, jnp.zeros((count, T), F4), unroll=2)
        inner = jnp.sum(total, axis=1, keepdims=True) / width
        cubed = scale * scale * scale * inner

        def finish(b, carry):
            at = cols_at(b)
            x = x_ref[:, at].astype(F4)
            token_grad_ref[:, at] = (scale * gain_ref[:, at] * back_acc[:, at] - x * cubed).astype(BF)
            return carry

        lax.fori_loop(0, blocks, finish, 0, unroll=2)

        def write(b, carry):
            projected_ref[:, cols_at(b)] = out_acc[:, cols_at(b)].astype(BF)
            return carry

        lax.fori_loop(0, g_ref.shape[1] // T, write, 0, unroll=4)


def project(rows, cols, pos, arrays, x, normed, scale, gain, g):
    sources = [(k, offset) for k, tiles in enumerate(arrays) for offset in range(0, tiles.shape[0], 32)]
    resident = (x, normed, scale, gain, g)
    sums = (x.shape[1] // T, T)
    return pl.pallas_call(
        lambda *refs: project_kernel(sources, *refs),
        out_shape=(
            jax.ShapeDtypeStruct(g.shape, BF),
            jax.ShapeDtypeStruct(x.shape, BF),
            jax.ShapeDtypeStruct(sums, F4),
        ),
        grid_spec=pltpu.PrefetchScalarGridSpec(
            num_scalar_prefetch=3,
            grid=(len(sources),),
            in_specs=[whole(a.shape) for a in resident] + [ANY] * len(arrays),
            out_specs=[whole(g.shape), whole(x.shape), whole(sums)],
            scratch_shapes=[
                pltpu.VMEM(g.shape, F4),
                pltpu.VMEM(x.shape, F4),
                pltpu.VMEM((2, 32, T, T), BF),
                pltpu.SemaphoreType.DMA((2,)),
            ],
        ),
        compiler_params=params(60),
        cost_estimate=cost(2, 0),
        name="project",
    )(rows, cols, pos, *resident, *arrays)


def joined(pieces, *ties):
    each = pieces[0].shape[0]

    def kernel(*refs):
        for j in range(4):
            refs[-1][j * each : (j + 1) * each] = refs[j][...]

    return pl.pallas_call(
        kernel,
        out_shape=jax.ShapeDtypeStruct((4 * each, T, T), BF),
        in_specs=[pl.BlockSpec(memory_space=pltpu.VMEM)] * 4 + [ANY] * len(ties),
        compiler_params=params(16),
        cost_estimate=cost(1, 0),
        name="joined",
    )(*pieces, *ties)


def held(values, *ties):
    return pl.pallas_call(
        lambda *refs: None,
        out_shape=[jax.ShapeDtypeStruct(a.shape, a.dtype) for a in values],
        in_specs=[ANY] * (len(values) + len(ties)),
        out_specs=[ANY] * len(values),
        input_output_aliases={k: k for k in range(len(values))},
        cost_estimate=cost(1, 0),
        name="held",
    )(*values, *ties)


def relayed(left, right, tie):
    half = left.shape[0] // 2

    def kernel(left_ref, right_ref, tie_ref, left_out, right_out):
        left_out[...] = left_ref[...]
        right_out[...] = right_ref[...]

    return pl.pallas_call(
        kernel,
        out_shape=[jax.ShapeDtypeStruct((half, T, T), BF)] * 2,
        grid=(2,),
        in_specs=[
            pl.BlockSpec((half // 2, T, T), lambda i: (i, 0, 0)),
            pl.BlockSpec((half // 2, T, T), lambda i: (2 + i, 0, 0)),
            ANY,
        ],
        out_specs=[pl.BlockSpec((half // 2, T, T), lambda i: (i, 0, 0))] * 2,
        compiler_params=params(60),
        cost_estimate=cost(1, 0),
        name="relayed",
    )(left, right, tie)


def ring(piece, axes, shift):
    if isinstance(axes, str):
        axes = (axes, axes)
    pairs = []
    for source in range(128):
        at = dict(y=source // 32, z=source // 8 % 4, c=source // 4 % 2, x=source % 4)
        axis = axes[at["c"]]
        to = dict(at, **{axis: (at[axis] + shift) % 4})
        pairs.append((source, to["y"] * 32 + to["z"] * 8 + to["c"] * 4 + to["x"]))
    return lax.ppermute(piece, ALL, pairs)


def exchange(pieces, axis):
    return [pieces[0]] + [ring(pieces[j], axis, j) for j in (1, 2, 3)]


def add_four(refs, i):
    a, b, c, d = (r[i].astype(F4) for r in refs)
    return (a + c) + (b + d)


def put_sums(ref, i, value):
    rows = value.shape[0]
    for part in range(3):
        rounded = value.astype(BF)
        ref[i, part * rows : (part + 1) * rows] = rounded
        value = value - rounded.astype(F4)
    ref[i, 3 * rows :] = jnp.zeros((T - 3 * rows, T), BF)


def get_sums(ref, i, rows):
    low, mid, high = (ref[i, part * rows : (part + 1) * rows].astype(F4) for part in (2, 1, 0))
    return (low + mid) + high


def add_sums(refs, i, rows):
    a, b, c, d = (get_sums(r, i, rows) for r in refs)
    return (a + c) + (b + d)


def cut_sum(pieces, sums):
    each = pieces[0].shape[0] // 4

    def kernel(*refs):
        total = add_four(refs[:4], ...).astype(BF)
        for ahead, out in enumerate(refs[-4:]):

            @pl.when(pl.program_id(0) == ahead)
            def _(out=out):
                out[:each] = total
                put_sums(out, each, refs[4][...] + refs[5][...])

    return pl.pallas_call(
        kernel,
        out_shape=[jax.ShapeDtypeStruct((each + 1, T, T), BF)] * 4,
        grid=(4,),
        in_specs=[pl.BlockSpec((each, T, T), lambda i: (i, 0, 0))] * 4 + [whole(a.shape) for a in sums],
        out_specs=[whole((each + 1, T, T))] * 4,
        compiler_params=params(32),
        cost_estimate=cost(1, 0),
        name="cut_sum",
    )(*pieces, *sums)


def next_sum(pieces, rows, cuts):
    each = (pieces[0].shape[0] - 1) // cuts

    def kernel(*refs):
        sums = add_sums(refs[:4], cuts * each, rows)
        for ahead, out in enumerate(refs[4:]):
            for i in range(each):
                out[i] = add_four(refs[:4], ahead * each + i).astype(BF)
            put_sums(out, each, sums)

    return pl.pallas_call(
        kernel,
        out_shape=[jax.ShapeDtypeStruct((each + 1, T, T), BF)] * cuts,
        in_specs=[pl.BlockSpec(memory_space=pltpu.VMEM)] * 4,
        compiler_params=params(16),
        cost_estimate=cost(1, 0),
        name="next_sum",
    )(*pieces)


def place(pieces, pos, rows):
    def kernel(pos_ref, *refs):
        out_ref, sums_ref = refs[4:]
        for back in range(4):
            source = lax.rem(pos_ref[3] + 4 - back, 4)
            for u in range(4):
                out_ref[4 * source + u] = refs[back][u].astype(F4)
        sums_ref[...] = add_sums(refs[:4], 4, rows)

    return pl.pallas_call(
        kernel,
        out_shape=(jax.ShapeDtypeStruct((16, T, T), F4), jax.ShapeDtypeStruct((rows, T), F4)),
        in_specs=[pl.BlockSpec(memory_space=pltpu.SMEM)] + [pl.BlockSpec(memory_space=pltpu.VMEM)] * 4,
        compiler_params=params(16),
        cost_estimate=cost(1, 0),
        name="place",
    )(pos, *pieces)


def shards(tokens, gain, tiles, rows, cols, cotangent):
    gain2 = gain.reshape(1, -1)
    pos = jnp.stack([lax.axis_index(a).astype(jnp.int32) for a in ("y", "z", "c", "x")])
    first, second = ("z", "y"), ("y", "z")
    one, two, three = (tuple(order[k] for order in ORDER) for k in range(3))

    def other_core(value):
        return lax.ppermute(value, "c", [(0, 1), (1, 0)])

    tokens_other, g_other = other_core(tokens), other_core(cotangent)
    normed, turned, scale = norm(tokens, gain2)
    _, turned_other, _ = norm(tokens_other, gain2)
    line = joined(exchange([tiles] * 4, first), turned, turned_other)
    left, right = ring(line, second, 1), ring(line, second, 3)
    operands = (rows, cols, pos, turned, turned_other, cotangent, g_other)
    part0, part2, part1 = grads((0, 2, 1), *operands)
    left_half, right_half = relayed(left, right, part0)
    left, right = held((left, right), left_half)
    part0, part2, part1, part3 = grads((3,), *operands, (part0, part2, part1), (left_half,))
    near = [line, left, right]
    swapped = [other_core(block) for block in near]
    far = held((ring(left_half, second, 1), ring(right_half, second, 3)), part3, *swapped)
    part0, part2, part1, part3 = held((part0, part2, part1, part3), far[0])
    arrays = near + list(far) + swapped + [other_core(block) for block in far]
    projected, token_grad, sums = project(rows, cols, pos, arrays, tokens, normed, scale, gain2, cotangent)
    count = sums.shape[0]
    mid = cut_sum(exchange([part0, part1, part2, part3], one), (sums, other_core(sums)))
    ends = next_sum(exchange(mid, two), count, 4)
    (sent,) = next_sum(exchange(ends, three), count, 1)
    tile_grad, sums = place(exchange([sent] * 4, "x"), pos, count)
    sums = jnp.where(pos[2] == 0, sums, other_core(sums))
    return (projected, token_grad, tile_grad, sums.reshape(-1))


def solution(mesh):
    grid = Mesh(mesh.devices.reshape(4, 4, 2, 4), ALL)
    owners = ("y", "z", "c")
    placed = (P(ALL, None), P(), P(owners, None, None), P(), P(), P(ALL, None))
    return jax.shard_map(
        shards,
        mesh=grid,
        in_specs=placed,
        out_specs=(P(ALL, None), P(ALL, None), P(owners, None, None), P()),
        check_vma=False,
    )
```

```python
import jax
import jax.numpy as jnp
from jax import lax
from jax.experimental import pallas as pl
from jax.experimental.pallas import tpu as pltpu
from jax.sharding import Mesh, PartitionSpec as P

BF = jnp.bfloat16
F4 = jnp.float32
T = 128
ALL = ("y", "z", "c", "x")


def params(limit):
    return pltpu.CompilerParams(vmem_limit_bytes=limit * 1024 * 1024)


def cost(micros, nbytes):
    return pl.CostEstimate(flops=int(micros * 1.1e9), bytes_accessed=nbytes, transcendentals=0)


def whole(shape):
    zeros = (0,) * len(shape)
    return pl.BlockSpec(shape, lambda *_: zeros, pipeline_mode=pl.Buffered(1))


def dot(a, b):
    return jnp.dot(a, b, preferred_element_type=F4)


def dot_t(a, b):
    return lax.dot_general(a, b, (((1,), (1,)), ((), ())), preferred_element_type=F4)


ANY = pl.BlockSpec(memory_space=pl.ANY)


def cols_at(index):
    return pl.ds(pl.multiple_of(index * T, T), T)


def norm_kernel(x_ref, gain_ref, normed_ref, turned_ref, scale_ref):
    count, width = x_ref.shape
    blocks = width // T

    def squares(b, total):
        x = x_ref[:, cols_at(b)].astype(F4)
        return total + x * x

    total = lax.fori_loop(0, blocks, squares, jnp.zeros((count, T), F4), unroll=4)
    scale = lax.rsqrt(jnp.sum(total, axis=1, keepdims=True) / width + 1e-05)
    scale_ref[...] = jnp.broadcast_to(scale, (count, T))

    def fill(b, carry):
        x = x_ref[:, cols_at(b)].astype(F4)
        normed = (x * scale * gain_ref[:, cols_at(b)]).astype(BF)
        normed_ref[:, cols_at(b)] = normed
        turned_ref[b] = normed.T
        return carry

    lax.fori_loop(0, blocks, fill, 0, unroll=4)


def norm(x, gain):
    count, width = x.shape
    return pl.pallas_call(
        norm_kernel,
        out_shape=(
            jax.ShapeDtypeStruct((count, width), BF),
            jax.ShapeDtypeStruct((width // T, T, count), BF),
            jax.ShapeDtypeStruct((count, T), F4),
        ),
        compiler_params=params(16),
        cost_estimate=cost(1, 0),
        name="norm",
    )(x, gain)


def owned_at(pos, core, to_first, to_second):
    to_z = jnp.where(core == 0, to_first, to_second)
    to_y = jnp.where(core == 0, to_second, to_first)
    return (lax.rem(pos[0] + to_y, 4) * 4 + lax.rem(pos[1] + to_z, 4)) * 32 + core * 16


ORDER = (("x", "y", "z"), ("y", "z", "x"))


def listed(ahead, i, pos):
    y, z, c, x = pos[0], pos[1], pos[2], pos[3]
    one, two, three = ahead, i // 16, i // 4 % 4
    to_x = x + jnp.where(c == 0, one, three)
    to_y = y + jnp.where(c == 0, two, one)
    to_z = z + jnp.where(c == 0, three, two)
    return (lax.rem(to_y, 4) * 4 + lax.rem(to_z, 4)) * 32 + c * 16 + 4 * lax.rem(to_x, 4) + i % 4


STEP = 16


def grad_kernel(aheads, each, rows, cols, pos, turned_ref, turned_other_ref, own_ref, other_ref, *refs):
    at = pl.program_id(0)

    for k, (ahead, out_ref) in enumerate(zip(aheads, refs[-len(aheads) :])):

        @pl.when(at // each == k)
        def _(k=k, ahead=ahead, out_ref=out_ref):
            def one(t, carry):
                index = listed(ahead, (at - k * each) * STEP + t, pos)
                r, q = rows[index], cols[index]
                left = jnp.concatenate([turned_ref[r], turned_other_ref[r]], axis=1)
                right = jnp.concatenate([own_ref[:, cols_at(q)], other_ref[:, cols_at(q)]], axis=0)
                out_ref[t] = dot(left, right).astype(BF)
                return carry

            lax.fori_loop(0, STEP, one, 0, unroll=16)


def grads(aheads, rows, cols, pos, turned, turned_other, own, other, carried=(), ties=()):
    piece = 64
    each = piece // STEP

    def out_spec(k):
        return pl.BlockSpec((STEP, T, T), lambda i, *_: (jnp.clip(i - k * each, 0, each - 1), 0, 0))

    resident = (turned, turned_other, own, other)
    return pl.pallas_call(
        lambda *refs: grad_kernel(aheads, each, *refs),
        out_shape=[jax.ShapeDtypeStruct(a.shape, a.dtype) for a in carried]
        + [jax.ShapeDtypeStruct((piece, T, T), BF)] * len(aheads),
        grid_spec=pltpu.PrefetchScalarGridSpec(
            num_scalar_prefetch=3,
            grid=(len(aheads) * each,),
            in_specs=[whole(a.shape) for a in resident] + [ANY] * (len(carried) + len(ties)),
            out_specs=[ANY] * len(carried) + [out_spec(k) for k in range(len(aheads))],
        ),
        input_output_aliases={7 + k: k for k in range(len(carried))},
        compiler_params=params(60),
        cost_estimate=cost(2, 0),
        name="grads",
    )(rows, cols, pos, *resident, *carried, *ties)


def project_kernel(sources, rows, cols, pos, x_ref, normed_ref, scale_ref, gain_ref, g_ref, *refs):
    projected_ref, token_grad_ref, sums_ref, out_acc, back_acc, held_ref, sem = refs[-7:]
    s = pl.program_id(0)
    count, width = x_ref.shape
    blocks = width // T
    slot = lax.rem(s, 2)

    def fetch(k):
        array, offset = sources[k]
        pltpu.make_async_copy(refs[array].at[pl.ds(offset, 32)], held_ref.at[k % 2], sem.at[k % 2]).start()

    @pl.when(s == 0)
    def _():
        fetch(0)
        out_acc[...] = jnp.zeros_like(out_acc)
        back_acc[...] = jnp.zeros_like(back_acc)

    for k in range(1, len(sources)):

        @pl.when(s == k - 1)
        def _(k=k):
            fetch(k)

    pltpu.make_async_copy(refs[0].at[pl.ds(0, 32)], held_ref.at[slot], sem.at[slot]).wait()
    core = jnp.where(s < 8, pos[2], 1 - pos[2])
    pair = lax.rem(s, 8) // 2
    behind = jnp.where(pair < 2, pair, 5 - pair)

    def one(k, carry):
        i = lax.rem(s, 2) * 32 + k
        index = owned_at(pos, core, 4 - i // 16, 4 - behind) + i % 16
        r, q = cols_at(rows[index]), cols_at(cols[index])
        weight = held_ref[slot, k]
        out_acc[:, q] += dot(normed_ref[:, r], weight)
        back_acc[:, r] += dot_t(g_ref[:, q], weight)
        return carry

    lax.fori_loop(0, 32, one, 0, unroll=32)

    @pl.when(s == pl.num_programs(0) - 1)
    def _():
        scale = scale_ref[...]

        def products(b, total):
            at = cols_at(b)
            x = x_ref[:, at].astype(F4)
            back = back_acc[:, at]
            sums_ref[pl.ds(b, 1), :] = jnp.sum(back * x * scale, axis=0, keepdims=True)
            return total + x * gain_ref[:, at] * back

        total = lax.fori_loop(0, blocks, products, jnp.zeros((count, T), F4), unroll=2)
        inner = jnp.sum(total, axis=1, keepdims=True) / width
        cubed = scale * scale * scale * inner

        def finish(b, carry):
            at = cols_at(b)
            x = x_ref[:, at].astype(F4)
            token_grad_ref[:, at] = (scale * gain_ref[:, at] * back_acc[:, at] - x * cubed).astype(BF)
            return carry

        lax.fori_loop(0, blocks, finish, 0, unroll=2)

        def write(b, carry):
            projected_ref[:, cols_at(b)] = out_acc[:, cols_at(b)].astype(BF)
            return carry

        lax.fori_loop(0, g_ref.shape[1] // T, write, 0, unroll=4)


def project(rows, cols, pos, arrays, x, normed, scale, gain, g):
    sources = [(k, offset) for k, tiles in enumerate(arrays) for offset in range(0, tiles.shape[0], 32)]
    resident = (x, normed, scale, gain, g)
    sums = (x.shape[1] // T, T)
    return pl.pallas_call(
        lambda *refs: project_kernel(sources, *refs),
        out_shape=(
            jax.ShapeDtypeStruct(g.shape, BF),
            jax.ShapeDtypeStruct(x.shape, BF),
            jax.ShapeDtypeStruct(sums, F4),
        ),
        grid_spec=pltpu.PrefetchScalarGridSpec(
            num_scalar_prefetch=3,
            grid=(len(sources),),
            in_specs=[whole(a.shape) for a in resident] + [ANY] * len(arrays),
            out_specs=[whole(g.shape), whole(x.shape), whole(sums)],
            scratch_shapes=[
                pltpu.VMEM(g.shape, F4),
                pltpu.VMEM(x.shape, F4),
                pltpu.VMEM((2, 32, T, T), BF),
                pltpu.SemaphoreType.DMA((2,)),
            ],
        ),
        compiler_params=params(60),
        cost_estimate=cost(2, 0),
        name="project",
    )(rows, cols, pos, *resident, *arrays)


def joined(pieces, *ties):
    each = pieces[0].shape[0]

    def kernel(*refs):
        for j in range(4):
            refs[-1][j * each : (j + 1) * each] = refs[j][...]

    return pl.pallas_call(
        kernel,
        out_shape=jax.ShapeDtypeStruct((4 * each, T, T), BF),
        in_specs=[pl.BlockSpec(memory_space=pltpu.VMEM)] * 4 + [ANY] * len(ties),
        compiler_params=params(16),
        cost_estimate=cost(1, 0),
        name="joined",
    )(*pieces, *ties)


def held(values, *ties):
    return pl.pallas_call(
        lambda *refs: None,
        out_shape=[jax.ShapeDtypeStruct(a.shape, a.dtype) for a in values],
        in_specs=[ANY] * (len(values) + len(ties)),
        out_specs=[ANY] * len(values),
        input_output_aliases={k: k for k in range(len(values))},
        cost_estimate=cost(1, 0),
        name="held",
    )(*values, *ties)


def relayed(left, right, *ties):
    half = left.shape[0] // 2

    def kernel(left_ref, right_ref, *refs):
        left_out, right_out = refs[-2:]
        left_out[...] = left_ref[...]
        right_out[...] = right_ref[...]

    return pl.pallas_call(
        kernel,
        out_shape=[jax.ShapeDtypeStruct((half, T, T), BF)] * 2,
        grid=(2,),
        in_specs=[
            pl.BlockSpec((half // 2, T, T), lambda i: (i, 0, 0)),
            pl.BlockSpec((half // 2, T, T), lambda i: (2 + i, 0, 0)),
        ]
        + [ANY] * len(ties),
        out_specs=[pl.BlockSpec((half // 2, T, T), lambda i: (i, 0, 0))] * 2,
        compiler_params=params(60),
        cost_estimate=cost(1, 0),
        name="relayed",
    )(left, right, *ties)


def ring(piece, axes, shift):
    if isinstance(axes, str):
        axes = (axes, axes)
    pairs = []
    for source in range(128):
        at = dict(y=source // 32, z=source // 8 % 4, c=source // 4 % 2, x=source % 4)
        axis = axes[at["c"]]
        to = dict(at, **{axis: (at[axis] + shift) % 4})
        pairs.append((source, to["y"] * 32 + to["z"] * 8 + to["c"] * 4 + to["x"]))
    return lax.ppermute(piece, ALL, pairs)


def exchange(pieces, axis):
    return [pieces[0]] + [ring(pieces[j], axis, j) for j in (1, 2, 3)]


def add_four(refs, i):
    a, b, c, d = (r[i].astype(F4) for r in refs)
    return (a + c) + (b + d)


def put_sums(ref, i, value):
    rows = value.shape[0]
    for part in range(3):
        rounded = value.astype(BF)
        ref[i, part * rows : (part + 1) * rows] = rounded
        value = value - rounded.astype(F4)
    ref[i, 3 * rows :] = jnp.zeros((T - 3 * rows, T), BF)


def get_sums(ref, i, rows):
    low, mid, high = (ref[i, part * rows : (part + 1) * rows].astype(F4) for part in (2, 1, 0))
    return (low + mid) + high


def add_sums(refs, i, rows):
    a, b, c, d = (get_sums(r, i, rows) for r in refs)
    return (a + c) + (b + d)


def cut_sum(pieces, sums):
    each = pieces[0].shape[0] // 4

    def kernel(*refs):
        total = add_four(refs[:4], ...).astype(BF)
        for ahead, out in enumerate(refs[-4:]):

            @pl.when(pl.program_id(0) == ahead)
            def _(out=out):
                out[:each] = total
                put_sums(out, each, refs[4][...] + refs[5][...])

    return pl.pallas_call(
        kernel,
        out_shape=[jax.ShapeDtypeStruct((each + 1, T, T), BF)] * 4,
        grid=(4,),
        in_specs=[pl.BlockSpec((each, T, T), lambda i: (i, 0, 0))] * 4 + [whole(a.shape) for a in sums],
        out_specs=[whole((each + 1, T, T))] * 4,
        compiler_params=params(32),
        cost_estimate=cost(1, 0),
        name="cut_sum",
    )(*pieces, *sums)


def next_sum(pieces, rows, cuts):
    each = (pieces[0].shape[0] - 1) // cuts

    def kernel(*refs):
        sums = add_sums(refs[:4], cuts * each, rows)
        for ahead, out in enumerate(refs[4:]):
            for i in range(each):
                out[i] = add_four(refs[:4], ahead * each + i).astype(BF)
            put_sums(out, each, sums)

    return pl.pallas_call(
        kernel,
        out_shape=[jax.ShapeDtypeStruct((each + 1, T, T), BF)] * cuts,
        in_specs=[pl.BlockSpec(memory_space=pltpu.VMEM)] * 4,
        compiler_params=params(16),
        cost_estimate=cost(1, 0),
        name="next_sum",
    )(*pieces)


def place(pieces, pos, rows):
    def kernel(pos_ref, *refs):
        out_ref, sums_ref = refs[4:]
        for back in range(4):
            source = lax.rem(pos_ref[3] + 4 - back, 4)
            for u in range(4):
                out_ref[4 * source + u] = refs[back][u].astype(F4)
        sums_ref[...] = add_sums(refs[:4], 4, rows)

    return pl.pallas_call(
        kernel,
        out_shape=(jax.ShapeDtypeStruct((16, T, T), F4), jax.ShapeDtypeStruct((rows, T), F4)),
        in_specs=[pl.BlockSpec(memory_space=pltpu.SMEM)] + [pl.BlockSpec(memory_space=pltpu.VMEM)] * 4,
        compiler_params=params(16),
        cost_estimate=cost(1, 0),
        name="place",
    )(pos, *pieces)


def shards(tokens, gain, tiles, rows, cols, cotangent):
    gain2 = gain.reshape(1, -1)
    pos = jnp.stack([lax.axis_index(a).astype(jnp.int32) for a in ("y", "z", "c", "x")])
    first, second = ("z", "y"), ("y", "z")
    one, two, three = (tuple(order[k] for order in ORDER) for k in range(3))

    def other_core(value):
        return lax.ppermute(value, "c", [(0, 1), (1, 0)])

    tokens_other, g_other = other_core(tokens), other_core(cotangent)
    normed, turned, scale = norm(tokens, gain2)
    _, turned_other, _ = norm(tokens_other, gain2)
    line = joined(exchange([tiles] * 4, first), turned, turned_other)
    left, right = ring(line, second, 1), ring(line, second, 3)
    operands = (rows, cols, pos, turned, turned_other, cotangent, g_other)
    part0, part2, part1 = grads((0, 2, 1), *operands)
    line_swapped = other_core(line)
    left_half, right_half = relayed(left, right, part0, line_swapped)
    left, right = held((left, right), left_half)
    part2, part1 = held((part2, part1), left_half)
    (part3,) = grads((3,), *operands, (), (left_half,))
    near = [line, left, right]
    swapped = [line_swapped, other_core(left), other_core(right)]
    far = held((ring(left_half, second, 1), ring(right_half, second, 3)), part3, *swapped)
    arrays = near + list(far) + swapped + [other_core(block) for block in far]
    projected, token_grad, sums = project(rows, cols, pos, arrays, tokens, normed, scale, gain2, cotangent)
    count = sums.shape[0]
    mid = cut_sum(exchange([part0, part1, part2, part3], one), (sums, other_core(sums)))
    ends = next_sum(exchange(mid, two), count, 4)
    (sent,) = next_sum(exchange(ends, three), count, 1)
    tile_grad, sums = place(exchange([sent] * 4, "x"), pos, count)
    sums = jnp.where(pos[2] == 0, sums, other_core(sums))
    return (projected, token_grad, tile_grad, sums.reshape(-1))


def solution(mesh):
    grid = Mesh(mesh.devices.reshape(4, 4, 2, 4), ALL)
    owners = ("y", "z", "c")
    placed = (P(ALL, None), P(), P(owners, None, None), P(), P(), P(ALL, None))
    return jax.shard_map(
        shards,
        mesh=grid,
        in_specs=placed,
        out_specs=(P(ALL, None), P(ALL, None), P(owners, None, None), P()),
        check_vma=False,
    )
```

```python
import jax
import jax.numpy as jnp
from jax import lax
from jax.experimental import pallas as pl
from jax.experimental.pallas import tpu as pltpu
from jax.sharding import Mesh, PartitionSpec as P

BF = jnp.bfloat16
F4 = jnp.float32
T = 128
ALL = ("y", "z", "c", "x")


def params(limit):
    return pltpu.CompilerParams(vmem_limit_bytes=limit * 1024 * 1024)


def cost(micros, nbytes):
    return pl.CostEstimate(flops=int(micros * 1.1e9), bytes_accessed=nbytes, transcendentals=0)


def whole(shape):
    zeros = (0,) * len(shape)
    return pl.BlockSpec(shape, lambda *_: zeros, pipeline_mode=pl.Buffered(1))


def dot(a, b):
    return jnp.dot(a, b, preferred_element_type=F4)


def dot_t(a, b):
    return lax.dot_general(a, b, (((1,), (1,)), ((), ())), preferred_element_type=F4)


ANY = pl.BlockSpec(memory_space=pl.ANY)


def cols_at(index):
    return pl.ds(pl.multiple_of(index * T, T), T)


def norm_kernel(x_ref, gain_ref, normed_ref, turned_ref, scale_ref):
    count, width = x_ref.shape
    blocks = width // T

    def squares(b, total):
        x = x_ref[:, cols_at(b)].astype(F4)
        return total + x * x

    total = lax.fori_loop(0, blocks, squares, jnp.zeros((count, T), F4), unroll=4)
    scale = lax.rsqrt(jnp.sum(total, axis=1, keepdims=True) / width + 1e-05)
    scale_ref[...] = jnp.broadcast_to(scale, (count, T))

    def fill(b, carry):
        x = x_ref[:, cols_at(b)].astype(F4)
        normed = (x * scale * gain_ref[:, cols_at(b)]).astype(BF)
        normed_ref[:, cols_at(b)] = normed
        turned_ref[b] = normed.T
        return carry

    lax.fori_loop(0, blocks, fill, 0, unroll=4)


def norm(x, gain):
    count, width = x.shape
    return pl.pallas_call(
        norm_kernel,
        out_shape=(
            jax.ShapeDtypeStruct((count, width), BF),
            jax.ShapeDtypeStruct((width // T, T, count), BF),
            jax.ShapeDtypeStruct((count, T), F4),
        ),
        compiler_params=params(16),
        cost_estimate=cost(1, 0),
        name="norm",
    )(x, gain)


def owned_at(pos, core, to_first, to_second):
    to_z = jnp.where(core == 0, to_first, to_second)
    to_y = jnp.where(core == 0, to_second, to_first)
    return (lax.rem(pos[0] + to_y, 4) * 4 + lax.rem(pos[1] + to_z, 4)) * 32 + core * 16


ORDER = (("x", "y", "z"), ("y", "z", "x"))


def listed(ahead, i, pos):
    y, z, c, x = pos[0], pos[1], pos[2], pos[3]
    one, two, three = ahead, i // 16, i // 4 % 4
    to_x = x + jnp.where(c == 0, one, three)
    to_y = y + jnp.where(c == 0, two, one)
    to_z = z + jnp.where(c == 0, three, two)
    return (lax.rem(to_y, 4) * 4 + lax.rem(to_z, 4)) * 32 + c * 16 + 4 * lax.rem(to_x, 4) + i % 4


STEP = 16


def grad_kernel(aheads, each, rows, cols, pos, turned_ref, turned_other_ref, own_ref, other_ref, *refs):
    at = pl.program_id(0)

    for k, (ahead, out_ref) in enumerate(zip(aheads, refs[-len(aheads) :])):

        @pl.when(at // each == k)
        def _(k=k, ahead=ahead, out_ref=out_ref):
            def one(t, carry):
                index = listed(ahead, (at - k * each) * STEP + t, pos)
                r, q = rows[index], cols[index]
                left = jnp.concatenate([turned_ref[r], turned_other_ref[r]], axis=1)
                right = jnp.concatenate([own_ref[:, cols_at(q)], other_ref[:, cols_at(q)]], axis=0)
                out_ref[t] = dot(left, right).astype(BF)
                return carry

            lax.fori_loop(0, STEP, one, 0, unroll=16)


def grads(aheads, rows, cols, pos, turned, turned_other, own, other, carried=(), ties=()):
    piece = 64
    each = piece // STEP

    def out_spec(k):
        return pl.BlockSpec((STEP, T, T), lambda i, *_: (jnp.clip(i - k * each, 0, each - 1), 0, 0))

    resident = (turned, turned_other, own, other)
    return pl.pallas_call(
        lambda *refs: grad_kernel(aheads, each, *refs),
        out_shape=[jax.ShapeDtypeStruct(a.shape, a.dtype) for a in carried]
        + [jax.ShapeDtypeStruct((piece, T, T), BF)] * len(aheads),
        grid_spec=pltpu.PrefetchScalarGridSpec(
            num_scalar_prefetch=3,
            grid=(len(aheads) * each,),
            in_specs=[whole(a.shape) for a in resident] + [ANY] * (len(carried) + len(ties)),
            out_specs=[ANY] * len(carried) + [out_spec(k) for k in range(len(aheads))],
        ),
        input_output_aliases={7 + k: k for k in range(len(carried))},
        compiler_params=params(60),
        cost_estimate=cost(2, 0),
        name="grads",
    )(rows, cols, pos, *resident, *carried, *ties)


def project_kernel(sources, rows, cols, pos, x_ref, normed_ref, scale_ref, gain_ref, g_ref, *refs):
    projected_ref, token_grad_ref, sums_ref, out_acc, back_acc, held_ref, sem = refs[-7:]
    s = pl.program_id(0)
    count, width = x_ref.shape
    blocks = width // T
    slot = lax.rem(s, 2)

    def fetch(k):
        array, offset = sources[k]
        pltpu.make_async_copy(refs[array].at[pl.ds(offset, 32)], held_ref.at[k % 2], sem.at[k % 2]).start()

    @pl.when(s == 0)
    def _():
        fetch(0)
        out_acc[...] = jnp.zeros_like(out_acc)
        back_acc[...] = jnp.zeros_like(back_acc)

    for k in range(1, len(sources)):

        @pl.when(s == k - 1)
        def _(k=k):
            fetch(k)

    pltpu.make_async_copy(refs[0].at[pl.ds(0, 32)], held_ref.at[slot], sem.at[slot]).wait()
    core = jnp.where(s < 8, pos[2], 1 - pos[2])
    pair = lax.rem(s, 8) // 2
    behind = jnp.where(pair < 2, pair, 5 - pair)

    def one(k, carry):
        i = lax.rem(s, 2) * 32 + k
        index = owned_at(pos, core, 4 - i // 16, 4 - behind) + i % 16
        r, q = cols_at(rows[index]), cols_at(cols[index])
        weight = held_ref[slot, k]
        out_acc[:, q] += dot(normed_ref[:, r], weight)
        back_acc[:, r] += dot_t(g_ref[:, q], weight)
        return carry

    lax.fori_loop(0, 32, one, 0, unroll=32)

    @pl.when(s == pl.num_programs(0) - 1)
    def _():
        scale = scale_ref[...]

        def products(b, total):
            at = cols_at(b)
            x = x_ref[:, at].astype(F4)
            back = back_acc[:, at]
            sums_ref[pl.ds(b, 1), :] = jnp.sum(back * x * scale, axis=0, keepdims=True)
            return total + x * gain_ref[:, at] * back

        total = lax.fori_loop(0, blocks, products, jnp.zeros((count, T), F4), unroll=2)
        inner = jnp.sum(total, axis=1, keepdims=True) / width
        cubed = scale * scale * scale * inner

        def finish(b, carry):
            at = cols_at(b)
            x = x_ref[:, at].astype(F4)
            token_grad_ref[:, at] = (scale * gain_ref[:, at] * back_acc[:, at] - x * cubed).astype(BF)
            return carry

        lax.fori_loop(0, blocks, finish, 0, unroll=2)

        def write(b, carry):
            projected_ref[:, cols_at(b)] = out_acc[:, cols_at(b)].astype(BF)
            return carry

        lax.fori_loop(0, g_ref.shape[1] // T, write, 0, unroll=4)


def project(rows, cols, pos, arrays, x, normed, scale, gain, g):
    sources = [(k, offset) for k, tiles in enumerate(arrays) for offset in range(0, tiles.shape[0], 32)]
    resident = (x, normed, scale, gain, g)
    sums = (x.shape[1] // T, T)
    return pl.pallas_call(
        lambda *refs: project_kernel(sources, *refs),
        out_shape=(
            jax.ShapeDtypeStruct(g.shape, BF),
            jax.ShapeDtypeStruct(x.shape, BF),
            jax.ShapeDtypeStruct(sums, F4),
        ),
        grid_spec=pltpu.PrefetchScalarGridSpec(
            num_scalar_prefetch=3,
            grid=(len(sources),),
            in_specs=[whole(a.shape) for a in resident] + [ANY] * len(arrays),
            out_specs=[whole(g.shape), whole(x.shape), whole(sums)],
            scratch_shapes=[
                pltpu.VMEM(g.shape, F4),
                pltpu.VMEM(x.shape, F4),
                pltpu.VMEM((2, 32, T, T), BF),
                pltpu.SemaphoreType.DMA((2,)),
            ],
        ),
        compiler_params=params(60),
        cost_estimate=cost(2, 0),
        name="project",
    )(rows, cols, pos, *resident, *arrays)


def joined(pieces, *ties):
    each = pieces[0].shape[0]

    def kernel(*refs):
        for j in range(4):
            refs[-1][j * each : (j + 1) * each] = refs[j][...]

    return pl.pallas_call(
        kernel,
        out_shape=jax.ShapeDtypeStruct((4 * each, T, T), BF),
        in_specs=[pl.BlockSpec(memory_space=pltpu.VMEM)] * 4 + [ANY] * len(ties),
        compiler_params=params(16),
        cost_estimate=cost(1, 0),
        name="joined",
    )(*pieces, *ties)


def held(values, *ties):
    return pl.pallas_call(
        lambda *refs: None,
        out_shape=[jax.ShapeDtypeStruct(a.shape, a.dtype) for a in values],
        in_specs=[ANY] * (len(values) + len(ties)),
        out_specs=[ANY] * len(values),
        input_output_aliases={k: k for k in range(len(values))},
        cost_estimate=cost(1, 0),
        name="held",
    )(*values, *ties)


def relayed(left, right, tie):
    half = left.shape[0] // 2

    def kernel(left_ref, right_ref, tie_ref, left_out, right_out):
        left_out[...] = left_ref[...]
        right_out[...] = right_ref[...]

    return pl.pallas_call(
        kernel,
        out_shape=[jax.ShapeDtypeStruct((half, T, T), BF)] * 2,
        grid=(2,),
        in_specs=[
            pl.BlockSpec((half // 2, T, T), lambda i: (i, 0, 0)),
            pl.BlockSpec((half // 2, T, T), lambda i: (2 + i, 0, 0)),
            ANY,
        ],
        out_specs=[pl.BlockSpec((half // 2, T, T), lambda i: (i, 0, 0))] * 2,
        compiler_params=params(60),
        cost_estimate=cost(1, 0),
        name="relayed",
    )(left, right, tie)


def ring(piece, axes, shift):
    if isinstance(axes, str):
        axes = (axes, axes)
    pairs = []
    for source in range(128):
        at = dict(y=source // 32, z=source // 8 % 4, c=source // 4 % 2, x=source % 4)
        axis = axes[at["c"]]
        to = dict(at, **{axis: (at[axis] + shift) % 4})
        pairs.append((source, to["y"] * 32 + to["z"] * 8 + to["c"] * 4 + to["x"]))
    return lax.ppermute(piece, ALL, pairs)


def exchange(pieces, axis):
    return [pieces[0]] + [ring(pieces[j], axis, j) for j in (1, 2, 3)]


def add_four(refs, i):
    a, b, c, d = (r[i].astype(F4) for r in refs)
    return (a + c) + (b + d)


def put_sums(ref, i, value):
    rows = value.shape[0]
    for part in range(3):
        rounded = value.astype(BF)
        ref[i, part * rows : (part + 1) * rows] = rounded
        value = value - rounded.astype(F4)
    ref[i, 3 * rows :] = jnp.zeros((T - 3 * rows, T), BF)


def get_sums(ref, i, rows):
    low, mid, high = (ref[i, part * rows : (part + 1) * rows].astype(F4) for part in (2, 1, 0))
    return (low + mid) + high


def add_sums(refs, i, rows):
    a, b, c, d = (get_sums(r, i, rows) for r in refs)
    return (a + c) + (b + d)


def cut_sum(pieces, sums):
    each = pieces[0].shape[0] // 4

    def kernel(*refs):
        total = add_four(refs[:4], ...).astype(BF)
        for ahead, out in enumerate(refs[-4:]):

            @pl.when(pl.program_id(0) == ahead)
            def _(out=out):
                out[:each] = total
                put_sums(out, each, refs[4][...] + refs[5][...])

    return pl.pallas_call(
        kernel,
        out_shape=[jax.ShapeDtypeStruct((each + 1, T, T), BF)] * 4,
        grid=(4,),
        in_specs=[pl.BlockSpec((each, T, T), lambda i: (i, 0, 0))] * 4 + [whole(a.shape) for a in sums],
        out_specs=[whole((each + 1, T, T))] * 4,
        compiler_params=params(32),
        cost_estimate=cost(1, 0),
        name="cut_sum",
    )(*pieces, *sums)


def next_sum(pieces, rows, cuts):
    each = (pieces[0].shape[0] - 1) // cuts

    def kernel(*refs):
        sums = add_sums(refs[:4], cuts * each, rows)
        for ahead, out in enumerate(refs[4:]):
            for i in range(each):
                out[i] = add_four(refs[:4], ahead * each + i).astype(BF)
            put_sums(out, each, sums)

    return pl.pallas_call(
        kernel,
        out_shape=[jax.ShapeDtypeStruct((each + 1, T, T), BF)] * cuts,
        in_specs=[pl.BlockSpec(memory_space=pltpu.VMEM)] * 4,
        compiler_params=params(16),
        cost_estimate=cost(1, 0),
        name="next_sum",
    )(*pieces)


def place(pieces, pos, rows):
    def kernel(pos_ref, *refs):
        out_ref, sums_ref = refs[4:]
        for back in range(4):
            source = lax.rem(pos_ref[3] + 4 - back, 4)
            for u in range(4):
                out_ref[4 * source + u] = refs[back][u].astype(F4)
        sums_ref[...] = add_sums(refs[:4], 4, rows)

    return pl.pallas_call(
        kernel,
        out_shape=(jax.ShapeDtypeStruct((16, T, T), F4), jax.ShapeDtypeStruct((rows, T), F4)),
        in_specs=[pl.BlockSpec(memory_space=pltpu.SMEM)] + [pl.BlockSpec(memory_space=pltpu.VMEM)] * 4,
        compiler_params=params(16),
        cost_estimate=cost(1, 0),
        name="place",
    )(pos, *pieces)


def shards(tokens, gain, tiles, rows, cols, cotangent):
    gain2 = gain.reshape(1, -1)
    pos = jnp.stack([lax.axis_index(a).astype(jnp.int32) for a in ("y", "z", "c", "x")])
    first, second = ("z", "y"), ("y", "z")
    one, two, three = (tuple(order[k] for order in ORDER) for k in range(3))

    def other_core(value):
        return lax.ppermute(value, "c", [(0, 1), (1, 0)])

    tokens_other, g_other = other_core(tokens), other_core(cotangent)
    normed, turned, scale = norm(tokens, gain2)
    _, turned_other, _ = norm(tokens_other, gain2)
    line = joined(exchange([tiles] * 4, first), turned, turned_other)
    left, right = ring(line, second, 1), ring(line, second, 3)
    operands = (rows, cols, pos, turned, turned_other, cotangent, g_other)
    part0, part2, part1 = grads((0, 2, 1), *operands)
    left_half, right_half = relayed(left, right, part0)
    left, right = held((left, right), left_half)
    part0, part2, part1, part3 = grads((3,), *operands, (part0, part2, part1), (left_half,))
    near = [line, left, right]
    swapped = [other_core(block) for block in near]
    far = held((ring(left_half, second, 1), ring(right_half, second, 3)), part3, *swapped)
    arrays = near + list(far) + swapped + [other_core(block) for block in far]
    projected, token_grad, sums = project(rows, cols, pos, arrays, tokens, normed, scale, gain2, cotangent)
    count = sums.shape[0]
    mid = cut_sum(exchange([part0, part1, part2, part3], one), (sums, other_core(sums)))
    ends = next_sum(exchange(mid, two), count, 4)
    (sent,) = next_sum(exchange(ends, three), count, 1)
    tile_grad, sums = place(exchange([sent] * 4, "x"), pos, count)
    sums = jnp.where(pos[2] == 0, sums, other_core(sums))
    return (projected, token_grad, tile_grad, sums.reshape(-1))


def solution(mesh):
    grid = Mesh(mesh.devices.reshape(4, 4, 2, 4), ALL)
    owners = ("y", "z", "c")
    placed = (P(ALL, None), P(), P(owners, None, None), P(), P(), P(ALL, None))
    return jax.shard_map(
        shards,
        mesh=grid,
        in_specs=placed,
        out_specs=(P(ALL, None), P(ALL, None), P(owners, None, None), P()),
        check_vma=False,
    )
```

```python
import jax
import jax.numpy as jnp
from jax import lax
from jax.experimental import pallas as pl
from jax.experimental.pallas import tpu as pltpu
from jax.sharding import Mesh, PartitionSpec as P

BF = jnp.bfloat16
F4 = jnp.float32
T = 128
ALL = ("y", "z", "c", "x")


def params(limit):
    return pltpu.CompilerParams(vmem_limit_bytes=limit * 1024 * 1024)


def cost(micros, nbytes):
    return pl.CostEstimate(flops=int(micros * 1.1e9), bytes_accessed=nbytes, transcendentals=0)


def whole(shape):
    zeros = (0,) * len(shape)
    return pl.BlockSpec(shape, lambda *_: zeros, pipeline_mode=pl.Buffered(1))


def dot(a, b):
    return jnp.dot(a, b, preferred_element_type=F4)


def dot_t(a, b):
    return lax.dot_general(a, b, (((1,), (1,)), ((), ())), preferred_element_type=F4)


ANY = pl.BlockSpec(memory_space=pl.ANY)


def cols_at(index):
    return pl.ds(pl.multiple_of(index * T, T), T)


def norm_kernel(x_ref, gain_ref, normed_ref, turned_ref, scale_ref):
    count, width = x_ref.shape
    blocks = width // T

    def squares(b, total):
        x = x_ref[:, cols_at(b)].astype(F4)
        return total + x * x

    total = lax.fori_loop(0, blocks, squares, jnp.zeros((count, T), F4), unroll=4)
    scale = lax.rsqrt(jnp.sum(total, axis=1, keepdims=True) / width + 1e-05)
    scale_ref[...] = jnp.broadcast_to(scale, (count, T))

    def fill(b, carry):
        x = x_ref[:, cols_at(b)].astype(F4)
        normed = (x * scale * gain_ref[:, cols_at(b)]).astype(BF)
        normed_ref[:, cols_at(b)] = normed
        turned_ref[b] = normed.T
        return carry

    lax.fori_loop(0, blocks, fill, 0, unroll=4)


def norm(x, gain):
    count, width = x.shape
    return pl.pallas_call(
        norm_kernel,
        out_shape=(
            jax.ShapeDtypeStruct((count, width), BF),
            jax.ShapeDtypeStruct((width // T, T, count), BF),
            jax.ShapeDtypeStruct((count, T), F4),
        ),
        compiler_params=params(16),
        cost_estimate=cost(1, 0),
        name="norm",
    )(x, gain)


def owned_at(pos, core, to_first, to_second):
    to_z = jnp.where(core == 0, to_first, to_second)
    to_y = jnp.where(core == 0, to_second, to_first)
    return (lax.rem(pos[0] + to_y, 4) * 4 + lax.rem(pos[1] + to_z, 4)) * 32 + core * 16


ORDER = (("x", "y", "z"), ("y", "z", "x"))


def listed(ahead, i, pos):
    y, z, c, x = pos[0], pos[1], pos[2], pos[3]
    one, two, three = ahead, i // 16, i // 4 % 4
    to_x = x + jnp.where(c == 0, one, three)
    to_y = y + jnp.where(c == 0, two, one)
    to_z = z + jnp.where(c == 0, three, two)
    return (lax.rem(to_y, 4) * 4 + lax.rem(to_z, 4)) * 32 + c * 16 + 4 * lax.rem(to_x, 4) + i % 4


STEP = 16


def grad_kernel(aheads, each, rows, cols, pos, turned_ref, turned_other_ref, own_ref, other_ref, *refs):
    at = pl.program_id(0)

    for k, (ahead, out_ref) in enumerate(zip(aheads, refs[-len(aheads) :])):

        @pl.when(at // each == k)
        def _(k=k, ahead=ahead, out_ref=out_ref):
            def one(t, carry):
                index = listed(ahead, (at - k * each) * STEP + t, pos)
                r, q = rows[index], cols[index]
                left = jnp.concatenate([turned_ref[r], turned_other_ref[r]], axis=1)
                right = jnp.concatenate([own_ref[:, cols_at(q)], other_ref[:, cols_at(q)]], axis=0)
                out_ref[t] = dot(left, right).astype(BF)
                return carry

            lax.fori_loop(0, STEP, one, 0, unroll=16)


def grads(aheads, rows, cols, pos, turned, turned_other, own, other, carried=(), ties=()):
    piece = 64
    each = piece // STEP

    def out_spec(k):
        return pl.BlockSpec((STEP, T, T), lambda i, *_: (jnp.clip(i - k * each, 0, each - 1), 0, 0))

    resident = (turned, turned_other, own, other)
    return pl.pallas_call(
        lambda *refs: grad_kernel(aheads, each, *refs),
        out_shape=[jax.ShapeDtypeStruct(a.shape, a.dtype) for a in carried]
        + [jax.ShapeDtypeStruct((piece, T, T), BF)] * len(aheads),
        grid_spec=pltpu.PrefetchScalarGridSpec(
            num_scalar_prefetch=3,
            grid=(len(aheads) * each,),
            in_specs=[whole(a.shape) for a in resident] + [ANY] * (len(carried) + len(ties)),
            out_specs=[ANY] * len(carried) + [out_spec(k) for k in range(len(aheads))],
        ),
        input_output_aliases={7 + k: k for k in range(len(carried))},
        compiler_params=params(60),
        cost_estimate=cost(2, 0),
        name="grads",
    )(rows, cols, pos, *resident, *carried, *ties)


def project_kernel(sources, rows, cols, pos, x_ref, normed_ref, scale_ref, gain_ref, g_ref, *refs):
    projected_ref, token_grad_ref, sums_ref, out_acc, back_acc, held_ref, sem = refs[-7:]
    s = pl.program_id(0)
    count, width = x_ref.shape
    blocks = width // T
    slot = lax.rem(s, 2)

    def fetch(k):
        array, offset = sources[k]
        pltpu.make_async_copy(refs[array].at[pl.ds(offset, 32)], held_ref.at[k % 2], sem.at[k % 2]).start()

    @pl.when(s == 0)
    def _():
        fetch(0)
        out_acc[...] = jnp.zeros_like(out_acc)
        back_acc[...] = jnp.zeros_like(back_acc)

    for k in range(1, len(sources)):

        @pl.when(s == k - 1)
        def _(k=k):
            fetch(k)

    pltpu.make_async_copy(refs[0].at[pl.ds(0, 32)], held_ref.at[slot], sem.at[slot]).wait()
    core = jnp.where(s < 8, pos[2], 1 - pos[2])
    pair = lax.rem(s, 8) // 2
    behind = jnp.where(pair < 2, pair, 5 - pair)

    def one(k, carry):
        i = lax.rem(s, 2) * 32 + k
        index = owned_at(pos, core, 4 - i // 16, 4 - behind) + i % 16
        r, q = cols_at(rows[index]), cols_at(cols[index])
        weight = held_ref[slot, k]
        out_acc[:, q] += dot(normed_ref[:, r], weight)
        back_acc[:, r] += dot_t(g_ref[:, q], weight)
        return carry

    lax.fori_loop(0, 32, one, 0, unroll=32)

    @pl.when(s == pl.num_programs(0) - 1)
    def _():
        scale = scale_ref[...]

        def products(b, total):
            at = cols_at(b)
            x = x_ref[:, at].astype(F4)
            back = back_acc[:, at]
            sums_ref[pl.ds(b, 1), :] = jnp.sum(back * x * scale, axis=0, keepdims=True)
            return total + x * gain_ref[:, at] * back

        total = lax.fori_loop(0, blocks, products, jnp.zeros((count, T), F4), unroll=2)
        inner = jnp.sum(total, axis=1, keepdims=True) / width
        cubed = scale * scale * scale * inner

        def finish(b, carry):
            at = cols_at(b)
            x = x_ref[:, at].astype(F4)
            token_grad_ref[:, at] = (scale * gain_ref[:, at] * back_acc[:, at] - x * cubed).astype(BF)
            return carry

        lax.fori_loop(0, blocks, finish, 0, unroll=2)

        def write(b, carry):
            projected_ref[:, cols_at(b)] = out_acc[:, cols_at(b)].astype(BF)
            return carry

        lax.fori_loop(0, g_ref.shape[1] // T, write, 0, unroll=4)


def project(rows, cols, pos, arrays, x, normed, scale, gain, g):
    sources = [(k, offset) for k, tiles in enumerate(arrays) for offset in range(0, tiles.shape[0], 32)]
    resident = (x, normed, scale, gain, g)
    sums = (x.shape[1] // T, T)
    return pl.pallas_call(
        lambda *refs: project_kernel(sources, *refs),
        out_shape=(
            jax.ShapeDtypeStruct(g.shape, BF),
            jax.ShapeDtypeStruct(x.shape, BF),
            jax.ShapeDtypeStruct(sums, F4),
        ),
        grid_spec=pltpu.PrefetchScalarGridSpec(
            num_scalar_prefetch=3,
            grid=(len(sources),),
            in_specs=[whole(a.shape) for a in resident] + [ANY] * len(arrays),
            out_specs=[whole(g.shape), whole(x.shape), whole(sums)],
            scratch_shapes=[
                pltpu.VMEM(g.shape, F4),
                pltpu.VMEM(x.shape, F4),
                pltpu.VMEM((2, 32, T, T), BF),
                pltpu.SemaphoreType.DMA((2,)),
            ],
        ),
        compiler_params=params(60),
        cost_estimate=cost(2, 0),
        name="project",
    )(rows, cols, pos, *resident, *arrays)


def joined(pieces, *ties):
    each = pieces[0].shape[0]

    def kernel(*refs):
        for j in range(4):
            refs[-1][j * each : (j + 1) * each] = refs[j][...]

    return pl.pallas_call(
        kernel,
        out_shape=jax.ShapeDtypeStruct((4 * each, T, T), BF),
        in_specs=[pl.BlockSpec(memory_space=pltpu.VMEM)] * 4 + [ANY] * len(ties),
        compiler_params=params(16),
        cost_estimate=cost(1, 0),
        name="joined",
    )(*pieces, *ties)


def held(values, *ties):
    return pl.pallas_call(
        lambda *refs: None,
        out_shape=[jax.ShapeDtypeStruct(a.shape, a.dtype) for a in values],
        in_specs=[ANY] * (len(values) + len(ties)),
        out_specs=[ANY] * len(values),
        input_output_aliases={k: k for k in range(len(values))},
        cost_estimate=cost(1, 0),
        name="held",
    )(*values, *ties)


def relayed(left, right, tie):
    half = left.shape[0] // 2

    def kernel(left_ref, right_ref, tie_ref, left_out, right_out):
        left_out[...] = left_ref[...]
        right_out[...] = right_ref[...]

    return pl.pallas_call(
        kernel,
        out_shape=[jax.ShapeDtypeStruct((half, T, T), BF)] * 2,
        grid=(2,),
        in_specs=[
            pl.BlockSpec((half // 2, T, T), lambda i: (i, 0, 0)),
            pl.BlockSpec((half // 2, T, T), lambda i: (2 + i, 0, 0)),
            ANY,
        ],
        out_specs=[pl.BlockSpec((half // 2, T, T), lambda i: (i, 0, 0))] * 2,
        compiler_params=params(60),
        cost_estimate=cost(1, 0),
        name="relayed",
    )(left, right, tie)


def ring(piece, axes, shift):
    if isinstance(axes, str):
        axes = (axes, axes)
    pairs = []
    for source in range(128):
        at = dict(y=source // 32, z=source // 8 % 4, c=source // 4 % 2, x=source % 4)
        axis = axes[at["c"]]
        to = dict(at, **{axis: (at[axis] + shift) % 4})
        pairs.append((source, to["y"] * 32 + to["z"] * 8 + to["c"] * 4 + to["x"]))
    return lax.ppermute(piece, ALL, pairs)


def exchange(pieces, axis):
    return [pieces[0]] + [ring(pieces[j], axis, j) for j in (2, 1, 3)]


def add_four(refs, i):
    a, b, c, d = (r[i].astype(F4) for r in refs)
    return (a + b) + (c + d)


def put_sums(ref, i, value):
    rows = value.shape[0]
    for part in range(3):
        rounded = value.astype(BF)
        ref[i, part * rows : (part + 1) * rows] = rounded
        value = value - rounded.astype(F4)
    ref[i, 3 * rows :] = jnp.zeros((T - 3 * rows, T), BF)


def get_sums(ref, i, rows):
    low, mid, high = (ref[i, part * rows : (part + 1) * rows].astype(F4) for part in (2, 1, 0))
    return (low + mid) + high


def add_sums(refs, i, rows):
    a, b, c, d = (get_sums(r, i, rows) for r in refs)
    return (a + b) + (c + d)


def cut_sum(pieces, sums):
    each = pieces[0].shape[0] // 4

    def kernel(*refs):
        total = add_four(refs[:4], ...).astype(BF)
        for ahead, out in enumerate(refs[-4:]):

            @pl.when(pl.program_id(0) == ahead)
            def _(out=out):
                out[:each] = total
                put_sums(out, each, refs[4][...] + refs[5][...])

    return pl.pallas_call(
        kernel,
        out_shape=[jax.ShapeDtypeStruct((each + 1, T, T), BF)] * 4,
        grid=(4,),
        in_specs=[pl.BlockSpec((each, T, T), lambda i: (i, 0, 0))] * 4 + [whole(a.shape) for a in sums],
        out_specs=[whole((each + 1, T, T))] * 4,
        compiler_params=params(32),
        cost_estimate=cost(1, 0),
        name="cut_sum",
    )(*pieces, *sums)


def next_sum(pieces, rows, cuts):
    each = (pieces[0].shape[0] - 1) // cuts

    def kernel(*refs):
        sums = add_sums(refs[:4], cuts * each, rows)
        for ahead, out in enumerate(refs[4:]):
            for i in range(each):
                out[i] = add_four(refs[:4], ahead * each + i).astype(BF)
            put_sums(out, each, sums)

    return pl.pallas_call(
        kernel,
        out_shape=[jax.ShapeDtypeStruct((each + 1, T, T), BF)] * cuts,
        in_specs=[pl.BlockSpec(memory_space=pltpu.VMEM)] * 4,
        compiler_params=params(16),
        cost_estimate=cost(1, 0),
        name="next_sum",
    )(*pieces)


def place(pieces, pos, rows):
    def kernel(pos_ref, *refs):
        out_ref, sums_ref = refs[4:]
        for k, back in enumerate((0, 2, 1, 3)):
            source = lax.rem(pos_ref[3] + 4 - back, 4)
            for u in range(4):
                out_ref[4 * source + u] = refs[k][u].astype(F4)
        sums_ref[...] = add_sums(refs[:4], 4, rows)

    return pl.pallas_call(
        kernel,
        out_shape=(jax.ShapeDtypeStruct((16, T, T), F4), jax.ShapeDtypeStruct((rows, T), F4)),
        in_specs=[pl.BlockSpec(memory_space=pltpu.SMEM)] + [pl.BlockSpec(memory_space=pltpu.VMEM)] * 4,
        compiler_params=params(16),
        cost_estimate=cost(1, 0),
        name="place",
    )(pos, *pieces)


def shards(tokens, gain, tiles, rows, cols, cotangent):
    gain2 = gain.reshape(1, -1)
    pos = jnp.stack([lax.axis_index(a).astype(jnp.int32) for a in ("y", "z", "c", "x")])
    first, second = ("z", "y"), ("y", "z")
    one, two, three = (tuple(order[k] for order in ORDER) for k in range(3))

    def other_core(value):
        return lax.ppermute(value, "c", [(0, 1), (1, 0)])

    tokens_other, g_other = other_core(tokens), other_core(cotangent)
    normed, turned, scale = norm(tokens, gain2)
    _, turned_other, _ = norm(tokens_other, gain2)
    own, opposite, behind, ahead = exchange([tiles] * 4, first)
    line = joined([own, behind, opposite, ahead], turned, turned_other)
    left, right = ring(line, second, 1), ring(line, second, 3)
    operands = (rows, cols, pos, turned, turned_other, cotangent, g_other)
    part0, part2, part1 = grads((0, 2, 1), *operands)
    left_half, right_half = relayed(left, right, part0)
    left, right = held((left, right), left_half)
    part0, part2, part1, part3 = grads((3,), *operands, (part0, part2, part1), (left_half,))
    near = [line, left, right]
    swapped = [other_core(block) for block in near]
    far = held((ring(left_half, second, 1), ring(right_half, second, 3)), part3, *swapped)
    arrays = near + list(far) + swapped + [other_core(block) for block in far]
    projected, token_grad, sums = project(rows, cols, pos, arrays, tokens, normed, scale, gain2, cotangent)
    count = sums.shape[0]
    mid = cut_sum(exchange([part0, part1, part2, part3], one), (sums, other_core(sums)))
    ends = next_sum(exchange(mid, two), count, 4)
    (sent,) = next_sum(exchange(ends, three), count, 1)
    tile_grad, sums = place(exchange([sent] * 4, "x"), pos, count)
    sums = jnp.where(pos[2] == 0, sums, other_core(sums))
    return (projected, token_grad, tile_grad, sums.reshape(-1))


def solution(mesh):
    grid = Mesh(mesh.devices.reshape(4, 4, 2, 4), ALL)
    owners = ("y", "z", "c")
    placed = (P(ALL, None), P(), P(owners, None, None), P(), P(), P(ALL, None))
    return jax.shard_map(
        shards,
        mesh=grid,
        in_specs=placed,
        out_specs=(P(ALL, None), P(ALL, None), P(owners, None, None), P()),
        check_vma=False,
    )
```

```python
import jax
import jax.numpy as jnp
from jax import lax
from jax.experimental import pallas as pl
from jax.experimental.pallas import tpu as pltpu
from jax.sharding import Mesh, PartitionSpec as P

BF = jnp.bfloat16
F4 = jnp.float32
T = 128
ALL = ("y", "z", "c", "x")


def params(limit):
    return pltpu.CompilerParams(vmem_limit_bytes=limit * 1024 * 1024)


def cost(micros, nbytes):
    return pl.CostEstimate(flops=int(micros * 1.1e9), bytes_accessed=nbytes, transcendentals=0)


def whole(shape):
    zeros = (0,) * len(shape)
    return pl.BlockSpec(shape, lambda *_: zeros, pipeline_mode=pl.Buffered(1))


def dot(a, b):
    return jnp.dot(a, b, preferred_element_type=F4)


def dot_t(a, b):
    return lax.dot_general(a, b, (((1,), (1,)), ((), ())), preferred_element_type=F4)


ANY = pl.BlockSpec(memory_space=pl.ANY)


def cols_at(index):
    return pl.ds(pl.multiple_of(index * T, T), T)


def norm_kernel(x_ref, gain_ref, normed_ref, turned_ref, scale_ref):
    count, width = x_ref.shape
    blocks = width // T

    def squares(b, total):
        x = x_ref[:, cols_at(b)].astype(F4)
        return total + x * x

    total = lax.fori_loop(0, blocks, squares, jnp.zeros((count, T), F4), unroll=4)
    scale = lax.rsqrt(jnp.sum(total, axis=1, keepdims=True) / width + 1e-05)
    scale_ref[...] = jnp.broadcast_to(scale, (count, T))

    def fill(b, carry):
        x = x_ref[:, cols_at(b)].astype(F4)
        normed = (x * scale * gain_ref[:, cols_at(b)]).astype(BF)
        normed_ref[:, cols_at(b)] = normed
        turned_ref[b] = normed.T
        return carry

    lax.fori_loop(0, blocks, fill, 0, unroll=4)


def norm(x, gain):
    count, width = x.shape
    return pl.pallas_call(
        norm_kernel,
        out_shape=(
            jax.ShapeDtypeStruct((count, width), BF),
            jax.ShapeDtypeStruct((width // T, T, count), BF),
            jax.ShapeDtypeStruct((count, T), F4),
        ),
        compiler_params=params(60),
        cost_estimate=cost(1, 0),
        name="norm",
    )(x, gain)


def owned_at(pos, core, to_first, to_second):
    to_z = jnp.where(core == 0, to_first, to_second)
    to_y = jnp.where(core == 0, to_second, to_first)
    return (lax.rem(pos[0] + to_y, 4) * 4 + lax.rem(pos[1] + to_z, 4)) * 32 + core * 16


ORDER = (("x", "y", "z"), ("y", "z", "x"))


def listed(ahead, i, pos):
    y, z, c, x = pos[0], pos[1], pos[2], pos[3]
    one, two, three = ahead, i // 16, i // 4 % 4
    to_x = x + jnp.where(c == 0, one, three)
    to_y = y + jnp.where(c == 0, two, one)
    to_z = z + jnp.where(c == 0, three, two)
    return (lax.rem(to_y, 4) * 4 + lax.rem(to_z, 4)) * 32 + c * 16 + 4 * lax.rem(to_x, 4) + i % 4


STEP = 16


def grad_kernel(aheads, each, rows, cols, pos, turned_ref, turned_other_ref, own_ref, other_ref, *refs):
    at = pl.program_id(0)

    for k, (ahead, out_ref) in enumerate(zip(aheads, refs[-len(aheads) :])):

        @pl.when(at // each == k)
        def _(k=k, ahead=ahead, out_ref=out_ref):
            def one(t, carry):
                index = listed(ahead, (at - k * each) * STEP + t, pos)
                r, q = rows[index], cols[index]
                left = jnp.concatenate([turned_ref[r], turned_other_ref[r]], axis=1)
                right = jnp.concatenate([own_ref[:, cols_at(q)], other_ref[:, cols_at(q)]], axis=0)
                out_ref[t] = dot(left, right).astype(BF)
                return carry

            lax.fori_loop(0, STEP, one, 0, unroll=16)


def grads(aheads, rows, cols, pos, turned, turned_other, own, other, carried=(), ties=()):
    piece = 64
    each = piece // STEP

    def out_spec(k):
        return pl.BlockSpec((STEP, T, T), lambda i, *_: (jnp.clip(i - k * each, 0, each - 1), 0, 0))

    resident = (turned, turned_other, own, other)
    return pl.pallas_call(
        lambda *refs: grad_kernel(aheads, each, *refs),
        out_shape=[jax.ShapeDtypeStruct(a.shape, a.dtype) for a in carried]
        + [jax.ShapeDtypeStruct((piece, T, T), BF)] * len(aheads),
        grid_spec=pltpu.PrefetchScalarGridSpec(
            num_scalar_prefetch=3,
            grid=(len(aheads) * each,),
            in_specs=[whole(a.shape) for a in resident] + [ANY] * (len(carried) + len(ties)),
            out_specs=[ANY] * len(carried) + [out_spec(k) for k in range(len(aheads))],
        ),
        input_output_aliases={7 + k: k for k in range(len(carried))},
        compiler_params=params(60),
        cost_estimate=cost(2, 0),
        name="grads",
    )(rows, cols, pos, *resident, *carried, *ties)


def project_kernel(sources, rows, cols, pos, x_ref, normed_ref, scale_ref, gain_ref, g_ref, *refs):
    projected_ref, token_grad_ref, sums_ref, out_acc, back_acc, held_ref, sem = refs[-7:]
    s = pl.program_id(0)
    count, width = x_ref.shape
    blocks = width // T
    slot = lax.rem(s, 2)

    def fetch(k):
        array, offset = sources[k]
        pltpu.make_async_copy(refs[array].at[pl.ds(offset, 32)], held_ref.at[k % 2], sem.at[k % 2]).start()

    @pl.when(s == 0)
    def _():
        fetch(0)
        out_acc[...] = jnp.zeros_like(out_acc)
        back_acc[...] = jnp.zeros_like(back_acc)

    for k in range(1, len(sources)):

        @pl.when(s == k - 1)
        def _(k=k):
            fetch(k)

    pltpu.make_async_copy(refs[0].at[pl.ds(0, 32)], held_ref.at[slot], sem.at[slot]).wait()
    core = jnp.where(s < 8, pos[2], 1 - pos[2])
    pair = lax.rem(s, 8) // 2
    behind = jnp.where(pair < 2, pair, 5 - pair)

    def one(k, carry):
        i = lax.rem(s, 2) * 32 + k
        index = owned_at(pos, core, 4 - i // 16, 4 - behind) + i % 16
        r, q = cols_at(rows[index]), cols_at(cols[index])
        weight = held_ref[slot, k]
        out_acc[:, q] += dot(normed_ref[:, r], weight)
        back_acc[:, r] += dot_t(g_ref[:, q], weight)
        return carry

    lax.fori_loop(0, 32, one, 0, unroll=32)

    @pl.when(s == pl.num_programs(0) - 1)
    def _():
        scale = scale_ref[...]

        def products(b, total):
            at = cols_at(b)
            x = x_ref[:, at].astype(F4)
            back = back_acc[:, at]
            sums_ref[pl.ds(b, 1), :] = jnp.sum(back * x * scale, axis=0, keepdims=True)
            return total + x * gain_ref[:, at] * back

        total = lax.fori_loop(0, blocks, products, jnp.zeros((count, T), F4), unroll=2)
        inner = jnp.sum(total, axis=1, keepdims=True) / width
        cubed = scale * scale * scale * inner

        def finish(b, carry):
            at = cols_at(b)
            x = x_ref[:, at].astype(F4)
            token_grad_ref[:, at] = (scale * gain_ref[:, at] * back_acc[:, at] - x * cubed).astype(BF)
            return carry

        lax.fori_loop(0, blocks, finish, 0, unroll=2)

        def write(b, carry):
            projected_ref[:, cols_at(b)] = out_acc[:, cols_at(b)].astype(BF)
            return carry

        lax.fori_loop(0, g_ref.shape[1] // T, write, 0, unroll=4)


def project(rows, cols, pos, arrays, x, normed, scale, gain, g):
    sources = [(k, offset) for k, tiles in enumerate(arrays) for offset in range(0, tiles.shape[0], 32)]
    resident = (x, normed, scale, gain, g)
    sums = (x.shape[1] // T, T)
    return pl.pallas_call(
        lambda *refs: project_kernel(sources, *refs),
        out_shape=(
            jax.ShapeDtypeStruct(g.shape, BF),
            jax.ShapeDtypeStruct(x.shape, BF),
            jax.ShapeDtypeStruct(sums, F4),
        ),
        grid_spec=pltpu.PrefetchScalarGridSpec(
            num_scalar_prefetch=3,
            grid=(len(sources),),
            in_specs=[whole(a.shape) for a in resident] + [ANY] * len(arrays),
            out_specs=[whole(g.shape), whole(x.shape), whole(sums)],
            scratch_shapes=[
                pltpu.VMEM(g.shape, F4),
                pltpu.VMEM(x.shape, F4),
                pltpu.VMEM((2, 32, T, T), BF),
                pltpu.SemaphoreType.DMA((2,)),
            ],
        ),
        compiler_params=params(60),
        cost_estimate=cost(2, 0),
        name="project",
    )(rows, cols, pos, *resident, *arrays)


def joined(pieces, tie):
    each = pieces[0].shape[0]

    def kernel(*refs):
        for j in range(4):
            refs[-1][j] = refs[j][...]

    return pl.pallas_call(
        kernel,
        out_shape=jax.ShapeDtypeStruct((4, each, T, T), BF),
        grid=(4,),
        in_specs=[pl.BlockSpec((each // 4, T, T), lambda i: (i, 0, 0))] * 4 + [ANY],
        out_specs=pl.BlockSpec((4, each // 4, T, T), lambda i: (0, i, 0, 0)),
        compiler_params=params(32),
        cost_estimate=cost(1, 0),
        name="joined",
    )(*pieces, tie).reshape(4 * each, T, T)


def held(values, *ties):
    return pl.pallas_call(
        lambda *refs: None,
        out_shape=[jax.ShapeDtypeStruct(a.shape, a.dtype) for a in values],
        in_specs=[ANY] * (len(values) + len(ties)),
        out_specs=[ANY] * len(values),
        input_output_aliases={k: k for k in range(len(values))},
        cost_estimate=cost(1, 0),
        name="held",
    )(*values, *ties)


def relayed(left, right, tie):
    half = left.shape[0] // 2

    def kernel(left_ref, right_ref, tie_ref, left_out, right_out):
        left_out[...] = left_ref[...]
        right_out[...] = right_ref[...]

    return pl.pallas_call(
        kernel,
        out_shape=[jax.ShapeDtypeStruct((half, T, T), BF)] * 2,
        grid=(2,),
        in_specs=[
            pl.BlockSpec((half // 2, T, T), lambda i: (i, 0, 0)),
            pl.BlockSpec((half // 2, T, T), lambda i: (2 + i, 0, 0)),
            ANY,
        ],
        out_specs=[pl.BlockSpec((half // 2, T, T), lambda i: (i, 0, 0))] * 2,
        compiler_params=params(60),
        cost_estimate=cost(1, 0),
        name="relayed",
    )(left, right, tie)


def ring(piece, axes, shift):
    if isinstance(axes, str):
        axes = (axes, axes)
    pairs = []
    for source in range(128):
        at = dict(y=source // 32, z=source // 8 % 4, c=source // 4 % 2, x=source % 4)
        axis = axes[at["c"]]
        to = dict(at, **{axis: (at[axis] + shift) % 4})
        pairs.append((source, to["y"] * 32 + to["z"] * 8 + to["c"] * 4 + to["x"]))
    return lax.ppermute(piece, ALL, pairs)


def exchange(pieces, axis):
    return [pieces[0]] + [ring(pieces[j], axis, j) for j in (1, 2, 3)]


def add_four(refs, i):
    a, b, c, d = (r[i].astype(F4) for r in refs)
    return (a + c) + (b + d)


def put_sums(ref, i, value):
    rows = value.shape[0]
    for part in range(3):
        rounded = value.astype(BF)
        ref[i, part * rows : (part + 1) * rows] = rounded
        value = value - rounded.astype(F4)
    ref[i, 3 * rows :] = jnp.zeros((T - 3 * rows, T), BF)


def get_sums(ref, i, rows):
    low, mid, high = (ref[i, part * rows : (part + 1) * rows].astype(F4) for part in (2, 1, 0))
    return (low + mid) + high


def add_sums(refs, i, rows):
    a, b, c, d = (get_sums(r, i, rows) for r in refs)
    return (a + c) + (b + d)


def cut_sum(pieces, sums):
    each = pieces[0].shape[0] // 4

    def kernel(*refs):
        total = add_four(refs[:4], ...).astype(BF)
        for ahead, out in enumerate(refs[-4:]):

            @pl.when(pl.program_id(0) == ahead)
            def _(out=out):
                out[:each] = total
                put_sums(out, each, refs[4][...] + refs[5][...])

    return pl.pallas_call(
        kernel,
        out_shape=[jax.ShapeDtypeStruct((each + 1, T, T), BF)] * 4,
        grid=(4,),
        in_specs=[pl.BlockSpec((each, T, T), lambda i: (i, 0, 0))] * 4 + [whole(a.shape) for a in sums],
        out_specs=[whole((each + 1, T, T))] * 4,
        compiler_params=params(32),
        cost_estimate=cost(1, 0),
        name="cut_sum",
    )(*pieces, *sums)


def next_sum(pieces, rows, cuts):
    each = (pieces[0].shape[0] - 1) // cuts

    def kernel(*refs):
        sums = add_sums(refs[:4], cuts * each, rows)
        for ahead, out in enumerate(refs[4:]):
            for i in range(each):
                out[i] = add_four(refs[:4], ahead * each + i).astype(BF)
            put_sums(out, each, sums)

    return pl.pallas_call(
        kernel,
        out_shape=[jax.ShapeDtypeStruct((each + 1, T, T), BF)] * cuts,
        in_specs=[pl.BlockSpec(memory_space=pltpu.VMEM)] * 4,
        compiler_params=params(16),
        cost_estimate=cost(1, 0),
        name="next_sum",
    )(*pieces)


def place(pieces, pos, rows):
    def kernel(pos_ref, *refs):
        out_ref, sums_ref = refs[4:]
        for back in range(4):
            source = lax.rem(pos_ref[3] + 4 - back, 4)
            for u in range(4):
                out_ref[4 * source + u] = refs[back][u].astype(F4)
        sums_ref[...] = add_sums(refs[:4], 4, rows)

    return pl.pallas_call(
        kernel,
        out_shape=(jax.ShapeDtypeStruct((16, T, T), F4), jax.ShapeDtypeStruct((rows, T), F4)),
        in_specs=[pl.BlockSpec(memory_space=pltpu.SMEM)] + [pl.BlockSpec(memory_space=pltpu.VMEM)] * 4,
        compiler_params=params(16),
        cost_estimate=cost(1, 0),
        name="place",
    )(pos, *pieces)


def shards(tokens, gain, tiles, rows, cols, cotangent):
    gain2 = gain.reshape(1, -1)
    pos = jnp.stack([lax.axis_index(a).astype(jnp.int32) for a in ("y", "z", "c", "x")])
    first, second = ("z", "y"), ("y", "z")
    one, two, three = (tuple(order[k] for order in ORDER) for k in range(3))

    def other_core(value):
        return lax.ppermute(value, "c", [(0, 1), (1, 0)])

    tokens_other, g_other = other_core(tokens), other_core(cotangent)
    normed, turned, scale = norm(tokens, gain2)
    _, turned_other, _ = norm(tokens_other, gain2)
    line = joined(exchange([tiles] * 4, first), turned_other)
    left, right = ring(line, second, 1), ring(line, second, 3)
    operands = (rows, cols, pos, turned, turned_other, cotangent, g_other)
    part0, part2, part1 = grads((0, 2, 1), *operands)
    left_half, right_half = relayed(left, right, part0)
    left, right = held((left, right), left_half)
    part0, part2, part1, part3 = grads((3,), *operands, (part0, part2, part1), (left_half,))
    near = [line, left, right]
    swapped = [other_core(block) for block in near]
    far = held((ring(left_half, second, 1), ring(right_half, second, 3)), part3, *swapped)
    arrays = near + list(far) + swapped + [other_core(block) for block in far]
    projected, token_grad, sums = project(rows, cols, pos, arrays, tokens, normed, scale, gain2, cotangent)
    count = sums.shape[0]
    mid = cut_sum(exchange([part0, part1, part2, part3], one), (sums, other_core(sums)))
    ends = next_sum(exchange(mid, two), count, 4)
    (sent,) = next_sum(exchange(ends, three), count, 1)
    tile_grad, sums = place(exchange([sent] * 4, "x"), pos, count)
    sums = jnp.where(pos[2] == 0, sums, other_core(sums))
    return (projected, token_grad, tile_grad, sums.reshape(-1))


def solution(mesh):
    grid = Mesh(mesh.devices.reshape(4, 4, 2, 4), ALL)
    owners = ("y", "z", "c")
    placed = (P(ALL, None), P(), P(owners, None, None), P(), P(), P(ALL, None))
    return jax.shard_map(
        shards,
        mesh=grid,
        in_specs=placed,
        out_specs=(P(ALL, None), P(ALL, None), P(owners, None, None), P()),
        check_vma=False,
    )
```
